32 devices in a mesh: dp: 16 (over z, y, x), tensor: 2 (over core).
Axes of the slice: x: 2, y: 2, z: 4, core: 2. Of those that a mesh axis runs over, the one named last changes fastest.
Arguments:
- tokens_in: bfloat16 [8192, 2048], P(('dp', 'tensor')), may hold values from -6 to 6
- cotangent: bfloat16 [8192, 2048], P(('dp', 'tensor')), may hold values from -6 to 6
- segment_ids: int32 [8192], P('dp'), may hold values from 0 to 3, as said below
- destination: int32 [8192], P(('dp', 'tensor')), may hold values from 0 to 8191, as said below
- source: int32 [8192], P(('dp', 'tensor')), may hold values from 0 to 8191, as said below
- w_query: float32 [2048, 2048], P('dp', 'tensor'), may hold values from -0.125 to 0.125
- w_key: float32 [2048, 2048], P('dp', 'tensor'), may hold values from -0.125 to 0.125
- w_value: float32 [2048, 2048], P('dp', 'tensor'), may hold values from -0.125 to 0.125
- w_out: float32 [2048, 2048], P('tensor', 'dp'), may hold values from -0.5 to 0.5
- w_gate: float32 [2048, 8192], P('dp', 'tensor'), may hold values from -0.125 to 0.125
- w_up: float32 [2048, 8192], P('dp', 'tensor'), may hold values from -0.125 to 0.125
- w_down: float32 [8192, 2048], P('tensor', 'dp'), may hold values from -0.0625 to 0.0625
Outputs:
- layer_out: float32 [8192, 2048], P(('dp', 'tensor'))
- grad_in: float32 [8192, 2048], P(('dp', 'tensor'))
- grad_w_query: float32 [2048, 2048], P('dp', 'tensor')
- grad_w_key: float32 [2048, 2048], P('dp', 'tensor')
- grad_w_value: float32 [2048, 2048], P('dp', 'tensor')
- grad_w_out: float32 [2048, 2048], P('tensor', 'dp')
- grad_w_gate: float32 [2048, 8192], P('dp', 'tensor')
- grad_w_up: float32 [2048, 8192], P('dp', 'tensor')
- grad_w_down: float32 [8192, 2048], P('tensor', 'dp')
The draws below stay inside these ranges and needn't reach their ends.
Inputs may be any that keep to these rules, and one draw needn't show every extreme that they name: `segment_ids`: within each group of 512 balanced rows, the number of the sequence a row belongs to, never falling, all 4 sequences present, each of 1 to 255 rows, one of exactly 255 rows; sequences 2 k and 2 k + 1 together fill rows k * 256 to (k + 1) * 256 - 1 of the group. `destination`: a permutation of the 8192 rows; the 256 rows of each device go, 8 of them, to each device. The inverse of destination: source[destination[i]] = i.
All inputs are finite; a program needn't handle non-finite values.
Results may differ from the reference program's by a relative error of at most 0.014.
Values may be sent and summed in bfloat16 or wider, within the bound.
A program may use at most 320 MiB of HBM per device.

```python
import math
import jax
import jax.numpy as jnp
from jax import lax

D = 2048
HEADS = 16
HEAD_DIM = 128
FF = 8192
TOK_DEV = 256
SEGS = 4
GROUPS = 16
GROUP_ROWS = 512
TOKENS = 8192


def layout(key):
    key_first = jax.random.fold_in(key, 101)
    key_flip = jax.random.fold_in(key, 102)
    key_chosen = jax.random.fold_in(key, 104)
    key_senders = jax.random.fold_in(key, 106)
    key_within = jax.random.fold_in(key, 107)
    pairs = SEGS // 2
    first_len = jax.random.randint(key_first, (GROUPS, pairs), 1, TOK_DEV).astype(jnp.int32)
    chosen = jax.random.randint(key_chosen, (), 0, GROUPS)
    marked = (jnp.arange(GROUPS)[:, None] == chosen) & (jnp.arange(pairs)[None, :] == 0)
    first_len = jnp.where(marked, TOK_DEV - 1, first_len).astype(jnp.int32)
    flips = jax.random.randint(key_flip, (GROUPS, pairs), 0, 2)
    lead = jnp.where(flips == 1, TOK_DEV - first_len, first_len).astype(jnp.int32)
    trail = (TOK_DEV - lead).astype(jnp.int32)
    lengths = jnp.stack([lead, trail], axis=2).reshape(GROUPS, SEGS).astype(jnp.int32)
    ends = jnp.cumsum(lengths, axis=1).astype(jnp.int32)
    inside = jnp.arange(GROUP_ROWS, dtype=jnp.int32)
    segments = jnp.sum((inside[None, :, None] >= ends[:, None, :SEGS - 1]).astype(jnp.int32), axis=2).reshape(TOKENS).astype(jnp.int32)
    device_total = TOKENS // TOK_DEV
    per_peer = TOK_DEV // device_total
    senders = jax.vmap(lambda sub_key: jax.random.permutation(sub_key, device_total))(jax.random.split(key_senders, device_total)).astype(jnp.int32)
    position = jnp.arange(TOKENS, dtype=jnp.int32)
    anchor_dev = senders[position // TOK_DEV, position % TOK_DEV // per_peer]
    grouped = jnp.argsort(anchor_dev, stable=True).astype(jnp.int32).reshape(device_total, TOK_DEV)
    within = jax.vmap(lambda sub_key: jax.random.permutation(sub_key, TOK_DEV))(jax.random.split(key_within, device_total)).astype(jnp.int32)
    anchor_row = jnp.arange(device_total, dtype=jnp.int32)[:, None] * TOK_DEV + within
    source_rows = jnp.zeros((TOKENS,), jnp.int32).at[grouped.reshape(-1)].set(anchor_row.reshape(-1))
    destination_rows = jnp.zeros((TOKENS,), jnp.int32).at[source_rows].set(position)
    return (segments, destination_rows, source_rows)


def draw_segment_ids(key, part):
    return layout(key)[0]


def draw_destination(key, part):
    return layout(key)[1]


def draw_source(key, part):
    return layout(key)[2]


def strengthened(entries, stream_key, source, target, blocks, factor):
    def block_of(dim):
        return (jnp.arange(entries.shape[dim]) // (entries.shape[dim] // blocks)).reshape((-1,) + (1,) * (entries.ndim - 1 - dim))

    near = jax.random.permutation(stream_key, blocks)[block_of(target)]
    other_side = (block_of(target) + blocks // 2) % blocks
    return jnp.where((block_of(source) == near) | (block_of(source) == other_side), factor * entries, entries)


def shard_levels(key, dims, pieces, least, largest):
    gain, own = 1.0, jax.random.fold_in(key, 6)
    for dim, shards_of in pieces:
        heights = jnp.exp(jax.random.uniform(jax.random.fold_in(own, dim), (shards_of,), jnp.float32, least / len(pieces), largest / len(pieces)))
        gain = gain * jnp.repeat(heights, dims[dim] // shards_of).reshape([-1 if axis == dim else 1 for axis in range(len(dims))])
    return gain


def gaussian(own_key, shape, scale, reach, cuts=(), kind=jnp.bfloat16):
    values = jax.random.normal(own_key, shape, jnp.float32) * scale
    if len(cuts) > 0:
        values = shard_levels(own_key, shape, cuts, -0.22, 0.18) * values
    return jnp.clip(values, min=-reach, max=reach).astype(kind)


def heavy_noise(stream_key, extent, scale, bound, cuts, heavy, kind=jnp.bfloat16):
    drawn = scale * jax.random.normal(stream_key, extent, jnp.float32)
    if cuts:
        drawn = drawn * shard_levels(stream_key, extent, cuts, -0.22, 0.18)
    return jnp.clip(strengthened(drawn, jax.random.fold_in(stream_key, 3), *heavy), -bound, bound).astype(kind)


def setup_inputs(seed: int = 0) -> dict:
    key_of = jax.random.split(jax.random.key(seed), 13)
    return {
        "tokens_in": heavy_noise(key_of[0], (TOKENS, D), 1.0, 6.0, ((0, 32),), (0, 1, 32, 2.75)),
        "cotangent": heavy_noise(key_of[1], (TOKENS, D), 1.0, 6.0, ((0, 32),), (0, 1, 32, 2.75)),
        "segment_ids": draw_segment_ids(jax.random.fold_in(key_of[12], 71), 0),
        "destination": draw_destination(jax.random.fold_in(key_of[12], 71), 0),
        "source": draw_source(jax.random.fold_in(key_of[12], 71), 0),
        "w_query": gaussian(key_of[5], (D, D), D ** -0.5, 0.125, ((0, 16), (1, 2)), jnp.float32),
        "w_key": gaussian(key_of[6], (D, D), D ** -0.5, 0.125, ((0, 16), (1, 2)), jnp.float32),
        "w_value": gaussian(key_of[7], (D, D), D ** -0.5, 0.125, ((0, 16), (1, 2)), jnp.float32),
        "w_out": gaussian(key_of[8], (D, D), (D // 16) ** -0.5, 0.5, ((0, 2), (1, 16)), jnp.float32),
        "w_gate": gaussian(key_of[9], (D, FF), D ** -0.5, 0.125, ((0, 16), (1, 2)), jnp.float32),
        "w_up": gaussian(key_of[10], (D, FF), D ** -0.5, 0.125, ((0, 16), (1, 2)), jnp.float32),
        "w_down": gaussian(key_of[11], (FF, D), FF ** -0.5, 0.0625, ((0, 2), (1, 16)), jnp.float32),
    }


EPSILON = 1e-05
NEG_LARGE = -1e+30

@jax.custom_vjp
def low(v):
    return lax.optimization_barrier(v.astype(jnp.bfloat16)).astype(jnp.float32)

@jax.custom_vjp
def low_back(v):
    return v

def low_keep(v):
    return (low(v), None)

def low_pass(kept, grad):
    return (grad,)

def back_keep(v):
    return (v, None)

def back_low(kept, grad):
    return (low(grad),)
low.defvjp(low_keep, low_pass)
low_back.defvjp(back_keep, back_low)

def matmul(left, right):
    return jnp.dot(left, right, precision=lax.Precision.HIGHEST)

def layer_norm(values):
    center = values - lax.optimization_barrier(jnp.mean(values, axis=-1, keepdims=True))
    spread = lax.optimization_barrier(jnp.mean(center * center, axis=-1, keepdims=True))
    return center * lax.rsqrt(spread + EPSILON)

def rotate(values, cos_rows, sin_rows):
    row_total = values.shape[0]
    heads_view = values.reshape(row_total, -1, HEAD_DIM)
    half_dim = HEAD_DIM // 2
    first_half = heads_view[..., :half_dim]
    second_half = heads_view[..., half_dim:]
    cos_wide = cos_rows[:, None, :]
    sin_wide = sin_rows[:, None, :]
    turned = jnp.concatenate([first_half * cos_wide - second_half * sin_wide, second_half * cos_wide + first_half * sin_wide], axis=-1)
    return turned.reshape(row_total, -1)

def geometry(segments):
    row_total = segments.shape[0]
    seq_numbers = jnp.arange(SEGS, dtype=jnp.int32)
    starts = lax.optimization_barrier(jnp.sum((segments[:, None] < seq_numbers[None, :]).astype(jnp.int32), axis=0)).astype(jnp.int32)
    onehot = segments[:, None] == seq_numbers[None, :]
    offset = lax.optimization_barrier(jnp.sum(jnp.where(onehot, starts[None, :], 0), axis=1)).astype(jnp.int32)
    row_index = jnp.arange(row_total, dtype=jnp.int32)
    places = row_index - offset
    half_dim = HEAD_DIM // 2
    frequency = jnp.exp(-jnp.arange(half_dim, dtype=jnp.float32) * (2.0 * math.log(10000.0) / HEAD_DIM))
    angles = places.astype(jnp.float32)[:, None] * frequency[None, :]
    visible = (segments[:, None] == segments[None, :]) & (row_index[None, :] <= row_index[:, None])
    return (jnp.cos(angles), jnp.sin(angles), visible)

def layer(values, weights, cos_rows, sin_rows, visible):
    query_w, key_w, value_w, out_w, gate_w, up_w, down_w = [low(weight) for weight in weights]
    normed_one = low(layer_norm(values))
    queries = low(rotate(low_back(matmul(normed_one, query_w)), cos_rows, sin_rows))
    key_rows = low(rotate(low_back(matmul(normed_one, key_w)), cos_rows, sin_rows))
    value_rows = low(low_back(matmul(normed_one, value_w)))
    head_shape = (GROUP_ROWS, HEADS, HEAD_DIM)
    scores = jnp.einsum('qhd,khd->hqk', queries.reshape(head_shape), key_rows.reshape(head_shape), precision=lax.Precision.HIGHEST) * (1.0 / math.sqrt(HEAD_DIM))
    scores = jnp.where(visible[None], low_back(scores), NEG_LARGE)
    probabilities = low(jax.nn.softmax(scores, axis=-1))
    attended = jnp.einsum('hqk,khd->qhd', probabilities, value_rows.reshape(head_shape), precision=lax.Precision.HIGHEST)
    attended = low(low_back(attended)).reshape(GROUP_ROWS, D)
    middle = values + low_back(matmul(attended, out_w))
    normed_two = low(layer_norm(middle))
    gate_lin = low_back(matmul(normed_two, gate_w))
    up_lin = low_back(matmul(normed_two, up_w))
    hidden = low(jax.nn.silu(gate_lin) * up_lin)
    return middle + low_back(matmul(hidden, down_w))

def reference(tokens_in, cotangent, segment_ids, destination, source, w_query, w_key, w_value, w_out, w_gate, w_up, w_down):
    arrived = tokens_in.astype(jnp.float32)[source].reshape(GROUPS, GROUP_ROWS, D)
    upstream = cotangent.astype(jnp.float32)[source].reshape(GROUPS, GROUP_ROWS, D)
    segments = segment_ids.reshape(GROUPS, GROUP_ROWS)
    masters = (w_query, w_key, w_value, w_out, w_gate, w_up, w_down)

    def one_group(totals, item):
        rows_given, rows_grad, seg_rows = item
        cos_rows, sin_rows, visible = geometry(seg_rows)

        def forward(values, *weights):
            return layer(values, weights, cos_rows, sin_rows, visible)
        result, backward = jax.vjp(forward, rows_given, *masters)
        gradients = backward(rows_grad)
        new_totals = tuple((total + extra for total, extra in zip(totals, gradients[1:])))
        return (new_totals, (result, gradients[0]))
    starting = tuple((jnp.zeros_like(weight) for weight in masters))
    totals, (outputs, input_grads) = lax.scan(one_group, starting, (arrived, upstream, segments))
    layer_out = outputs.reshape(TOKENS, D)[destination]
    grad_in = input_grads.reshape(TOKENS, D)[destination]
    return (layer_out, grad_in, totals[0], totals[1], totals[2], totals[3], totals[4], totals[5], totals[6])
```

```python
import math

import jax
import jax.numpy as jnp
from jax import lax
from jax.experimental import pallas as pl
from jax.experimental.pallas import tpu as pltpu
from jax.sharding import Mesh
from jax.sharding import PartitionSpec as P

HEAD_DIM = 128
SEGS = 4
EPSILON = 1e-05
NEG_LARGE = -1e30
F32 = jnp.float32
BF16 = jnp.bfloat16
FLIP = ((0, 1), (1, 0))


def project(left, right):
    return jnp.dot(left, right, preferred_element_type=F32)


def project_t(left, right):
    return lax.dot_general(left, right, (((1,), (1,)), ((), ())), preferred_element_type=F32)


def outer_sum(left, right):
    return lax.dot_general(left, right, (((0,), (0,)), ((), ())), preferred_element_type=F32)


def norm_parts(values):
    center = values - jnp.mean(values, axis=-1, keepdims=True)
    spread = jnp.mean(center * center, axis=-1, keepdims=True)
    scale = lax.rsqrt(spread + EPSILON)
    return center * scale, scale


def norm_back(normed, scale, gradient):
    mean_grad = jnp.mean(gradient, axis=-1, keepdims=True)
    mean_both = jnp.mean(gradient * normed, axis=-1, keepdims=True)
    return (gradient - mean_grad - normed * mean_both) * scale


def to_x(values):
    return lax.ppermute(values, "x", FLIP)


def to_y(values):
    return lax.ppermute(values, "y", FLIP)


def to_core(values):
    return lax.ppermute(values, "c", FLIP)


def plane_gather(rows):
    half = rows.shape[0] // 2
    first, second = rows[:half], rows[half:]
    first_x = to_x(first)
    second_y = to_y(second)
    first_far = to_y(jnp.concatenate([first, first_x]))
    second_far = to_x(jnp.concatenate([second, second_y]))
    mine = jnp.concatenate(
        [
            first,
            second,
            first_x,
            second_far[:half],
            first_far[:half],
            second_y,
            first_far[half:],
            second_far[half:],
        ]
    )
    return jnp.concatenate([mine, to_core(mine)])


def plane_scatter(far, near):
    block = near.shape[0] // 4
    half = block // 2
    got = to_core(far.astype(BF16))
    paired = (near + got.astype(F32)).astype(BF16).reshape(4, 2, half, -1)
    by_y = to_y(jnp.concatenate([paired[2, 0], paired[3, 0]])).astype(F32)
    by_x = to_x(jnp.concatenate([paired[1, 1], paired[3, 1]])).astype(F32)
    own_first = paired[0, 0].astype(F32) + by_y[:half]
    own_second = paired[0, 1].astype(F32) + by_x[:half]
    x_first = (paired[1, 0].astype(F32) + by_y[half:]).astype(BF16)
    y_second = (paired[2, 1].astype(F32) + by_x[half:]).astype(BF16)
    return jnp.concatenate(
        [own_first + to_x(x_first).astype(F32), own_second + to_y(y_second).astype(F32)]
    )


def ring_next(values):
    total = lax.axis_size("z")
    return lax.ppermute(values, "z", [(i, (i + 1) % total) for i in range(total)])


def ring_gather(block):
    total = lax.axis_size("z")
    place = lax.axis_index("z")
    rows = block.shape[0]
    whole = jnp.zeros((total * rows, block.shape[1]), block.dtype)
    current = block
    whole = lax.dynamic_update_slice(whole, current, (place * rows, 0))
    for step in range(1, total):
        current = ring_next(current)
        owner = lax.rem(place - step + total, total)
        whole = lax.dynamic_update_slice(whole, current, (owner * rows, 0))
    return whole, current


def ring_outer(left, right):
    total = lax.axis_size("z")
    place = lax.axis_index("z")
    columns = left.shape[1] // total
    running = None
    for step in range(total):
        owner = lax.rem(place + 2 * total - 1 - step, total)
        piece = lax.dynamic_slice(left, (0, owner * columns), (left.shape[0], columns))
        term = outer_sum(piece, right)
        if running is not None:
            term = term + ring_next(running).astype(F32)
        running = term.astype(BF16)
    return running


def to_plane(values):
    pieces = values.reshape(-1, values.shape[2])
    return lax.all_to_all(pieces, ("y", "x"), split_axis=0, concat_axis=0, tiled=True)


def spread(weight):
    rows, columns = weight.shape
    return weight.reshape(rows, 4, columns // 4).transpose(1, 0, 2).astype(BF16)


def from_plane(block):
    rows = block.shape[0] // 4
    got = lax.all_to_all(block, ("y", "x"), split_axis=0, concat_axis=0, tiled=True)
    return got.reshape(4, rows, block.shape[1])


def gathered(block):
    return block.transpose(1, 0, 2).reshape(block.shape[1], -1).astype(F32)


def turn(values, cos_rows, sin_rows):
    return values * cos_rows + pltpu.roll(values, HEAD_DIM // 2, 1) * sin_rows


def visible_of(places):
    size = places.shape[0]
    row = lax.broadcasted_iota(jnp.int32, (size, size), 0)
    column = lax.broadcasted_iota(jnp.int32, (size, size), 1)
    return (column <= row) & (row - column <= places)


def soft_of(queries, keys, visible):
    scores = project_t(queries, keys) * (1.0 / math.sqrt(HEAD_DIM))
    scores = jnp.where(visible, scores, NEG_LARGE)
    weights = jnp.exp(scores - jnp.max(scores, axis=1, keepdims=True))
    return weights / jnp.sum(weights, axis=1, keepdims=True)


def attend_kernel(lin_ref, cos_ref, sin_ref, place_ref, low_ref, out_ref):
    width = out_ref.shape[1]
    cos_rows, sin_rows = cos_ref[...], sin_ref[...]
    visible = visible_of(place_ref[...])
    for start in range(0, width, HEAD_DIM):
        here = slice(start, start + HEAD_DIM)
        key_at = slice(width + start, width + start + HEAD_DIM)
        value_at = slice(2 * width + start, 2 * width + start + HEAD_DIM)
        queries = turn(lin_ref[:, here], cos_rows, sin_rows).astype(BF16)
        keys = turn(lin_ref[:, key_at], cos_rows, sin_rows).astype(BF16)
        values = lin_ref[:, value_at].astype(BF16)
        low_ref[:, here] = queries
        low_ref[:, key_at] = keys
        low_ref[:, value_at] = values
        soft = soft_of(queries, keys, visible).astype(BF16)
        out_ref[:, here] = project(soft, values).astype(BF16)


def attend_back_kernel(low_ref, grad_ref, cos_ref, sin_ref, place_ref, out_ref):
    width = grad_ref.shape[1]
    cos_rows, sin_rows = cos_ref[...], -sin_ref[...]
    visible = visible_of(place_ref[...])
    scale = 1.0 / math.sqrt(HEAD_DIM)
    for start in range(0, width, HEAD_DIM):
        here = slice(start, start + HEAD_DIM)
        key_at = slice(width + start, width + start + HEAD_DIM)
        value_at = slice(2 * width + start, 2 * width + start + HEAD_DIM)
        queries, keys, values = low_ref[:, here], low_ref[:, key_at], low_ref[:, value_at]
        grad = grad_ref[:, here]
        soft = soft_of(queries, keys, visible)
        grad_soft = project_t(grad, values)
        inner = jnp.sum(soft * grad_soft, axis=1, keepdims=True)
        grad_scores = (soft * (grad_soft - inner)).astype(BF16)
        grad_query = project(grad_scores, keys) * scale
        grad_key = outer_sum(grad_scores, queries) * scale
        out_ref[:, here] = turn(grad_query, cos_rows, sin_rows).astype(BF16)
        out_ref[:, key_at] = turn(grad_key, cos_rows, sin_rows).astype(BF16)
        out_ref[:, value_at] = outer_sum(soft.astype(BF16), grad).astype(BF16)


def row_spec(rows, columns):
    return pl.BlockSpec((rows, columns), lambda i: (i, 0))


def attend(lin, cos_rows, sin_rows, places, block):
    rows, width = lin.shape[0], lin.shape[1] // 3
    return pl.pallas_call(
        attend_kernel,
        grid=(rows // block,),
        in_specs=[
            row_spec(block, 3 * width),
            row_spec(block, HEAD_DIM),
            row_spec(block, HEAD_DIM),
            row_spec(block, 1),
        ],
        out_specs=[row_spec(block, 3 * width), row_spec(block, width)],
        out_shape=[
            jax.ShapeDtypeStruct((rows, 3 * width), BF16),
            jax.ShapeDtypeStruct((rows, width), BF16),
        ],
        cost_estimate=pl.CostEstimate(
            flops=4 * rows * block * width,
            bytes_accessed=rows * (20 * width + 1024),
            transcendentals=rows * block * width // HEAD_DIM,
        ),
        name="attend",
    )(lin, cos_rows, sin_rows, places)


def attend_back(low, grad, cos_rows, sin_rows, places, block):
    rows, width = grad.shape
    return pl.pallas_call(
        attend_back_kernel,
        grid=(rows // block,),
        in_specs=[
            row_spec(block, 3 * width),
            row_spec(block, width),
            row_spec(block, HEAD_DIM),
            row_spec(block, HEAD_DIM),
            row_spec(block, 1),
        ],
        out_specs=row_spec(block, 3 * width),
        out_shape=jax.ShapeDtypeStruct((rows, 3 * width), BF16),
        cost_estimate=pl.CostEstimate(
            flops=10 * rows * block * width,
            bytes_accessed=rows * (14 * width + 1024),
            transcendentals=rows * block * width // HEAD_DIM,
        ),
        name="attend_back",
    )(low, grad, cos_rows, sin_rows, places)


def plane_places(segment_ids):
    segments = lax.all_gather(segment_ids, ("y", "x"), axis=0)
    groups, size = segments.shape
    numbers = jnp.arange(SEGS, dtype=jnp.int32)
    starts = jnp.sum((segments[:, :, None] < numbers).astype(jnp.int32), axis=1)
    onehot = segments[:, :, None] == numbers
    offset = jnp.sum(jnp.where(onehot, starts[:, None, :], 0), axis=2)
    places = jnp.arange(size, dtype=jnp.int32)[None, :] - offset
    places = places.reshape(2, 2, 2, size // 2)
    places = jnp.where(lax.axis_index("y") == 1, places[::-1], places)
    places = jnp.where(lax.axis_index("x") == 1, places[:, ::-1], places)
    places = jnp.where(lax.axis_index("c") == 1, places[:, :, ::-1], places)
    return places.transpose(2, 0, 1, 3).reshape(-1, 1)


def after(values, *gates):
    return lax.optimization_barrier((values,) + gates)[0]


EVERY = ("z", "y", "x", "c")


def exchange(rows):
    return lax.all_to_all(rows, EVERY, split_axis=0, concat_axis=0, tiled=True)


def on_device(
    tokens_in,
    cotangent,
    segment_ids,
    destination,
    source,
    w_query,
    w_key,
    w_value,
    w_out,
    w_gate,
    w_up,
    w_down,
):
    tok_rows = tokens_in.shape[0]
    devices = lax.axis_size(EVERY)
    per_peer = tok_rows // devices
    row_index = jnp.arange(tok_rows, dtype=jnp.int32)
    peer_to = destination // tok_rows
    ahead_rows = (peer_to[None, :] == peer_to[:, None]) & (
        destination[None, :] < destination[:, None]
    )
    send_slot = peer_to * per_peer + jnp.sum(ahead_rows.astype(jnp.int32), axis=1)
    peer_from = source // tok_rows
    before = (peer_from[None, :] == peer_from[:, None]) & (row_index[None, :] < row_index[:, None])
    recv_slot = peer_from * per_peer + jnp.sum(before.astype(jnp.int32), axis=1)
    send_pick = (send_slot[:, None] == row_index[None, :]).astype(BF16)
    recv_pick = (recv_slot[:, None] == row_index[None, :]).astype(BF16)

    arrived = project(recv_pick, exchange(outer_sum(send_pick, tokens_in).astype(BF16)))
    upstream_low = project(
        recv_pick, exchange(outer_sum(send_pick, cotangent).astype(BF16))
    ).astype(BF16)
    upstream = upstream_low.astype(F32)

    attention_block = to_plane(
        jnp.concatenate([spread(w_query), spread(w_key), spread(w_value), spread(w_out.T)], axis=2)
    )
    forward_block = to_plane(jnp.concatenate([spread(w_gate), spread(w_up)], axis=2))
    down_block = to_plane(spread(w_down.T))
    attention_w, attention_last = ring_gather(attention_block)
    forward_w, forward_last = ring_gather(after(forward_block, attention_last))
    down_w, _ = ring_gather(after(down_block, forward_last))
    head_width = attention_w.shape[1] // 4
    hidden_width = down_w.shape[1]
    qkv_w = attention_w[:, : 3 * head_width]
    out_w = attention_w[:, 3 * head_width :]

    places = plane_places(segment_ids)
    half_dim = HEAD_DIM // 2
    frequency = jnp.exp(
        -jnp.arange(half_dim, dtype=F32) * (2.0 * math.log(10000.0) / HEAD_DIM)
    )
    angles = places.astype(F32) * frequency[None, :]
    cos_half, sin_half = jnp.cos(angles), jnp.sin(angles)
    cos_rows = jnp.concatenate([cos_half, cos_half], axis=1)
    sin_rows = jnp.concatenate([-sin_half, sin_half], axis=1)

    normed_one, scale_one = norm_parts(arrived)
    seen_one = plane_gather(normed_one.astype(BF16))
    total_rows = seen_one.shape[0]
    middle_row = total_rows // 2
    qkv_lin = project(seen_one, qkv_w)
    qkv_low, attended = attend(qkv_lin, cos_rows, sin_rows, places, tok_rows)
    middle = arrived + plane_scatter(
        project_t(attended[middle_row:], out_w), project_t(attended[:middle_row], out_w)
    )
    normed_two, scale_two = norm_parts(middle)
    seen_two = plane_gather(normed_two.astype(BF16))
    grad_two_all = plane_gather(upstream_low)

    gate_lin = project(seen_two, forward_w[:, :hidden_width])
    up_lin = project(seen_two, forward_w[:, hidden_width:])
    sigmoid = jax.nn.sigmoid(gate_lin)
    hidden = (gate_lin * sigmoid * up_lin).astype(BF16)
    summed_down = from_plane(ring_outer(grad_two_all, hidden))
    output = middle + plane_scatter(
        project_t(hidden[middle_row:], down_w), project_t(hidden[:middle_row], down_w)
    )
    grad_hidden = project(grad_two_all, down_w)
    grad_gate = grad_hidden * up_lin * (sigmoid * (1.0 + gate_lin * (1.0 - sigmoid)))
    grad_up = grad_hidden * (gate_lin * sigmoid)
    grad_both = jnp.concatenate([grad_gate.astype(BF16), grad_up.astype(BF16)], axis=1)
    grad_normed_two = plane_scatter(
        project_t(grad_both[middle_row:], forward_w), project_t(grad_both[:middle_row], forward_w)
    )
    summed_forward = from_plane(ring_outer(seen_two, grad_both))
    grad_middle = upstream + norm_back(normed_two, scale_two, grad_normed_two)
    grad_one_all = plane_gather(grad_middle.astype(BF16))
    grad_attended = project(grad_one_all, out_w).astype(BF16)
    grad_qkv = attend_back(qkv_low, grad_attended, cos_rows, sin_rows, places, tok_rows)
    grad_normed_one = plane_scatter(
        project_t(grad_qkv[middle_row:], qkv_w), project_t(grad_qkv[:middle_row], qkv_w)
    )
    grad_inputs = grad_middle + norm_back(normed_one, scale_one, grad_normed_one)
    summed_out = from_plane(ring_outer(grad_one_all, attended))
    summed_qkv = from_plane(ring_outer(seen_one, grad_qkv))

    def give_back(rows):
        packed = outer_sum(recv_pick, rows.astype(BF16)).astype(BF16)
        return project(send_pick, exchange(packed))

    return (
        give_back(output),
        give_back(grad_inputs),
        gathered(summed_qkv[:, :, :head_width]),
        gathered(summed_qkv[:, :, head_width : 2 * head_width]),
        gathered(summed_qkv[:, :, 2 * head_width :]),
        gathered(summed_out).T,
        gathered(summed_forward[:, :, :hidden_width]),
        gathered(summed_forward[:, :, hidden_width:]),
        gathered(summed_down).T,
    )


def solution(mesh):
    groups, cores = mesh.shape["dp"], mesh.shape["tensor"]
    whole = Mesh(mesh.devices.reshape(groups // 4, 2, 2, cores), EVERY)
    rows = P(EVERY, None)
    tall = P(("z", "y", "x"), "c")
    wide = P("c", ("z", "y", "x"))
    in_specs = (
        rows,
        rows,
        P(("z", "y", "x")),
        P(EVERY),
        P(EVERY),
        tall,
        tall,
        tall,
        wide,
        tall,
        tall,
        wide,
    )
    out_specs = (rows, rows, tall, tall, tall, wide, tall, tall, wide)
    return jax.shard_map(
        on_device, mesh=whole, in_specs=in_specs, out_specs=out_specs, check_vma=False
    )
```

```python
import functools
import math

import jax
import jax.numpy as jnp
from jax import lax
from jax.experimental import pallas as pl
from jax.experimental.pallas import tpu as pltpu
from jax.sharding import Mesh
from jax.sharding import PartitionSpec as P

HEAD_DIM = 128
SEGS = 4
EPSILON = 1e-05
NEG_LARGE = -1e30
F32 = jnp.float32
BF16 = jnp.bfloat16
MESH = pl.DeviceIdType.MESH
IDS = ("gather_one", "gather_up", "gather_two", "gather_middle", "product_out", "product_down", "product_forward", "product_qkv")


def project(left, right):
    return jnp.dot(left, right, preferred_element_type=F32)


def project_t(left, right):
    return lax.dot_general(left, right, (((1,), (1,)), ((), ())), preferred_element_type=F32)


def outer_sum(left, right):
    return lax.dot_general(left, right, (((0,), (0,)), ((), ())), preferred_element_type=F32)


def norm_parts(values):
    center = values - jnp.mean(values, axis=-1, keepdims=True)
    spread = jnp.mean(center * center, axis=-1, keepdims=True)
    scale = lax.rsqrt(spread + EPSILON)
    return center * scale, scale


def norm_back(normed, scale, gradient):
    mean_grad = jnp.mean(gradient, axis=-1, keepdims=True)
    mean_both = jnp.mean(gradient * normed, axis=-1, keepdims=True)
    return (gradient - mean_grad - normed * mean_both) * scale


def flip(axis):
    return {axis: 1 - lax.axis_index(axis)}


def greet(axes, ring):
    barrier = pltpu.get_barrier_semaphore()
    for axis in axes:
        pl.semaphore_signal(barrier, inc=1, device_id=flip(axis), device_id_type=MESH)
    count = len(axes)
    if ring:
        total = lax.axis_size("z")
        behind = lax.rem(lax.axis_index("z") + total - 1, total)
        pl.semaphore_signal(barrier, inc=1, device_id={"z": behind}, device_id_type=MESH)
        count += 1
    pl.semaphore_wait(barrier, count)


def ring_copy(source, target, send, recv):
    total = lax.axis_size("z")
    ahead = lax.rem(lax.axis_index("z") + 1, total)
    return pltpu.make_async_remote_copy(
        src_ref=source,
        dst_ref=target,
        send_sem=send,
        recv_sem=recv,
        device_id={"z": ahead},
        device_id_type=MESH,
    )


def gather_kernel(ring, *refs):
    if ring:
        own, passing, out, passed, send, recv, local = refs
    else:
        own, out, send, recv, local = refs
    rows = own.shape[0]
    half = rows // 2

    def part(block, side):
        return out.at[pl.ds(block * rows + side * half, half)]

    def push(axis, source, target, slot):
        copy = pltpu.make_async_remote_copy(
            src_ref=source,
            dst_ref=target,
            send_sem=send.at[slot],
            recv_sem=recv.at[slot],
            device_id=flip(axis),
            device_id_type=MESH,
        )
        copy.start()
        return copy

    keep = pltpu.make_async_copy(own, out.at[pl.ds(0, rows)], local)
    keep.start()
    greet(("x", "y", "c"), ring)
    first, second = own.at[pl.ds(0, half)], own.at[pl.ds(half, half)]
    x_first = push("x", first, part(1, 0), 0)
    y_second = push("y", second, part(2, 1), 1)
    x_second = push("x", second, part(1, 1), 2)
    y_first = push("y", first, part(2, 0), 3)
    if ring:
        around = ring_copy(passing, passed, send.at[13], recv.at[13])
        around.start()
    across = [push("c", own, out.at[pl.ds(4 * rows, rows)], 4)]
    x_first.wait_recv()
    far_first = push("y", part(1, 0), part(3, 0), 5)
    across.append(push("c", part(1, 0), part(5, 0), 6))
    y_second.wait_recv()
    far_second = push("x", part(2, 1), part(3, 1), 7)
    across.append(push("c", part(2, 1), part(6, 1), 8))
    x_second.wait_recv()
    across.append(push("c", part(1, 1), part(5, 1), 9))
    y_first.wait_recv()
    across.append(push("c", part(2, 0), part(6, 0), 10))
    far_first.wait_recv()
    across.append(push("c", part(3, 0), part(7, 0), 11))
    far_second.wait_recv()
    across.append(push("c", part(3, 1), part(7, 1), 12))
    for copy in across:
        copy.wait_recv()
    for copy in across + [x_first, y_second, x_second, y_first, far_first, far_second]:
        copy.wait_send()
    keep.wait()
    if ring:
        around.wait()


def plane_gather(rows, name, passing=None):
    ring = passing is not None
    shapes = [jax.ShapeDtypeStruct((8 * rows.shape[0], rows.shape[1]), rows.dtype)]
    operands = [rows]
    if ring:
        shapes.append(jax.ShapeDtypeStruct(passing.shape, passing.dtype))
        operands.append(passing)
    got = pl.pallas_call(
        functools.partial(gather_kernel, ring),
        in_specs=[pl.BlockSpec(memory_space=pl.ANY)] * len(operands),
        out_specs=[pl.BlockSpec(memory_space=pl.ANY)] * len(shapes),
        out_shape=shapes,
        scratch_shapes=[
            pltpu.SemaphoreType.DMA((14,)),
            pltpu.SemaphoreType.DMA((14,)),
            pltpu.SemaphoreType.DMA(()),
        ],
        compiler_params=pltpu.CompilerParams(
            collective_id=IDS.index(name), has_side_effects=True
        ),
        cost_estimate=pl.CostEstimate(flops=0, bytes_accessed=120 << 20, transcendentals=0),
        name=name,
    )(*operands)
    return tuple(got) if ring else got[0]


def scatter_kernel(ring, *refs):
    if ring:
        rows_ref, weight_ref, passing, out_ref, passed = refs[:5]
    else:
        rows_ref, weight_ref, out_ref = refs[:3]
    left, weight, away, got, near, by_y, by_x, end_y, end_x, send, recv, local = refs[-12:]
    block, width = out_ref.shape
    half = block // 2
    tile = 512

    def push(axis, source, target, slot):
        copy = pltpu.make_async_remote_copy(
            src_ref=source,
            dst_ref=target,
            send_sem=send.at[slot],
            recv_sem=recv.at[slot],
            device_id=flip(axis),
            device_id_type=MESH,
        )
        copy.start()
        return copy

    fetch_weight = pltpu.make_async_copy(weight_ref, weight, local.at[8])
    fetch_weight.start()
    order = (7, 6, 3, 5, 2, 4, 1, 0)
    fetches = {}
    for index in order:
        at = pl.ds(index * block, block)
        fetches[index] = pltpu.make_async_copy(rows_ref.at[at], left.at[at], local.at[index])
        fetches[index].start()
    greet(("x", "y", "c"), ring)
    if ring:
        around = ring_copy(passing, passed, send.at[10], recv.at[10])
        around.start()
    fetch_weight.wait()

    def multiply(index, store):
        fetches[index].wait()
        here = left[pl.ds(index * block, block), :]

        @pl.loop(0, width // tile)
        def _(step):
            at = pl.ds(pl.multiple_of(step * tile, tile), tile)
            store(at, project_t(here, weight[at, :]))

    crossing = {}
    sent = []

    def compute_far(index):
        def store(at, value):
            away[index, :, at] = value.astype(BF16)

        multiply(4 + index, store)
        crossing[index] = push("c", away.at[index], got.at[index], index)

    def compute_near(index):
        crossing[index].wait_recv()

        def store(at, value):
            near[index, :, at] = (value + got[index, :, at].astype(F32)).astype(BF16)

        multiply(index, store)

    lower, upper = pl.ds(0, half), pl.ds(half, half)
    compute_far(3)
    compute_far(2)
    compute_near(3)
    y_far = push("y", near.at[3, lower], by_y.at[1], 4)
    x_far = push("x", near.at[3, upper], by_x.at[1], 5)
    compute_far(1)
    compute_near(2)
    y_near = push("y", near.at[2, lower], by_y.at[0], 6)
    compute_far(0)
    compute_near(1)
    x_near = push("x", near.at[1, upper], by_x.at[0], 7)
    compute_near(0)
    y_far.wait_recv()
    near[1, lower, :] = (near[1, lower, :].astype(F32) + by_y[1].astype(F32)).astype(BF16)
    x_last = push("x", near.at[1, lower], end_x, 8)
    x_far.wait_recv()
    near[2, upper, :] = (near[2, upper, :].astype(F32) + by_x[1].astype(F32)).astype(BF16)
    y_last = push("y", near.at[2, upper], end_y, 9)
    y_near.wait_recv()
    out_ref[lower, :] = near[0, lower, :].astype(F32) + by_y[0].astype(F32)
    x_near.wait_recv()
    out_ref[upper, :] = near[0, upper, :].astype(F32) + by_x[0].astype(F32)
    x_last.wait_recv()
    out_ref[lower, :] += end_x[...].astype(F32)
    y_last.wait_recv()
    out_ref[upper, :] += end_y[...].astype(F32)
    for copy in (crossing[0], crossing[1], crossing[2], crossing[3]):
        copy.wait_send()
    for copy in (y_far, x_far, y_near, x_near, x_last, y_last):
        copy.wait_send()
    if ring:
        around.wait()


def plane_product(rows, weight, name, passing=None):
    ring = passing is not None
    total, inner = rows.shape
    width = weight.shape[0]
    block = total // 8
    half = block // 2
    shapes = [jax.ShapeDtypeStruct((block, width), F32)]
    operands = [rows, weight]
    specs = [pl.BlockSpec(memory_space=pl.ANY)] * 2
    out_specs = [pl.BlockSpec(memory_space=pltpu.VMEM)]
    if ring:
        shapes.append(jax.ShapeDtypeStruct(passing.shape, passing.dtype))
        operands.append(passing)
        specs.append(pl.BlockSpec(memory_space=pl.ANY))
        out_specs.append(pl.BlockSpec(memory_space=pl.ANY))
    got = pl.pallas_call(
        functools.partial(scatter_kernel, ring),
        in_specs=specs,
        out_specs=out_specs,
        out_shape=shapes,
        scratch_shapes=[
            pltpu.VMEM((total, inner), BF16),
            pltpu.VMEM((width, inner), BF16),
            pltpu.VMEM((4, block, width), BF16),
            pltpu.VMEM((4, block, width), BF16),
            pltpu.VMEM((4, block, width), BF16),
            pltpu.VMEM((2, half, width), BF16),
            pltpu.VMEM((2, half, width), BF16),
            pltpu.VMEM((half, width), BF16),
            pltpu.VMEM((half, width), BF16),
            pltpu.SemaphoreType.DMA((11,)),
            pltpu.SemaphoreType.DMA((11,)),
            pltpu.SemaphoreType.DMA((9,)),
        ],
        compiler_params=pltpu.CompilerParams(
            collective_id=IDS.index(name), has_side_effects=True, vmem_limit_bytes=48 << 20
        ),
        cost_estimate=pl.CostEstimate(
            flops=2 * total * inner * width, bytes_accessed=120 << 20, transcendentals=0
        ),
        name=name,
    )(*operands)
    return tuple(got) if ring else got[0]


def ring_gather(block):
    return lax.all_gather(block, "z", axis=0, tiled=True)


def ring_sum(values):
    return lax.psum_scatter(values.astype(BF16), "z", scatter_dimension=0, tiled=True)


def to_plane(values):
    pieces = values.reshape(-1, values.shape[2])
    return lax.all_to_all(pieces, ("y", "x"), split_axis=0, concat_axis=0, tiled=True)


def spread(weight):
    rows, columns = weight.shape
    return weight.reshape(rows, 4, columns // 4).transpose(1, 0, 2).astype(BF16)


def from_plane(block):
    rows = block.shape[0] // 4
    got = lax.all_to_all(block, ("y", "x"), split_axis=0, concat_axis=0, tiled=True)
    return got.reshape(4, rows, block.shape[1])


def gathered(block):
    return block.transpose(1, 0, 2).reshape(block.shape[1], -1).astype(F32)


def turn(values, cos_rows, sin_rows):
    return values * cos_rows + pltpu.roll(values, HEAD_DIM // 2, 1) * sin_rows


def visible_of(places):
    size = places.shape[0]
    row = lax.broadcasted_iota(jnp.int32, (size, size), 0)
    column = lax.broadcasted_iota(jnp.int32, (size, size), 1)
    return (column <= row) & (row - column <= places)


def soft_of(queries, keys, visible):
    scores = project_t(queries, keys) * (1.0 / math.sqrt(HEAD_DIM))
    scores = jnp.where(visible, scores, NEG_LARGE)
    weights = jnp.exp(scores - jnp.max(scores, axis=1, keepdims=True))
    return weights / jnp.sum(weights, axis=1, keepdims=True)


def attend_kernel(lin_ref, cos_ref, sin_ref, place_ref, low_ref, out_ref):
    width = out_ref.shape[1]
    cos_rows, sin_rows = cos_ref[...], sin_ref[...]
    visible = visible_of(place_ref[...])
    for start in range(0, width, HEAD_DIM):
        here = slice(start, start + HEAD_DIM)
        key_at = slice(width + start, width + start + HEAD_DIM)
        value_at = slice(2 * width + start, 2 * width + start + HEAD_DIM)
        queries = turn(lin_ref[:, here], cos_rows, sin_rows).astype(BF16)
        keys = turn(lin_ref[:, key_at], cos_rows, sin_rows).astype(BF16)
        values = lin_ref[:, value_at].astype(BF16)
        low_ref[:, here] = queries
        low_ref[:, key_at] = keys
        low_ref[:, value_at] = values
        soft = soft_of(queries, keys, visible).astype(BF16)
        out_ref[:, here] = project(soft, values).astype(BF16)


def attend_back_kernel(low_ref, grad_ref, cos_ref, sin_ref, place_ref, out_ref):
    width = grad_ref.shape[1]
    cos_rows, sin_rows = cos_ref[...], -sin_ref[...]
    visible = visible_of(place_ref[...])
    scale = 1.0 / math.sqrt(HEAD_DIM)
    for start in range(0, width, HEAD_DIM):
        here = slice(start, start + HEAD_DIM)
        key_at = slice(width + start, width + start + HEAD_DIM)
        value_at = slice(2 * width + start, 2 * width + start + HEAD_DIM)
        queries, keys, values = low_ref[:, here], low_ref[:, key_at], low_ref[:, value_at]
        grad = grad_ref[:, here]
        soft = soft_of(queries, keys, visible)
        grad_soft = project_t(grad, values)
        inner = jnp.sum(soft * grad_soft, axis=1, keepdims=True)
        grad_scores = (soft * (grad_soft - inner)).astype(BF16)
        grad_query = project(grad_scores, keys) * scale
        grad_key = outer_sum(grad_scores, queries) * scale
        out_ref[:, here] = turn(grad_query, cos_rows, sin_rows).astype(BF16)
        out_ref[:, key_at] = turn(grad_key, cos_rows, sin_rows).astype(BF16)
        out_ref[:, value_at] = outer_sum(soft.astype(BF16), grad).astype(BF16)


def row_spec(rows, columns):
    return pl.BlockSpec((rows, columns), lambda i: (i, 0))


def attend(lin, cos_rows, sin_rows, places, block):
    rows, width = lin.shape[0], lin.shape[1] // 3
    return pl.pallas_call(
        attend_kernel,
        grid=(rows // block,),
        in_specs=[
            row_spec(block, 3 * width),
            row_spec(block, HEAD_DIM),
            row_spec(block, HEAD_DIM),
            row_spec(block, 1),
        ],
        out_specs=[row_spec(block, 3 * width), row_spec(block, width)],
        out_shape=[
            jax.ShapeDtypeStruct((rows, 3 * width), BF16),
            jax.ShapeDtypeStruct((rows, width), BF16),
        ],
        cost_estimate=pl.CostEstimate(
            flops=4 * rows * block * width,
            bytes_accessed=rows * (20 * width + 1024),
            transcendentals=rows * block * width // HEAD_DIM,
        ),
        name="attend",
    )(lin, cos_rows, sin_rows, places)


def attend_back(low, grad, cos_rows, sin_rows, places, block):
    rows, width = grad.shape
    return pl.pallas_call(
        attend_back_kernel,
        grid=(rows // block,),
        in_specs=[
            row_spec(block, 3 * width),
            row_spec(block, width),
            row_spec(block, HEAD_DIM),
            row_spec(block, HEAD_DIM),
            row_spec(block, 1),
        ],
        out_specs=row_spec(block, 3 * width),
        out_shape=jax.ShapeDtypeStruct((rows, 3 * width), BF16),
        cost_estimate=pl.CostEstimate(
            flops=10 * rows * block * width,
            bytes_accessed=rows * (14 * width + 1024),
            transcendentals=rows * block * width // HEAD_DIM,
        ),
        name="attend_back",
    )(low, grad, cos_rows, sin_rows, places)


def plane_places(segment_ids):
    segments = lax.all_gather(segment_ids, ("y", "x"), axis=0)
    groups, size = segments.shape
    numbers = jnp.arange(SEGS, dtype=jnp.int32)
    starts = jnp.sum((segments[:, :, None] < numbers).astype(jnp.int32), axis=1)
    onehot = segments[:, :, None] == numbers
    offset = jnp.sum(jnp.where(onehot, starts[:, None, :], 0), axis=2)
    places = jnp.arange(size, dtype=jnp.int32)[None, :] - offset
    places = places.reshape(2, 2, 2, size // 2)
    places = jnp.where(lax.axis_index("y") == 1, places[::-1], places)
    places = jnp.where(lax.axis_index("x") == 1, places[:, ::-1], places)
    places = jnp.where(lax.axis_index("c") == 1, places[:, :, ::-1], places)
    return places.transpose(2, 0, 1, 3).reshape(-1, 1)


def after(values, *gates):
    return lax.optimization_barrier((values,) + gates)[0]


EVERY = ("z", "y", "x", "c")


def exchange(rows):
    return lax.all_to_all(rows, EVERY, split_axis=0, concat_axis=0, tiled=True)


def on_device(
    tokens_in,
    cotangent,
    segment_ids,
    destination,
    source,
    w_query,
    w_key,
    w_value,
    w_out,
    w_gate,
    w_up,
    w_down,
):
    tok_rows = tokens_in.shape[0]
    devices = lax.axis_size(EVERY)
    per_peer = tok_rows // devices
    row_index = jnp.arange(tok_rows, dtype=jnp.int32)
    peer_to = destination // tok_rows
    ahead_rows = (peer_to[None, :] == peer_to[:, None]) & (
        destination[None, :] < destination[:, None]
    )
    send_slot = peer_to * per_peer + jnp.sum(ahead_rows.astype(jnp.int32), axis=1)
    peer_from = source // tok_rows
    before = (peer_from[None, :] == peer_from[:, None]) & (row_index[None, :] < row_index[:, None])
    recv_slot = peer_from * per_peer + jnp.sum(before.astype(jnp.int32), axis=1)
    send_pick = (send_slot[:, None] == row_index[None, :]).astype(BF16)
    recv_pick = (recv_slot[:, None] == row_index[None, :]).astype(BF16)

    arrived = project(recv_pick, exchange(outer_sum(send_pick, tokens_in).astype(BF16)))
    upstream_low = project(
        recv_pick, exchange(outer_sum(send_pick, cotangent).astype(BF16))
    ).astype(BF16)
    upstream = upstream_low.astype(F32)

    attention_block = to_plane(
        jnp.concatenate([spread(w_query), spread(w_key), spread(w_value), spread(w_out.T)], axis=2)
    )
    forward_block = to_plane(jnp.concatenate([spread(w_gate), spread(w_up)], axis=2))
    down_block = to_plane(spread(w_down.T))
    attention_w = ring_gather(attention_block)
    forward_w = ring_gather(after(forward_block, attention_block))
    down_w = ring_gather(after(down_block, forward_block))
    head_width = attention_w.shape[1] // 4
    hidden_width = down_w.shape[1]
    qkv_w = attention_w[:, : 3 * head_width]
    out_w = attention_w[:, 3 * head_width :]

    places = plane_places(segment_ids)
    half_dim = HEAD_DIM // 2
    frequency = jnp.exp(
        -jnp.arange(half_dim, dtype=F32) * (2.0 * math.log(10000.0) / HEAD_DIM)
    )
    angles = places.astype(F32) * frequency[None, :]
    cos_half, sin_half = jnp.cos(angles), jnp.sin(angles)
    cos_rows = jnp.concatenate([cos_half, cos_half], axis=1)
    sin_rows = jnp.concatenate([-sin_half, sin_half], axis=1)

    normed_one, scale_one = norm_parts(arrived)
    seen_one = plane_gather(normed_one.astype(BF16), "gather_one")
    grad_two_all = plane_gather(after(upstream_low, seen_one), "gather_up")
    qkv_lin = project(seen_one, qkv_w)
    qkv_low, attended = attend(qkv_lin, cos_rows, sin_rows, places, tok_rows)
    middle = arrived + plane_product(attended, out_w, "product_out")
    normed_two, scale_two = norm_parts(middle)
    seen_two = plane_gather(normed_two.astype(BF16), "gather_two")

    gate_lin = project(seen_two, forward_w[:, :hidden_width])
    up_lin = project(seen_two, forward_w[:, hidden_width:])
    sigmoid = jax.nn.sigmoid(gate_lin)
    hidden = (gate_lin * sigmoid * up_lin).astype(BF16)
    summed_down = from_plane(ring_sum(outer_sum(grad_two_all, hidden)))
    grad_hidden = project(grad_two_all, down_w)
    grad_gate = grad_hidden * up_lin * (sigmoid * (1.0 + gate_lin * (1.0 - sigmoid)))
    grad_up = grad_hidden * (gate_lin * sigmoid)
    grad_both = jnp.concatenate([grad_gate.astype(BF16), grad_up.astype(BF16)], axis=1)
    summed_forward = from_plane(ring_sum(outer_sum(seen_two, grad_both)))
    grad_normed_two = plane_product(grad_both, forward_w, "product_forward")
    grad_middle = upstream + norm_back(normed_two, scale_two, grad_normed_two)
    grad_one_all = plane_gather(grad_middle.astype(BF16), "gather_middle")
    grad_attended = project(grad_one_all, out_w).astype(BF16)
    grad_qkv = attend_back(qkv_low, grad_attended, cos_rows, sin_rows, places, tok_rows)
    summed_qkv = from_plane(ring_sum(outer_sum(seen_one, grad_qkv)))
    summed_out = from_plane(ring_sum(outer_sum(grad_one_all, attended)))
    grad_normed_one = plane_product(grad_qkv, qkv_w, "product_qkv")
    grad_inputs = grad_middle + norm_back(normed_one, scale_one, grad_normed_one)
    output = middle + plane_product(after(hidden, grad_normed_one), down_w, "product_down")

    def give_back(rows):
        packed = outer_sum(recv_pick, rows.astype(BF16)).astype(BF16)
        return project(send_pick, exchange(packed))

    return (
        give_back(output),
        give_back(grad_inputs),
        gathered(summed_qkv[:, :, :head_width]),
        gathered(summed_qkv[:, :, head_width : 2 * head_width]),
        gathered(summed_qkv[:, :, 2 * head_width :]),
        gathered(summed_out).T,
        gathered(summed_forward[:, :, :hidden_width]),
        gathered(summed_forward[:, :, hidden_width:]),
        gathered(summed_down).T,
    )


def solution(mesh):
    groups, cores = mesh.shape["dp"], mesh.shape["tensor"]
    whole = Mesh(mesh.devices.reshape(groups // 4, 2, 2, cores), EVERY)
    rows = P(EVERY, None)
    tall = P(("z", "y", "x"), "c")
    wide = P("c", ("z", "y", "x"))
    in_specs = (
        rows,
        rows,
        P(("z", "y", "x")),
        P(EVERY),
        P(EVERY),
        tall,
        tall,
        tall,
        wide,
        tall,
        tall,
        wide,
    )
    out_specs = (rows, rows, tall, tall, tall, wide, tall, tall, wide)
    return jax.shard_map(
        on_device, mesh=whole, in_specs=in_specs, out_specs=out_specs, check_vma=False
    )
```

```python
import functools
import math

import jax
import jax.numpy as jnp
from jax import lax
from jax.experimental import pallas as pl
from jax.experimental.pallas import tpu as pltpu
from jax.sharding import Mesh
from jax.sharding import PartitionSpec as P

HEAD_DIM = 128
SEGS = 4
EPSILON = 1e-05
NEG_LARGE = -1e30
F32 = jnp.float32
BF16 = jnp.bfloat16
MESH = pl.DeviceIdType.MESH
IDS = (
    "dispatch",
    "gather_one",
    "gather_two",
    "gather_middle",
    "product_out",
    "product_forward",
    "product_qkv",
    "product_down",
    "gather_up",
    "attend",
    "attend_back",
)


def project(left, right):
    return jnp.dot(left, right, preferred_element_type=F32)


def project_t(left, right):
    return lax.dot_general(left, right, (((1,), (1,)), ((), ())), preferred_element_type=F32)


def outer_sum(left, right):
    return lax.dot_general(left, right, (((0,), (0,)), ((), ())), preferred_element_type=F32)


def norm_parts(values):
    center = values - jnp.mean(values, axis=-1, keepdims=True)
    spread = jnp.mean(center * center, axis=-1, keepdims=True)
    scale = lax.rsqrt(spread + EPSILON)
    return center * scale, scale


def norm_back(normed, scale, gradient):
    mean_grad = jnp.mean(gradient, axis=-1, keepdims=True)
    mean_both = jnp.mean(gradient * normed, axis=-1, keepdims=True)
    return (gradient - mean_grad - normed * mean_both) * scale


def flip(*axes):
    return {axis: 1 - lax.axis_index(axis) for axis in axes}


def owner_at(step):
    total = lax.axis_size("z")
    return lax.rem(lax.axis_index("z") + total - step, total)


def greet(peers, ring):
    barrier = pltpu.get_barrier_semaphore()
    for axes in peers:
        pl.semaphore_signal(barrier, inc=1, device_id=flip(*axes), device_id_type=MESH)
    count = len(peers)
    if ring:
        pl.semaphore_signal(barrier, inc=1, device_id={"z": owner_at(1)}, device_id_type=MESH)
        count += 1
    pl.semaphore_wait(barrier, count)


def push(axes, source, target, send, recv):
    copy = pltpu.make_async_remote_copy(
        src_ref=source,
        dst_ref=target,
        send_sem=send,
        recv_sem=recv,
        device_id=flip(*axes),
        device_id_type=MESH,
    )
    copy.start()
    return copy


class Ride:
    def __init__(self, gathers=(), sums=()):
        self.gathers, self.sums = tuple(gathers), tuple(sums)
        self.operands, self.shapes, self.scratch = [], [], []
        self.aliases = {}
        self.steps = 0
        for whole, first, count in self.gathers:
            self.aliases[len(self.operands)] = len(self.shapes)
            self.operands.append(whole)
            self.shapes.append(jax.ShapeDtypeStruct(whole.shape, whole.dtype))
            self.steps += count
        for running, adds in self.sums:
            self.operands += [running, *adds]
            self.shapes.append(jax.ShapeDtypeStruct(running.shape, running.dtype))
            self.steps += 1 + len(adds)
            for _ in adds:
                self.scratch += [
                    pltpu.VMEM(running.shape, running.dtype),
                    pltpu.VMEM(running.shape, running.dtype),
                    pltpu.SemaphoreType.DMA(()),
                ]
        if self.steps:
            self.scratch += [
                pltpu.SemaphoreType.DMA((self.steps,)),
                pltpu.SemaphoreType.DMA((self.steps,)),
            ]

    def board(self, inputs, outputs, scratch):
        inputs, outputs, scratch = list(inputs), list(outputs), list(scratch)
        self.loads, self.copies, self.prepares, self.begun = [], [], [], 0
        if not self.steps:
            return
        send, recv = scratch[-2], scratch[-1]
        ahead = {"z": owner_at(lax.axis_size("z") - 1)}

        def plan(source, target, prepare=None):
            slot = len(self.copies)
            self.copies.append(
                pltpu.make_async_remote_copy(
                    src_ref=source,
                    dst_ref=target,
                    send_sem=send.at[slot],
                    recv_sem=recv.at[slot],
                    device_id=ahead,
                    device_id_type=MESH,
                )
            )
            self.prepares.append(prepare)

        def adding(load, landed, own):
            def prepare():
                load.wait()
                height = 64

                @pl.loop(0, own.shape[0] // height)
                def _(index):
                    at = pl.ds(pl.multiple_of(index * height, height), height)
                    own[at, :] = (own[at, :].astype(F32) + landed[at, :].astype(F32)).astype(BF16)

            return prepare

        for _, first, count in self.gathers:
            inputs.pop(0)
            whole = outputs.pop(0)
            rows = whole.shape[0] // lax.axis_size("z")
            for step in range(first, first + count):
                at = pl.ds(pl.multiple_of(owner_at(step) * rows, rows), rows)
                plan(whole.at[at], whole.at[at])
        for _, adds in self.sums:
            running = inputs.pop(0)
            final = outputs.pop(0)
            held = []
            for _ in adds:
                landed, own, loaded = scratch[:3]
                scratch = scratch[3:]
                load = pltpu.make_async_copy(inputs.pop(0), own, loaded)
                held.append((load, landed, own))
                self.loads.append(load)
            targets = [landed for _, landed, _ in held] + [final]
            plan(running, targets[0])
            for (load, landed, own), target in zip(held, targets[1:]):
                plan(own, target, adding(load, landed, own))

    def start(self, number):
        if self.prepares[number]:
            self.prepares[number]()
        self.copies[number].start()
        self.begun = number + 1

    def begin(self):
        for load in self.loads:
            load.start()
        if self.copies:
            self.start(0)

    def advance(self):
        if 0 < self.begun < len(self.copies):
            self.copies[self.begun - 1].wait_recv()
            self.start(self.begun)

    def finish(self):
        while self.begun < len(self.copies):
            self.advance()
        if self.copies:
            self.copies[-1].wait_recv()
        for copy in self.copies:
            copy.wait_send()


def block_at(core, y, x):
    def moved(axis, offset):
        here = lax.axis_index(axis)
        return 1 - here if offset else here

    return (moved("y", y) * 2 + moved("x", x)) * 2 + moved("c", core)


def communicate(body, operands, specs, shapes, out_specs, scratch, name, ride, flops=0):
    ride = ride or Ride()
    count_in, count_out, count_scratch = len(operands), len(shapes), len(scratch)
    all_in = count_in + len(ride.operands)
    all_out = count_out + len(ride.shapes)

    def kernel(*refs):
        inputs, outputs, held = refs[:all_in], refs[all_in : all_in + all_out], refs[all_in + all_out :]
        ride.board(inputs[count_in:], outputs[count_out:], held[count_scratch:])
        body(inputs[:count_in], outputs[:count_out], held[:count_scratch], ride)

    anywhere = pl.BlockSpec(memory_space=pl.ANY)
    got = pl.pallas_call(
        kernel,
        in_specs=list(specs) + [anywhere] * len(ride.operands),
        out_specs=list(out_specs) + [anywhere] * len(ride.shapes),
        out_shape=list(shapes) + ride.shapes,
        scratch_shapes=list(scratch) + ride.scratch,
        input_output_aliases={count_in + k: count_out + v for k, v in ride.aliases.items()},
        compiler_params=pltpu.CompilerParams(
            collective_id=IDS.index(name), has_side_effects=True, vmem_limit_bytes=50 << 20
        ),
        cost_estimate=pl.CostEstimate(
            flops=flops, bytes_accessed=120 << 20, transcendentals=0
        ),
        name=name,
    )(*operands, *ride.operands)
    return list(got)


class OwnRide(Ride):
    def __init__(self, count):
        super().__init__()
        self.steps = count

    def take(self, whole, semaphores):
        self.gathers = ((None, 0, self.steps),)
        super().board([None], [whole], semaphores)


def dispatch_kernel(count, narrow, steps, *refs):
    inputs, refs = refs[:count], refs[count:]
    places, packed, refs = refs[0], refs[1], refs[2:]
    wholes, refs = refs[: count - narrow + 1], refs[count - narrow + 1 :]
    all_places, landed, send, recv, local, rows_send, rows_recv = refs[:7]
    ride = OwnRide(steps)
    ride.take(wholes[0], refs[7:])
    me_y, me_x = lax.axis_index("y"), lax.axis_index("x")
    me_z, me_c = lax.axis_index("z"), lax.axis_index("c")
    rank = me_y * 2 + me_x
    rows = inputs[0].shape[0]
    at = pl.ds(pl.multiple_of(me_z * (4 * rows) + rank * rows, rows), rows)
    peers = ((("x",), me_y * 2 + 1 - me_x), (("y",), (1 - me_y) * 2 + me_x))
    peers += ((("y", "x"), (1 - me_y) * 2 + 1 - me_x),)

    def piece(index, owner):
        width = inputs[index].shape[1] // 4
        return inputs[index].at[:, pl.ds(pl.multiple_of(owner * width, width), width)]

    def target(index):
        width = inputs[index].shape[1] // 4
        if index < narrow:
            return wholes[0].at[at, pl.ds(index * width, width)]
        return wholes[index - narrow + 1].at[at]

    devices = packed.shape[0]
    me = (me_z * 4 + rank) * 2 + me_c
    keeps = [
        pltpu.make_async_copy(piece(index, rank), target(index), local.at[index])
        for index in range(count)
    ]
    keeps.append(pltpu.make_async_copy(places, all_places.at[rank], local.at[count]))
    keeps.append(pltpu.make_async_copy(packed.at[me], landed.at[me], local.at[count + 1]))
    for keep in keeps:
        keep.start()

    def device(shift):
        other = lax.rem(me + shift, devices)
        chip = other // 2
        return {"z": chip // 4, "y": lax.rem(chip // 2, 2), "x": lax.rem(chip, 2), "c": lax.rem(other, 2)}

    barrier = pltpu.get_barrier_semaphore()

    @pl.loop(1, devices)
    def _(shift):
        pl.semaphore_signal(barrier, inc=1, device_id=device(shift), device_id_type=MESH)

    pl.semaphore_wait(barrier, devices - 1)
    copies = {}

    def share(index, source_of, goal):
        for number, (axes, owner) in enumerate(peers):
            slot = 3 * index + number
            copies[index, number] = push(axes, source_of(owner), goal, send.at[slot], recv.at[slot])

    def arrive(index):
        keeps[index].wait()
        for number in range(3):
            copies[index, number].wait_recv()

    for index in range(narrow):
        share(index, functools.partial(piece, index), target(index))
    share(count, lambda owner: places, all_places.at[rank])

    @pl.loop(1, devices)
    def _(shift):
        other = lax.rem(me + shift, devices)
        pltpu.make_async_remote_copy(
            src_ref=packed.at[other],
            dst_ref=landed.at[me],
            send_sem=rows_send,
            recv_sem=rows_recv,
            device_id=device(shift),
            device_id_type=MESH,
        ).start()

    for index in range(narrow):
        arrive(index)
    ride.begin()
    for index in range(narrow, count):
        share(index, functools.partial(piece, index), target(index))
    most = pl.ds(0, devices - 1)
    pltpu.make_async_copy(packed.at[most], landed.at[most], rows_recv).wait()
    ride.advance()
    for index in range(narrow, count + 1):
        arrive(index)
    keeps[count + 1].wait()
    ride.finish()
    for copy in copies.values():
        copy.wait_send()
    pltpu.make_async_copy(packed.at[most], packed.at[most], rows_send).wait()


def dispatch(weights, narrow, places, packed, steps, name):
    rows = weights[0].shape[0]
    total = lax.axis_size("z")
    anywhere = pl.BlockSpec(memory_space=pl.ANY)
    count = len(weights)
    widths = [sum(weight.shape[1] // 4 for weight in weights[:narrow])]
    widths += [weight.shape[1] // 4 for weight in weights[narrow:]]
    shapes = [jax.ShapeDtypeStruct((total * 4 * rows, width), BF16) for width in widths]
    shapes.append(jax.ShapeDtypeStruct((4, *places.shape), places.dtype))
    shapes.append(jax.ShapeDtypeStruct(packed.shape, packed.dtype))
    return pl.pallas_call(
        functools.partial(dispatch_kernel, count, narrow, steps),
        in_specs=[anywhere] * (count + 2),
        out_specs=[anywhere] * len(shapes),
        out_shape=shapes,
        scratch_shapes=[
            pltpu.SemaphoreType.DMA((3 * count + 3,)),
            pltpu.SemaphoreType.DMA((3 * count + 3,)),
            pltpu.SemaphoreType.DMA((count + 2,)),
            pltpu.SemaphoreType.DMA(()),
            pltpu.SemaphoreType.DMA(()),
            pltpu.SemaphoreType.DMA((steps,)),
            pltpu.SemaphoreType.DMA((steps,)),
        ],
        compiler_params=pltpu.CompilerParams(
            collective_id=IDS.index(name), has_side_effects=True
        ),
        cost_estimate=pl.CostEstimate(flops=0, bytes_accessed=120 << 20, transcendentals=0),
        name=name,
    )(*weights, places, packed)


def gather_body(inputs, outputs, scratch, ride):
    (own,), (out,), (send, recv, local) = inputs, outputs, scratch
    rows = own.shape[0]
    half = rows // 2

    def part(core, y, x, side):
        start = block_at(core, y, x) * rows + side * half
        return out.at[pl.ds(pl.multiple_of(start, half), half)]

    def over(axis, source, target, slot):
        return push((axis,), source, target, send.at[slot], recv.at[slot])

    def across(y, x, side, slot):
        here = part(0, y, x, side)
        return over("c", here, here, slot)

    whole = out.at[pl.ds(pl.multiple_of(block_at(0, 0, 0) * rows, rows), rows)]
    keep = pltpu.make_async_copy(own, whole, local)
    keep.start()
    greet((("x",), ("y",), ("c",)), ride.steps > 0)
    first, second = own.at[pl.ds(0, half)], own.at[pl.ds(half, half)]
    x_first = over("x", first, part(0, 0, 0, 0), 0)
    y_second = over("y", second, part(0, 0, 0, 1), 1)
    x_second = over("x", second, part(0, 0, 0, 1), 2)
    y_first = over("y", first, part(0, 0, 0, 0), 3)
    ride.begin()
    crossed = [over("c", own, whole, 4)]
    x_first.wait_recv()
    far_first = over("y", part(0, 0, 1, 0), part(0, 0, 1, 0), 5)
    crossed.append(across(0, 1, 0, 6))
    y_second.wait_recv()
    far_second = over("x", part(0, 1, 0, 1), part(0, 1, 0, 1), 7)
    crossed.append(across(1, 0, 1, 8))
    x_second.wait_recv()
    crossed.append(across(0, 1, 1, 9))
    y_first.wait_recv()
    crossed.append(across(1, 0, 0, 10))
    ride.advance()
    far_first.wait_recv()
    crossed.append(across(1, 1, 0, 11))
    far_second.wait_recv()
    crossed.append(across(1, 1, 1, 12))
    for copy in crossed:
        copy.wait_recv()
    ride.finish()
    for copy in crossed + [x_first, y_second, x_second, y_first, far_first, far_second]:
        copy.wait_send()
    keep.wait()


def plane_gather(rows, name, ride=None):
    got = communicate(
        gather_body,
        [rows],
        [pl.BlockSpec(memory_space=pl.ANY)],
        [jax.ShapeDtypeStruct((8 * rows.shape[0], rows.shape[1]), rows.dtype)],
        [pl.BlockSpec(memory_space=pl.ANY)],
        [
            pltpu.SemaphoreType.DMA((13,)),
            pltpu.SemaphoreType.DMA((13,)),
            pltpu.SemaphoreType.DMA(()),
        ],
        name,
        ride,
    )
    return got[0], got[1:]


def product_body(starts, inputs, outputs, scratch, ride):
    (out_ref,) = outputs
    left, weight, away, got, near, by_y, by_x, end_y, end_x, send, recv, local = scratch
    block, width = out_ref.shape
    half = block // 2
    tile = 512
    pairs = [(inputs[2 * i], inputs[2 * i + 1], start) for i, start in enumerate(starts)]

    def over(axis, source, target, slot):
        return push((axis,), source, target, send.at[slot], recv.at[slot])

    waits = {"weight": []}
    column = 0
    for index, (rows_ref, weight_ref, start) in enumerate(pairs):
        inner = rows_ref.shape[1]
        copy = pltpu.make_async_copy(
            weight_ref.at[:, pl.ds(start, inner)],
            weight.at[:, pl.ds(column, inner)],
            local.at[index, 8],
        )
        copy.start()
        waits["weight"].append(copy)
        column += inner
    order = ((1, 1, 1), (1, 1, 0), (0, 1, 1), (1, 0, 1), (0, 1, 0), (1, 0, 0), (0, 0, 1), (0, 0, 0))
    for slot, key in enumerate(order):
        start = pl.multiple_of(block_at(*key) * block, block)
        waits[key] = []
        column = 0
        for index, (rows_ref, _, _) in enumerate(pairs):
            inner = rows_ref.shape[1]
            copy = pltpu.make_async_copy(
                rows_ref.at[pl.ds(start, block)],
                left.at[slot, :, pl.ds(column, inner)],
                local.at[index, slot],
            )
            copy.start()
            waits[key].append(copy)
            column += inner
    greet((("x",), ("y",), ("c",)), ride.steps > 0)
    ride.begin()
    for copy in waits["weight"]:
        copy.wait()

    def multiply(key, store):
        for copy in waits[key]:
            copy.wait()
        here = left[order.index(key)]

        @pl.loop(0, width // tile)
        def _(step):
            at = pl.ds(pl.multiple_of(step * tile, tile), tile)
            store(at, project_t(here, weight[at, :]))

    crossing = {}

    def compute_far(y, x):
        index = 2 * y + x

        def store(at, value):
            away[index, :, at] = value.astype(BF16)

        multiply((1, y, x), store)
        crossing[index] = over("c", away.at[index], got.at[index], index)

    def compute_near(y, x):
        index = 2 * y + x
        crossing[index].wait_recv()

        def store(at, value):
            near[index, :, at] = (value + got[index, :, at].astype(F32)).astype(BF16)

        multiply((0, y, x), store)

    lower, upper = pl.ds(0, half), pl.ds(half, half)
    compute_far(1, 1)
    compute_far(1, 0)
    compute_near(1, 1)
    y_far = over("y", near.at[3, lower], by_y.at[1], 4)
    x_far = over("x", near.at[3, upper], by_x.at[1], 5)
    compute_far(0, 1)
    compute_near(1, 0)
    y_near = over("y", near.at[2, lower], by_y.at[0], 6)
    compute_far(0, 0)
    compute_near(0, 1)
    x_near = over("x", near.at[1, upper], by_x.at[0], 7)
    compute_near(0, 0)
    y_far.wait_recv()
    near[1, lower, :] = (near[1, lower, :].astype(F32) + by_y[1].astype(F32)).astype(BF16)
    x_last = over("x", near.at[1, lower], end_x, 8)
    x_far.wait_recv()
    near[2, upper, :] = (near[2, upper, :].astype(F32) + by_x[1].astype(F32)).astype(BF16)
    y_last = over("y", near.at[2, upper], end_y, 9)
    ride.advance()
    y_near.wait_recv()
    out_ref[lower, :] = near[0, lower, :].astype(F32) + by_y[0].astype(F32)
    x_near.wait_recv()
    out_ref[upper, :] = near[0, upper, :].astype(F32) + by_x[0].astype(F32)
    x_last.wait_recv()
    out_ref[lower, :] += end_x[...].astype(F32)
    y_last.wait_recv()
    out_ref[upper, :] += end_y[...].astype(F32)
    ride.finish()
    for copy in list(crossing.values()) + [y_far, x_far, y_near, x_near, x_last, y_last]:
        copy.wait_send()


def plane_product(pairs, name, ride=None):
    total = pairs[0][0].shape[0]
    inner = sum(rows.shape[1] for rows, _, _ in pairs)
    width = pairs[0][1].shape[0]
    block = total // 8
    half = block // 2
    operands = []
    for rows, weight, _ in pairs:
        operands += [rows, weight]
    got = communicate(
        functools.partial(product_body, [start for _, _, start in pairs]),
        operands,
        [pl.BlockSpec(memory_space=pl.ANY)] * len(operands),
        [jax.ShapeDtypeStruct((block, width), F32)],
        [pl.BlockSpec(memory_space=pltpu.VMEM)],
        [
            pltpu.VMEM((8, block, inner), BF16),
            pltpu.VMEM((width, inner), BF16),
            pltpu.VMEM((4, block, width), BF16),
            pltpu.VMEM((4, block, width), BF16),
            pltpu.VMEM((4, block, width), BF16),
            pltpu.VMEM((2, half, width), BF16),
            pltpu.VMEM((2, half, width), BF16),
            pltpu.VMEM((half, width), BF16),
            pltpu.VMEM((half, width), BF16),
            pltpu.SemaphoreType.DMA((10,)),
            pltpu.SemaphoreType.DMA((10,)),
            pltpu.SemaphoreType.DMA((len(pairs), 9)),
        ],
        name,
        ride,
        flops=2 * total * inner * width,
    )
    return got[0], got[1:]


def ring_next(values):
    total = lax.axis_size("z")
    return lax.ppermute(values, "z", [(i, (i + 1) % total) for i in range(total)])


def ring_rows(whole, owner):
    rows = whole.shape[0] // lax.axis_size("z")
    return lax.dynamic_slice(whole, (owner * rows, 0), (rows, whole.shape[1]))


class Gathered:
    def __init__(self, whole, step=0):
        self.whole, self.step = whole, step

    def ride(self, count):
        count = min(count, lax.axis_size("z") - 1 - self.step)
        item = (self.whole, self.step, count)
        self.step += count
        return item

    def land(self, whole):
        self.whole = whole

    def walk(self, count):
        total = lax.axis_size("z")
        rows = self.whole.shape[0] // total
        last = min(self.step + count, total - 1)
        current = ring_rows(self.whole, owner_at(self.step)) if self.step < last else None
        while self.step < last:
            self.step += 1
            current = ring_next(current)
            self.whole = lax.dynamic_update_slice(self.whole, current, (owner_at(self.step) * rows, 0))

    def finish(self):
        self.walk(lax.axis_size("z"))
        return self.whole


class Summed:
    def __init__(self, whole):
        self.whole, self.step = whole, 0
        self.running = ring_rows(whole, owner_at(1))

    def block(self, step):
        return ring_rows(self.whole, owner_at((step + 1) % lax.axis_size("z")))

    def ride(self, count):
        count = min(count, lax.axis_size("z") - 1 - self.step)
        adds = tuple(self.block(self.step + 1 + k) for k in range(count - 1))
        self.step += count
        return (self.running, adds)

    def land(self, received):
        self.running = (received.astype(F32) + self.block(self.step).astype(F32)).astype(BF16)

    def walk(self, count):
        for _ in range(min(count, lax.axis_size("z") - 1 - self.step)):
            self.step += 1
            self.land(ring_next(self.running))

    def finish(self):
        self.walk(lax.axis_size("z"))
        return self.running


def from_plane(block):
    rows = block.shape[0] // 4
    me_y, me_x = lax.axis_index("y"), lax.axis_index("x")

    def piece(y, x):
        return lax.dynamic_slice(block, ((y * 2 + x) * rows, 0), (rows, block.shape[1]))

    own = piece(me_y, me_x)
    by_x = lax.ppermute(piece(me_y, 1 - me_x), "x", ((0, 1), (1, 0)))
    by_y = lax.ppermute(piece(1 - me_y, me_x), "y", ((0, 1), (1, 0)))
    far = lax.ppermute(piece(1 - me_y, 1 - me_x), ("y", "x"), ((0, 3), (1, 2), (2, 1), (3, 0)))

    def chosen(y, x):
        same_y, same_x = me_y == y, me_x == x
        return jnp.where(
            same_y, jnp.where(same_x, own, by_x), jnp.where(same_x, by_y, far)
        )

    return [chosen(y, x) for y in range(2) for x in range(2)]


def side_by_side(pieces, start=0, stop=None):
    return jnp.concatenate([piece[:, start:stop].astype(F32) for piece in pieces], axis=1)


def turn(values, cos_rows, sin_rows):
    return values * cos_rows + pltpu.roll(values, HEAD_DIM // 2, 1) * sin_rows


def visible_of(places):
    size = places.shape[0]
    row = lax.broadcasted_iota(jnp.int32, (size, size), 0)
    column = lax.broadcasted_iota(jnp.int32, (size, size), 1)
    return (column <= row) & (row - column <= places)


def soft_of(queries, keys, visible):
    scores = project_t(queries, keys) * (1.0 / math.sqrt(HEAD_DIM))
    scores = jnp.where(visible, scores, NEG_LARGE)
    weights = jnp.exp(scores - jnp.max(scores, axis=1, keepdims=True))
    return weights / jnp.sum(weights, axis=1, keepdims=True)


def attend_body(inputs, outputs):
    seen_ref, weight_ref, cos_ref, sin_ref, place_ref = inputs
    low_ref, out_ref = outputs
    width = out_ref.shape[1]
    cos_rows, sin_rows = cos_ref[...], sin_ref[...]
    visible = visible_of(place_ref[...])
    lin = project(seen_ref[...], weight_ref[...])
    for start in range(0, width, HEAD_DIM):
        here = slice(start, start + HEAD_DIM)
        key_at = slice(width + start, width + start + HEAD_DIM)
        value_at = slice(2 * width + start, 2 * width + start + HEAD_DIM)
        queries = turn(lin[:, here], cos_rows, sin_rows).astype(BF16)
        keys = turn(lin[:, key_at], cos_rows, sin_rows).astype(BF16)
        values = lin[:, value_at].astype(BF16)
        low_ref[:, here] = queries
        low_ref[:, key_at] = keys
        low_ref[:, value_at] = values
        soft = soft_of(queries, keys, visible).astype(BF16)
        out_ref[:, here] = project(soft, values).astype(BF16)


def attend_back_body(inputs, outputs):
    low_ref, seen_ref, weight_ref, cos_ref, sin_ref, place_ref = inputs
    (out_ref,) = outputs
    width = weight_ref.shape[1]
    cos_rows, sin_rows = cos_ref[...], -sin_ref[...]
    visible = visible_of(place_ref[...])
    scale = 1.0 / math.sqrt(HEAD_DIM)
    grad_all = project(seen_ref[...], weight_ref[...]).astype(BF16)
    for start in range(0, width, HEAD_DIM):
        here = slice(start, start + HEAD_DIM)
        key_at = slice(width + start, width + start + HEAD_DIM)
        value_at = slice(2 * width + start, 2 * width + start + HEAD_DIM)
        queries, keys, values = low_ref[:, here], low_ref[:, key_at], low_ref[:, value_at]
        grad = grad_all[:, here]
        soft = soft_of(queries, keys, visible)
        grad_soft = project_t(grad, values)
        inner = jnp.sum(soft * grad_soft, axis=1, keepdims=True)
        grad_scores = (soft * (grad_soft - inner)).astype(BF16)
        grad_query = project(grad_scores, keys) * scale
        grad_key = outer_sum(grad_scores, queries) * scale
        out_ref[:, here] = turn(grad_query, cos_rows, sin_rows).astype(BF16)
        out_ref[:, key_at] = turn(grad_key, cos_rows, sin_rows).astype(BF16)
        out_ref[:, value_at] = outer_sum(soft.astype(BF16), grad).astype(BF16)


def plane_peers():
    me_y, me_x = lax.axis_index("y"), lax.axis_index("x")
    return (
        (("x",), me_y * 2 + 1 - me_x),
        (("y",), (1 - me_y) * 2 + me_x),
        (("y", "x"), (1 - me_y) * 2 + 1 - me_x),
    )


def collect_copies(blocks, outs, send, recv, local):
    rank = lax.axis_index("y") * 2 + lax.axis_index("x")
    keeps, copies = [], []
    for index, (block, out) in enumerate(zip(blocks, outs)):
        rows = block.shape[0] // 4

        def piece(owner, block=block, rows=rows):
            return block.at[pl.ds(pl.multiple_of(owner * rows, rows), rows)]

        keeps.append(pltpu.make_async_copy(piece(rank), out.at[rank], local.at[index]))
        for number, (axes, owner) in enumerate(plane_peers()):
            copies.append(
                pltpu.make_async_remote_copy(
                    src_ref=piece(owner),
                    dst_ref=out.at[rank],
                    send_sem=send.at[3 * index + number],
                    recv_sem=recv.at[3 * index + number],
                    device_id=flip(*axes),
                    device_id_type=MESH,
                )
            )
    return keeps, copies


def collected_shape(block):
    return jax.ShapeDtypeStruct((4, block.shape[0] // 4, block.shape[1]), block.dtype)


def by_blocks(body, operands, specs, shapes, out_specs, blocks, name, ride, flops, collect=()):
    extra = len(collect)
    operands, shapes = list(operands) + list(collect), list(shapes)
    shapes += [collected_shape(block) for block in collect]
    anywhere = pl.BlockSpec(memory_space=pl.ANY)
    specs, out_specs = list(specs) + [anywhere] * extra, list(out_specs) + [anywhere] * extra
    scratch = []
    if extra:
        scratch = [
            pltpu.SemaphoreType.DMA((3 * extra,)),
            pltpu.SemaphoreType.DMA((3 * extra,)),
            pltpu.SemaphoreType.DMA((extra,)),
        ]
    count_in, count_out = len(operands), len(shapes)
    all_in = count_in + len(ride.operands)
    all_out = count_out + len(ride.shapes)

    def kernel(*refs):
        inputs, outputs, held = refs[:all_in], refs[all_in : all_in + all_out], refs[all_in + all_out :]
        step = pl.program_id(0)
        ride.board(inputs[count_in:], outputs[count_out:], held[len(scratch) :])
        keeps, copies = [], []
        if extra:
            keeps, copies = collect_copies(
                inputs[count_in - extra : count_in], outputs[count_out - extra : count_out], *held[:3]
            )
        if ride.copies or extra:

            @pl.when(step == 0)
            def _():
                greet([axes for axes, _ in plane_peers()] if extra else (), bool(ride.copies))
                ride.begin()
                for copy in keeps + copies:
                    copy.start()

        body(inputs[: count_in - extra], outputs[: count_out - extra])
        if ride.copies or extra:

            @pl.when(step == blocks - 1)
            def _():
                for copy in keeps:
                    copy.wait()
                for copy in copies:
                    copy.wait()
                ride.finish()

    params = {"collective_id": IDS.index(name), "has_side_effects": True} if ride.steps or extra else {}
    got = pl.pallas_call(
        kernel,
        grid=(blocks,),
        in_specs=list(specs) + [anywhere] * len(ride.operands),
        out_specs=list(out_specs) + [anywhere] * len(ride.shapes),
        out_shape=list(shapes) + ride.shapes,
        scratch_shapes=scratch + ride.scratch,
        input_output_aliases={count_in + k: count_out + v for k, v in ride.aliases.items()},
        compiler_params=pltpu.CompilerParams(vmem_limit_bytes=40 << 20, **params),
        cost_estimate=pl.CostEstimate(flops=flops, bytes_accessed=40 << 20, transcendentals=0),
        name=name,
    )(*operands, *ride.operands)
    return list(got)


def row_spec(rows, columns):
    return pl.BlockSpec((rows, columns), lambda i: (i, 0))


def attend(seen, weight, cos_rows, sin_rows, places, block, ride):
    rows, depth = seen.shape
    width = weight.shape[1] // 4
    got = by_blocks(
        attend_body,
        [seen, weight, cos_rows, sin_rows, places],
        [
            row_spec(block, depth),
            pl.BlockSpec((depth, 3 * width), lambda i: (0, 0)),
            row_spec(block, HEAD_DIM),
            row_spec(block, HEAD_DIM),
            row_spec(block, 1),
        ],
        [
            jax.ShapeDtypeStruct((rows, 3 * width), BF16),
            jax.ShapeDtypeStruct((rows, width), BF16),
        ],
        [row_spec(block, 3 * width), row_spec(block, width)],
        rows // block,
        "attend",
        ride,
        4 * rows * block * width + 6 * rows * depth * width,
    )
    return got[:2], got[2:]


def attend_back(low, seen, weight, cos_rows, sin_rows, places, block, ride, collect):
    rows, depth = seen.shape
    width = weight.shape[1] // 4
    got = by_blocks(
        attend_back_body,
        [low, seen, weight, cos_rows, sin_rows, places],
        [
            row_spec(block, 3 * width),
            row_spec(block, depth),
            pl.BlockSpec((depth, width), lambda i: (0, 3)),
            row_spec(block, HEAD_DIM),
            row_spec(block, HEAD_DIM),
            row_spec(block, 1),
        ],
        [jax.ShapeDtypeStruct((rows, 3 * width), BF16)],
        [row_spec(block, 3 * width)],
        rows // block,
        "attend_back",
        ride,
        10 * rows * block * width + 2 * rows * depth * width,
        collect,
    )
    last = 1 + len(collect)
    return got[:last], got[last:]


def plane_places(segments):
    groups, size = segments.shape
    numbers = jnp.arange(SEGS, dtype=jnp.int32)
    starts = jnp.sum((segments[:, :, None] < numbers).astype(jnp.int32), axis=1)
    onehot = segments[:, :, None] == numbers
    offset = jnp.sum(jnp.where(onehot, starts[:, None, :], 0), axis=2)
    places = jnp.arange(size, dtype=jnp.int32)[None, :] - offset
    return places.reshape(-1, 1)


def after(values, *gates):
    return lax.optimization_barrier((values,) + gates)[0]


EVERY = ("z", "y", "x", "c")


def exchange(rows):
    return lax.all_to_all(rows, EVERY, split_axis=0, concat_axis=0, tiled=True)


def on_device(
    tokens_in,
    cotangent,
    segment_ids,
    destination,
    source,
    w_query,
    w_key,
    w_value,
    w_out,
    w_gate,
    w_up,
    w_down,
):
    tok_rows = tokens_in.shape[0]
    devices = lax.axis_size(EVERY)
    per_peer = tok_rows // devices
    row_index = jnp.arange(tok_rows, dtype=jnp.int32)
    peer_to = destination // tok_rows
    ahead_rows = (peer_to[None, :] == peer_to[:, None]) & (
        destination[None, :] < destination[:, None]
    )
    send_slot = peer_to * per_peer + jnp.sum(ahead_rows.astype(jnp.int32), axis=1)
    peer_from = source // tok_rows
    before = (peer_from[None, :] == peer_from[:, None]) & (row_index[None, :] < row_index[:, None])
    recv_slot = peer_from * per_peer + jnp.sum(before.astype(jnp.int32), axis=1)
    send_pick = (send_slot[:, None] == row_index[None, :]).astype(BF16)
    recv_pick = (recv_slot[:, None] == row_index[None, :]).astype(BF16)

    packed = outer_sum(send_pick, tokens_in).astype(BF16)
    weights = [w_query, w_key, w_value, w_out.T, w_gate, w_up, w_down.T]
    attention_whole, gate_whole, up_whole, down_whole, segments, landed = dispatch(
        [weight.astype(BF16) for weight in weights],
        4,
        segment_ids.reshape(-1, 128),
        packed.reshape(devices, per_peer, -1),
        1,
        "dispatch",
    )
    arrived = project(recv_pick, landed.reshape(tok_rows, -1))
    attention_w, gate_w = Gathered(attention_whole, 1), Gathered(gate_whole)
    up_w, down_w = Gathered(up_whole), Gathered(down_whole)
    head_width = w_query.shape[1] // 4
    places = plane_places(segments.reshape(4, -1))
    half_dim = HEAD_DIM // 2
    frequency = jnp.exp(
        -jnp.arange(half_dim, dtype=F32) * (2.0 * math.log(10000.0) / HEAD_DIM)
    )
    angles = places.astype(F32) * frequency[None, :]
    cos_half, sin_half = jnp.cos(angles), jnp.sin(angles)
    cos_rows = jnp.concatenate([cos_half, cos_half], axis=1)
    sin_rows = jnp.concatenate([-sin_half, sin_half], axis=1)

    normed_one, scale_one = norm_parts(arrived)
    def give_back(rows):
        packed = outer_sum(recv_pick, rows.astype(BF16)).astype(BF16)
        return project(send_pick, exchange(packed))

    def riding(call, gathers=(), sums=()):
        ride = Ride(
            [weight.ride(count) for weight, count in gathers],
            [gradient.ride(count) for gradient, count in sums],
        )
        result, landed = call(ride)
        for (item, _), value in zip(tuple(gathers) + tuple(sums), landed):
            item.land(value)
        return result

    seen_one = riding(
        lambda ride: plane_gather(normed_one.astype(BF16), "gather_one", ride),
        [(attention_w, 2)],
    )
    attention = attention_w.finish()
    upstream_low = project(
        recv_pick,
        exchange(outer_sum(send_pick, after(cotangent, seen_one)).astype(BF16)),
    ).astype(BF16)
    upstream = upstream_low.astype(F32)
    qkv_low, attended = riding(
        lambda ride: attend(seen_one, attention, cos_rows, sin_rows, places, tok_rows, ride),
        [(gate_w, 1)],
    )
    middle = arrived + riding(
        lambda ride: plane_product([(attended, attention, 3 * head_width)], "product_out", ride),
        [(gate_w, 2)],
    )
    normed_two, scale_two = norm_parts(middle)
    seen_two = riding(
        lambda ride: plane_gather(normed_two.astype(BF16), "gather_two", ride), [(up_w, 2)]
    )
    grad_two_all = riding(
        lambda ride: plane_gather(after(upstream_low, seen_two), "gather_up", ride),
        [(up_w, 1), (down_w, 1)],
    )
    gate_whole, up_whole = gate_w.finish(), up_w.finish()
    down_w.walk(1)
    gate_lin = project(after(seen_two, grad_two_all), gate_whole)
    up_lin = project(seen_two, up_whole)
    sigmoid = jax.nn.sigmoid(gate_lin)
    hidden = (gate_lin * sigmoid * up_lin).astype(BF16)
    weight_down = outer_sum(after(grad_two_all, down_w.whole, hidden), hidden).astype(BF16)
    down_whole = down_w.finish()
    weight_down = after(weight_down, down_whole)
    summed_down = Summed(weight_down)
    grad_hidden = project(after(grad_two_all, weight_down), down_whole)
    summed_down.walk(2)
    grad_gate = (grad_hidden * up_lin * (sigmoid * (1.0 + gate_lin * (1.0 - sigmoid)))).astype(BF16)
    grad_up = (grad_hidden * (gate_lin * sigmoid)).astype(BF16)
    weight_gate = outer_sum(seen_two, grad_gate).astype(BF16)
    summed_gate = Summed(weight_gate)
    summed_up = Summed(outer_sum(seen_two, grad_up).astype(BF16))
    grad_normed_two = riding(
        lambda ride: plane_product(
            [(after(grad_gate, weight_gate), gate_whole, 0), (grad_up, up_whole, 0)],
            "product_forward",
            ride,
        ),
        (),
        [(summed_down, 1), (summed_gate, 1)],
    )
    output = middle + riding(
        lambda ride: plane_product(
            [(after(hidden, grad_normed_two), down_whole, 0)], "product_down", ride
        ),
        (),
        [(summed_gate, 2)],
    )
    layer_out = give_back(output)
    grad_middle = upstream + norm_back(normed_two, scale_two, grad_normed_two)
    grad_one_all = riding(
        lambda ride: plane_gather(
            after(grad_middle.astype(BF16), output), "gather_middle", ride
        ),
        (),
        [(summed_up, 2)],
    )
    grad_qkv, own_down, own_gate = riding(
        lambda ride: attend_back(
            qkv_low,
            grad_one_all,
            attention,
            cos_rows,
            sin_rows,
            places,
            tok_rows,
            ride,
            (summed_down.finish(), summed_gate.finish()),
        ),
        (),
        [(summed_up, 1)],
    )
    own_up = from_plane(summed_up.finish())
    summed_attention = Summed(
        jnp.concatenate(
            [
                outer_sum(seen_one, grad_qkv).astype(BF16),
                outer_sum(grad_one_all, attended).astype(BF16),
            ],
            axis=1,
        )
    )
    grad_normed_one = riding(
        lambda ride: plane_product(
            [
                (
                    after(grad_qkv, summed_attention.whole, layer_out, *own_up),
                    attention,
                    0,
                )
            ], "product_qkv", ride
        ),
        (),
        [(summed_attention, 2)],
    )
    grad_inputs = grad_middle + norm_back(normed_one, scale_one, grad_normed_one)
    own_attention = from_plane(summed_attention.finish())

    return (
        layer_out,
        give_back(grad_inputs),
        side_by_side(own_attention, 0, head_width),
        side_by_side(own_attention, head_width, 2 * head_width),
        side_by_side(own_attention, 2 * head_width, 3 * head_width),
        side_by_side(own_attention, 3 * head_width).T,
        side_by_side(own_gate),
        side_by_side(own_up),
        side_by_side(own_down).T,
    )


def solution(mesh):
    groups, cores = mesh.shape["dp"], mesh.shape["tensor"]
    whole = Mesh(mesh.devices.reshape(groups // 4, 2, 2, cores), EVERY)
    rows = P(EVERY, None)
    tall = P(("z", "y", "x"), "c")
    wide = P("c", ("z", "y", "x"))
    in_specs = (
        rows,
        rows,
        P(("z", "y", "x")),
        P(EVERY),
        P(EVERY),
        tall,
        tall,
        tall,
        wide,
        tall,
        tall,
        wide,
    )
    out_specs = (rows, rows, tall, tall, tall, wide, tall, tall, wide)
    return jax.shard_map(
        on_device, mesh=whole, in_specs=in_specs, out_specs=out_specs, check_vma=False
    )
```

```python
import functools
import math

import jax
import jax.numpy as jnp
from jax import lax
from jax.experimental import pallas as pl
from jax.experimental.pallas import tpu as pltpu
from jax.sharding import Mesh
from jax.sharding import PartitionSpec as P

HEAD_DIM = 128
SEGS = 4
EPSILON = 1e-05
NEG_LARGE = -1e30
VMEM_BYTES = 60 << 20
F32 = jnp.float32
BF16 = jnp.bfloat16
MESH = pl.DeviceIdType.MESH
IDS = (
    "dispatch",
    "gather_one",
    "gather_two",
    "gather_middle",
    "product_out",
    "product_forward",
    "product_qkv",
    "product_down",
    "gather_up",
    "attend",
    "attend_back",
)


def project(left, right):
    return jnp.dot(left, right, preferred_element_type=F32)


def project_t(left, right):
    return lax.dot_general(left, right, (((1,), (1,)), ((), ())), preferred_element_type=F32)


def outer_sum(left, right):
    return lax.dot_general(left, right, (((0,), (0,)), ((), ())), preferred_element_type=F32)


def norm_parts(values):
    center = values - jnp.mean(values, axis=-1, keepdims=True)
    spread = jnp.mean(center * center, axis=-1, keepdims=True)
    scale = lax.rsqrt(spread + EPSILON)
    return center * scale, scale


def norm_back(normed, scale, gradient):
    mean_grad = jnp.mean(gradient, axis=-1, keepdims=True)
    mean_both = jnp.mean(gradient * normed, axis=-1, keepdims=True)
    return (gradient - mean_grad - normed * mean_both) * scale


def flip(*axes):
    return {axis: 1 - lax.axis_index(axis) for axis in axes}


def owner_at(step):
    total = lax.axis_size("z")
    return lax.rem(lax.axis_index("z") + total - step, total)


def greet(peers, ring):
    barrier = pltpu.get_barrier_semaphore()
    for axes in peers:
        pl.semaphore_signal(barrier, inc=1, device_id=flip(*axes), device_id_type=MESH)
    count = len(peers)
    if ring:
        pl.semaphore_signal(barrier, inc=1, device_id={"z": owner_at(1)}, device_id_type=MESH)
        count += 1
    pl.semaphore_wait(barrier, count)


def push(axes, source, target, send, recv):
    copy = pltpu.make_async_remote_copy(
        src_ref=source,
        dst_ref=target,
        send_sem=send,
        recv_sem=recv,
        device_id=flip(*axes),
        device_id_type=MESH,
    )
    copy.start()
    return copy


class Ride:
    def __init__(self, gathers=(), sums=()):
        self.gathers, self.sums = tuple(gathers), tuple(sums)
        self.operands, self.shapes, self.scratch = [], [], []
        self.aliases = {}
        self.steps = 0
        for whole, first, count in self.gathers:
            self.aliases[len(self.operands)] = len(self.shapes)
            self.operands.append(whole)
            self.shapes.append(jax.ShapeDtypeStruct(whole.shape, whole.dtype))
            self.steps += count
        for running, whole, first, count in self.sums:
            self.operands += [whole] if running is None else [running, whole]
            block = (whole.shape[0] // lax.axis_size("z"), whole.shape[1])
            self.shapes.append(jax.ShapeDtypeStruct(block, whole.dtype))
            self.steps += count
            self.scratch += [
                pltpu.VMEM((count, *block), whole.dtype),
                pltpu.VMEM((count, *block), whole.dtype),
                pltpu.SemaphoreType.DMA((count + 1,)),
            ]
        if self.steps:
            self.scratch += [
                pltpu.SemaphoreType.DMA((self.steps,)),
                pltpu.SemaphoreType.DMA((self.steps,)),
            ]

    def board(self, inputs, outputs, scratch):
        inputs, outputs, scratch = list(inputs), list(outputs), list(scratch)
        self.loads, self.copies, self.prepares, self.begun = [], [], [], 0
        self.ends = []
        if not self.steps:
            return
        total = lax.axis_size("z")
        send, recv = scratch[-2], scratch[-1]
        ahead = {"z": owner_at(total - 1)}

        def rows_of(whole, step):
            rows = whole.shape[0] // total
            return whole.at[pl.ds(pl.multiple_of(owner_at(step % total) * rows, rows), rows)]

        def plan(source, target, prepare=None):
            slot = len(self.copies)
            self.copies.append(
                pltpu.make_async_remote_copy(
                    src_ref=source,
                    dst_ref=target,
                    send_sem=send.at[slot],
                    recv_sem=recv.at[slot],
                    device_id=ahead,
                    device_id_type=MESH,
                )
            )
            self.prepares.append(prepare)

        def adding(load, landed, own):
            def prepare():
                load.wait()
                height = 64

                @pl.loop(0, own.shape[0] // height)
                def _(index):
                    at = pl.ds(pl.multiple_of(index * height, height), height)
                    own[at, :] = (own[at, :].astype(F32) + landed[at, :].astype(F32)).astype(BF16)

            return prepare

        for _, first, count in self.gathers:
            inputs.pop(0)
            whole = outputs.pop(0)
            for step in range(first, first + count):
                plan(rows_of(whole, step), rows_of(whole, step))
        for running, _, first, count in self.sums:
            source = None if running is None else inputs.pop(0)
            whole, final = inputs.pop(0), outputs.pop(0)
            landed, own, loaded = scratch[:3]
            scratch = scratch[3:]
            if source is None:
                source = rows_of(whole, 1)
            prepare = None
            for k in range(count):
                load = pltpu.make_async_copy(rows_of(whole, first + 2 + k), own.at[k], loaded.at[k])
                self.loads.append(load)
                plan(source, landed.at[k], prepare)
                prepare, source = adding(load, landed.at[k], own.at[k]), own.at[k]
            last = len(self.copies) - 1
            keep = pltpu.make_async_copy(own.at[count - 1], final, loaded.at[count])
            self.ends.append((last, prepare, keep))

    def start(self, number):
        if self.prepares[number]:
            self.prepares[number]()
        self.copies[number].start()
        self.begun = number + 1

    def begin(self):
        for load in self.loads:
            load.start()
        if self.copies:
            self.start(0)

    def advance(self):
        if 0 < self.begun < len(self.copies):
            self.copies[self.begun - 1].wait_recv()
            self.start(self.begun)

    def finish(self):
        while self.begun < len(self.copies):
            self.advance()
        if self.copies:
            self.copies[-1].wait_recv()
        for _, prepare, keep in self.ends:
            prepare()
            keep.start()
        for copy in self.copies:
            copy.wait_send()
        for _, _, keep in self.ends:
            keep.wait()


def block_at(core, y, x):
    def moved(axis, offset):
        here = lax.axis_index(axis)
        return 1 - here if offset else here

    return (moved("y", y) * 2 + moved("x", x)) * 2 + moved("c", core)


def communicate(body, operands, specs, shapes, out_specs, scratch, name, ride, flops=0):
    ride = ride or Ride()
    count_in, count_out, count_scratch = len(operands), len(shapes), len(scratch)
    all_in = count_in + len(ride.operands)
    all_out = count_out + len(ride.shapes)

    def kernel(*refs):
        inputs, outputs, held = refs[:all_in], refs[all_in : all_in + all_out], refs[all_in + all_out :]
        ride.board(inputs[count_in:], outputs[count_out:], held[count_scratch:])
        body(inputs[:count_in], outputs[:count_out], held[:count_scratch], ride)

    anywhere = pl.BlockSpec(memory_space=pltpu.HBM)
    got = pl.pallas_call(
        kernel,
        in_specs=list(specs) + [anywhere] * len(ride.operands),
        out_specs=list(out_specs) + [anywhere] * len(ride.shapes),
        out_shape=list(shapes) + ride.shapes,
        scratch_shapes=list(scratch) + ride.scratch,
        input_output_aliases={count_in + k: count_out + v for k, v in ride.aliases.items()},
        compiler_params=pltpu.CompilerParams(
            collective_id=IDS.index(name), has_side_effects=True, vmem_limit_bytes=VMEM_BYTES
        ),
        cost_estimate=pl.CostEstimate(
            flops=flops, bytes_accessed=120 << 20, transcendentals=0
        ),
        name=name,
    )(*operands, *ride.operands)
    return list(got)


class OwnRide(Ride):
    def __init__(self, count):
        super().__init__()
        self.steps = count

    def take(self, whole, semaphores):
        self.gathers = ((None, 0, self.steps),)
        super().board([None], [whole], semaphores)


def dispatch_kernel(count, narrow, steps, *refs):
    inputs, refs = refs[:count], refs[count:]
    places, packed, refs = refs[0], refs[1], refs[2:]
    wholes, refs = refs[: count - narrow + 1], refs[count - narrow + 1 :]
    all_places, landed, send, recv, local, rows_send, rows_recv = refs[:7]
    ride = OwnRide(steps)
    ride.take(wholes[0], refs[7:])
    me_y, me_x = lax.axis_index("y"), lax.axis_index("x")
    me_z, me_c = lax.axis_index("z"), lax.axis_index("c")
    rank = me_y * 2 + me_x
    rows = inputs[0].shape[0]
    at = pl.ds(pl.multiple_of(me_z * (4 * rows) + rank * rows, rows), rows)
    peers = ((("x",), me_y * 2 + 1 - me_x), (("y",), (1 - me_y) * 2 + me_x))
    peers += ((("y", "x"), (1 - me_y) * 2 + 1 - me_x),)

    def piece(index, owner):
        width = inputs[index].shape[1] // 4
        return inputs[index].at[:, pl.ds(pl.multiple_of(owner * width, width), width)]

    def target(index):
        width = inputs[index].shape[1] // 4
        if index < narrow:
            return wholes[0].at[at, pl.ds(index * width, width)]
        return wholes[index - narrow + 1].at[at]

    devices = packed.shape[0]
    me = (me_z * 4 + rank) * 2 + me_c
    keeps = [
        pltpu.make_async_copy(piece(index, rank), target(index), local.at[index])
        for index in range(count)
    ]
    keeps.append(pltpu.make_async_copy(places, all_places.at[rank], local.at[count]))
    keeps.append(pltpu.make_async_copy(packed.at[me], landed.at[me], local.at[count + 1]))
    for keep in keeps:
        keep.start()

    def device(shift):
        other = lax.rem(me + shift, devices)
        chip = other // 2
        return {"z": chip // 4, "y": lax.rem(chip // 2, 2), "x": lax.rem(chip, 2), "c": lax.rem(other, 2)}

    barrier = pltpu.get_barrier_semaphore()

    @pl.loop(1, devices)
    def _(shift):
        pl.semaphore_signal(barrier, inc=1, device_id=device(shift), device_id_type=MESH)

    pl.semaphore_wait(barrier, devices - 1)
    copies = {}

    def share(index, source_of, goal):
        for number, (axes, owner) in enumerate(peers):
            slot = 3 * index + number
            copies[index, number] = push(axes, source_of(owner), goal, send.at[slot], recv.at[slot])

    def arrive(index):
        keeps[index].wait()
        for number in range(3):
            copies[index, number].wait_recv()

    for index in range(narrow):
        share(index, functools.partial(piece, index), target(index))
    share(count, lambda owner: places, all_places.at[rank])

    @pl.loop(1, devices)
    def _(shift):
        other = lax.rem(me + shift, devices)
        pltpu.make_async_remote_copy(
            src_ref=packed.at[other],
            dst_ref=landed.at[me],
            send_sem=rows_send,
            recv_sem=rows_recv,
            device_id=device(shift),
            device_id_type=MESH,
        ).start()

    for index in range(narrow):
        arrive(index)
    ride.begin()
    for index in range(narrow, count):
        share(index, functools.partial(piece, index), target(index))
    most = pl.ds(0, devices - 1)
    pltpu.make_async_copy(packed.at[most], landed.at[most], rows_recv).wait()
    ride.advance()
    for index in range(narrow, count + 1):
        arrive(index)
    keeps[count + 1].wait()
    ride.finish()
    for copy in copies.values():
        copy.wait_send()
    pltpu.make_async_copy(packed.at[most], packed.at[most], rows_send).wait()


def dispatch(weights, narrow, places, packed, steps, name):
    rows = weights[0].shape[0]
    total = lax.axis_size("z")
    anywhere = pl.BlockSpec(memory_space=pltpu.HBM)
    count = len(weights)
    widths = [sum(weight.shape[1] // 4 for weight in weights[:narrow])]
    widths += [weight.shape[1] // 4 for weight in weights[narrow:]]
    shapes = [jax.ShapeDtypeStruct((total * 4 * rows, width), BF16) for width in widths]
    shapes.append(jax.ShapeDtypeStruct((4, *places.shape), places.dtype))
    shapes.append(jax.ShapeDtypeStruct(packed.shape, packed.dtype))
    return pl.pallas_call(
        functools.partial(dispatch_kernel, count, narrow, steps),
        in_specs=[anywhere] * (count + 2),
        out_specs=[anywhere] * len(shapes),
        out_shape=shapes,
        scratch_shapes=[
            pltpu.SemaphoreType.DMA((3 * count + 3,)),
            pltpu.SemaphoreType.DMA((3 * count + 3,)),
            pltpu.SemaphoreType.DMA((count + 2,)),
            pltpu.SemaphoreType.DMA(()),
            pltpu.SemaphoreType.DMA(()),
            pltpu.SemaphoreType.DMA((steps,)),
            pltpu.SemaphoreType.DMA((steps,)),
        ],
        compiler_params=pltpu.CompilerParams(
            collective_id=IDS.index(name), has_side_effects=True, vmem_limit_bytes=VMEM_BYTES
        ),
        cost_estimate=pl.CostEstimate(flops=0, bytes_accessed=120 << 20, transcendentals=0),
        name=name,
    )(*weights, places, packed)


def gather_stages(own, out, send, recv, local, ride):
    rows = own.shape[0]
    half = rows // 2

    def part(core, y, x, side):
        start = block_at(core, y, x) * rows + side * half
        return out.at[pl.ds(pl.multiple_of(start, half), half)]

    def over(axis, source, target, slot):
        return push((axis,), source, target, send.at[slot], recv.at[slot])

    def across(y, x, side, slot):
        here = part(0, y, x, side)
        return over("c", here, here, slot)

    whole = out.at[pl.ds(pl.multiple_of(block_at(0, 0, 0) * rows, rows), rows)]
    keep = pltpu.make_async_copy(own, whole, local)
    keep.start()
    greet((("x",), ("y",), ("c",)), ride.steps > 0)
    first, second = own.at[pl.ds(0, half)], own.at[pl.ds(half, half)]
    x_first = over("x", first, part(0, 0, 0, 0), 0)
    y_second = over("y", second, part(0, 0, 0, 1), 1)
    x_second = over("x", second, part(0, 0, 0, 1), 2)
    y_first = over("y", first, part(0, 0, 0, 0), 3)
    ride.begin()
    crossed = [over("c", own, whole, 4)]
    yield
    x_first.wait_recv()
    far_first = over("y", part(0, 0, 1, 0), part(0, 0, 1, 0), 5)
    crossed.append(across(0, 1, 0, 6))
    y_second.wait_recv()
    far_second = over("x", part(0, 1, 0, 1), part(0, 1, 0, 1), 7)
    crossed.append(across(1, 0, 1, 8))
    yield
    x_second.wait_recv()
    crossed.append(across(0, 1, 1, 9))
    y_first.wait_recv()
    crossed.append(across(1, 0, 0, 10))
    ride.advance()
    yield
    far_first.wait_recv()
    crossed.append(across(1, 1, 0, 11))
    far_second.wait_recv()
    crossed.append(across(1, 1, 1, 12))
    for copy in crossed:
        copy.wait_recv()
    keep.wait()
    ride.advance()
    yield
    ride.finish()
    for copy in crossed + [x_first, y_second, x_second, y_first, far_first, far_second]:
        copy.wait_send()
    yield


def gather_body(inputs, outputs, scratch, ride):
    for _ in gather_stages(inputs[0], outputs[0], *scratch, ride):
        pass


def outer_tiles(sources, targets, tiles, stage, loads, stores, between=lambda: None):
    count = tiles[0].shape[0]
    tile = tiles[0].shape[2]
    total = sources[0][0].shape[1] // tile

    def fetch(index, slot):
        at = pl.ds(pl.multiple_of(index * tile, tile), tile)
        return [
            pltpu.make_async_copy(source.at[:, at], held.at[slot], loads.at[number, slot])
            for number, ((source, _), held) in enumerate(zip(sources, tiles))
        ]

    def keep(index, slot):
        at = pl.ds(pl.multiple_of(index * tile, tile), tile)
        return [
            pltpu.make_async_copy(
                stage.at[slot, :, pl.ds(start, size)], target.at[at], stores.at[number, slot]
            )
            for number, (target, start, size) in enumerate(targets)
        ]

    for copy in fetch(0, 0):
        copy.start()

    def multiply(index):
        slot = lax.rem(index, count)

        @pl.when(index + 1 < total)
        def _():
            for copy in fetch(index + 1, lax.rem(index + 1, count)):
                copy.start()

        @pl.when(index >= count)
        def _():
            for copy in keep(index - count, slot):
                copy.wait()

        for copy in fetch(index, slot):
            copy.wait()
        for (_, parts), held in zip(sources, tiles):
            left = held[slot]
            for start, size, right in parts:
                stage[slot, :, pl.ds(start, size)] = outer_sum(left, right()).astype(BF16)
        for copy in keep(index, slot):
            copy.start()

    pl.loop(0, total // 2)(multiply)
    between()
    pl.loop(total // 2, total)(multiply)
    for index in range(max(total - count, 0), total):
        for copy in keep(index, index % count):
            copy.wait()


def outer_scratch(rows, sources, columns, targets, tile=256):
    return [pltpu.VMEM((2, rows, tile), BF16)] * sources + [
        pltpu.VMEM((2, tile, columns), BF16),
        pltpu.SemaphoreType.DMA((sources, 2)),
        pltpu.SemaphoreType.DMA((targets, 2)),
    ]


def gather_hidden_body(inputs, outputs, scratch, ride):
    own, seen_ref, gate_ref, up_ref = inputs
    out, hidden_ref, by_gate_ref, by_up_ref, weight_ref = outputs
    seen, gate_w, up_w, hidden, by_gate, by_up, loads, stores, *outer = scratch[3:]
    blocks, block = seen.shape[0], seen.shape[1]
    width = gate_w.shape[1]
    tile = 512
    fetch = [
        pltpu.make_async_copy(gate_ref, gate_w, loads.at[0]),
        pltpu.make_async_copy(up_ref, up_w, loads.at[1]),
    ]
    for index in range(blocks):
        at = pl.ds(index * block, block)
        fetch.append(pltpu.make_async_copy(seen_ref.at[at], seen.at[index], loads.at[2 + index]))
    for index in (0, 2, 1, *range(3, len(fetch))):
        fetch[index].start()
    stages = gather_stages(own, out, *scratch[:3], ride)
    next(stages)
    fetch[0].wait()
    fetch[1].wait()
    kept = []
    for index in range(blocks):
        fetch[2 + index].wait()

        @pl.loop(0, width // tile)
        def _(step):
            at = pl.ds(pl.multiple_of(step * tile, tile), tile)
            here = seen[index]
            gate = project(here, gate_w[:, at])
            up = project(here, up_w[:, at])
            turned = 1.0 / (1.0 + jnp.exp(-gate))
            silu = gate * turned
            hidden[pl.ds(index * block, block), at] = (silu * up).astype(BF16)
            by_up[pl.ds(index * block, block), at] = silu.astype(BF16)
            by_gate[pl.ds(index * block, block), at] = (up * (turned * (1.0 + gate * (1.0 - turned)))).astype(BF16)

        rows_at = pl.ds(index * block, block)
        pairs = ((hidden, hidden_ref), (by_gate, by_gate_ref), (by_up, by_up_ref))
        for number, (held, target) in enumerate(pairs):
            copy = pltpu.make_async_copy(
                held.at[rows_at], target.at[rows_at], stores.at[number, index]
            )
            copy.start()
            kept.append(copy)
        if index in (3, 6):
            next(stages)
    next(stages)
    outer_tiles(
        [(out, [(0, width, lambda: hidden[...])])],
        [(weight_ref, 0, width)],
        outer[:1],
        *outer[1:],
    )
    next(stages)
    for copy in kept:
        copy.wait()


def plane_gather_hidden(rows, seen, gate_w, up_w, name, ride=None):
    total, depth = seen.shape
    width = gate_w.shape[1]
    block = rows.shape[0]
    blocks = total // block
    anywhere = pl.BlockSpec(memory_space=pltpu.HBM)
    got = communicate(
        gather_hidden_body,
        [rows, seen, gate_w, up_w],
        [anywhere] * 4,
        [jax.ShapeDtypeStruct((8 * rows.shape[0], rows.shape[1]), rows.dtype)]
        + [jax.ShapeDtypeStruct((total, width), BF16)] * 3
        + [jax.ShapeDtypeStruct((rows.shape[1], width), BF16)],
        [anywhere] * 5,
        [
            pltpu.SemaphoreType.DMA((13,)),
            pltpu.SemaphoreType.DMA((13,)),
            pltpu.SemaphoreType.DMA(()),
            pltpu.VMEM((blocks, block, depth), BF16),
            pltpu.VMEM((depth, width), BF16),
            pltpu.VMEM((depth, width), BF16),
            pltpu.VMEM((total, width), BF16),
            pltpu.VMEM((total, width), BF16),
            pltpu.VMEM((total, width), BF16),
            pltpu.SemaphoreType.DMA((2 + blocks,)),
            pltpu.SemaphoreType.DMA((3, blocks)),
        ]
        + outer_scratch(total, 1, width, 1),
        name,
        ride,
        flops=6 * total * depth * width,
    )
    return got[:5], got[5:]


def plane_gather(rows, name, ride=None):
    got = communicate(
        gather_body,
        [rows],
        [pl.BlockSpec(memory_space=pltpu.HBM)],
        [jax.ShapeDtypeStruct((8 * rows.shape[0], rows.shape[1]), rows.dtype)],
        [pl.BlockSpec(memory_space=pltpu.HBM)],
        [
            pltpu.SemaphoreType.DMA((13,)),
            pltpu.SemaphoreType.DMA((13,)),
            pltpu.SemaphoreType.DMA(()),
        ],
        name,
        ride,
    )
    return got[0], got[1:]


def product_body(make, starts, inputs, outputs, scratch, ride):
    out_ref = outputs[0]
    left, weight, away, got, near, by_y, by_x, end_y, end_x, send, recv, local = scratch[:12]
    block, width = out_ref.shape
    half = block // 2
    tile = 1024
    pairs = [(inputs[2 * i], inputs[2 * i + 1], start) for i, start in enumerate(starts)]

    def over(axis, source, target, slot):
        return push((axis,), source, target, send.at[slot], recv.at[slot])

    waits = {"weight": []}
    column = 0
    for index, (rows_ref, weight_ref, start) in enumerate(pairs):
        inner = weight_ref.shape[1] if make else rows_ref.shape[1]
        copy = pltpu.make_async_copy(
            weight_ref.at[:, pl.ds(start, inner)],
            weight.at[:, pl.ds(column, inner)],
            local.at[index, 8],
        )
        copy.start()
        waits["weight"].append(copy)
        column += inner
    order = ((1, 1, 1), (1, 1, 0), (0, 1, 1), (1, 0, 1), (0, 1, 0), (1, 0, 0), (0, 0, 1), (0, 0, 0))
    places = [pl.ds(pl.multiple_of(block_at(*key) * block, block), block) for key in order]
    if make:
        fill, follow = make(inputs, outputs, scratch[12:], left, places)
    else:
        for slot, key in enumerate(order):
            waits[key] = []
            column = 0
            for index, (rows_ref, _, _) in enumerate(pairs):
                inner = rows_ref.shape[1]
                copy = pltpu.make_async_copy(
                    rows_ref.at[places[slot]],
                    left.at[places[slot], pl.ds(column, inner)],
                    local.at[index, slot],
                )
                copy.start()
                waits[key].append(copy)
                column += inner
    greet((("x",), ("y",), ("c",)), ride.steps > 0)
    ride.begin()
    for copy in waits["weight"]:
        copy.wait()

    def multiply(key, store):
        slot = order.index(key)
        if make:
            fill(slot)
        else:
            for copy in waits[key]:
                copy.wait()
        here = left[places[slot], :]
        for start in range(0, width, tile):
            at = pl.ds(start, tile)
            store(at, project_t(here, weight[at, :]))

    crossing = {}

    def compute_far(y, x):
        index = 2 * y + x

        def store(at, value):
            away[index, :, at] = value.astype(BF16)

        multiply((1, y, x), store)
        crossing[index] = over("c", away.at[index], got.at[index], index)

    def compute_near(y, x):
        index = 2 * y + x
        crossing[index].wait_recv()

        def store(at, value):
            near[index, :, at] = (value + got[index, :, at].astype(F32)).astype(BF16)

        multiply((0, y, x), store)

    lower, upper = pl.ds(0, half), pl.ds(half, half)
    compute_far(1, 1)
    compute_far(1, 0)
    compute_near(1, 1)
    y_far = over("y", near.at[3, lower], by_y.at[1], 4)
    x_far = over("x", near.at[3, upper], by_x.at[1], 5)
    compute_far(0, 1)
    compute_near(1, 0)
    y_near = over("y", near.at[2, lower], by_y.at[0], 6)
    if make:
        ride.advance()
    compute_far(0, 0)
    compute_near(0, 1)
    x_near = over("x", near.at[1, upper], by_x.at[0], 7)
    y_far.wait_recv()
    near[1, lower, :] = (near[1, lower, :].astype(F32) + by_y[1].astype(F32)).astype(BF16)
    x_last = over("x", near.at[1, lower], end_x, 8)
    x_far.wait_recv()
    near[2, upper, :] = (near[2, upper, :].astype(F32) + by_x[1].astype(F32)).astype(BF16)
    y_last = over("y", near.at[2, upper], end_y, 9)
    if not make:
        ride.advance()
    compute_near(0, 0)
    if make:
        follow(ride.advance)
    y_near.wait_recv()
    out_ref[lower, :] = near[0, lower, :].astype(F32) + by_y[0].astype(F32)
    x_near.wait_recv()
    out_ref[upper, :] = near[0, upper, :].astype(F32) + by_x[0].astype(F32)
    x_last.wait_recv()
    out_ref[lower, :] += end_x[...].astype(F32)
    y_last.wait_recv()
    out_ref[upper, :] += end_y[...].astype(F32)
    ride.finish()
    for copy in list(crossing.values()) + [y_far, x_far, y_near, x_near, x_last, y_last]:
        copy.wait_send()


def product_scratch(total, inner, width, pairs):
    block = total // 8
    half = block // 2
    return [
        pltpu.VMEM((total, inner), BF16),
        pltpu.VMEM((width, inner), BF16),
        pltpu.VMEM((4, block, width), BF16),
        pltpu.VMEM((4, block, width), BF16),
        pltpu.VMEM((4, block, width), BF16),
        pltpu.VMEM((2, half, width), BF16),
        pltpu.VMEM((2, half, width), BF16),
        pltpu.VMEM((half, width), BF16),
        pltpu.VMEM((half, width), BF16),
        pltpu.SemaphoreType.DMA((10,)),
        pltpu.SemaphoreType.DMA((10,)),
        pltpu.SemaphoreType.DMA((pairs, 9)),
    ]


def hidden_back(inputs, outputs, scratch, left, places):
    by_gate_ref, gate_w, by_up_ref, up_w, grad_ref, down_ref, seen_ref = inputs
    weight_gate, weight_up = outputs[1:]
    down, rows, factors, down_load, row_loads, *outer = scratch
    width = down.shape[1]
    tile = 1024
    fetch_down = pltpu.make_async_copy(down_ref, down, down_load)
    fetch_down.start()

    def fetch(slot):
        at, held = places[slot], slot % 2
        return [
            pltpu.make_async_copy(grad_ref.at[at], rows.at[held], row_loads.at[0, held]),
            pltpu.make_async_copy(by_gate_ref.at[at], factors.at[held, 0], row_loads.at[1, held]),
            pltpu.make_async_copy(by_up_ref.at[at], factors.at[held, 1], row_loads.at[2, held]),
        ]

    for copy in fetch(0):
        copy.start()

    def fill(slot):
        if slot == 0:
            fetch_down.wait()
        for copy in fetch(slot):
            copy.wait()
        if slot + 1 < len(places):
            for copy in fetch(slot + 1):
                copy.start()
        held = slot % 2

        for start in range(0, width, tile):
            at, beside = pl.ds(start, tile), pl.ds(width + start, tile)
            grad = project(rows[held], down[:, at])
            left[places[slot], at] = (grad * factors[held, 0, :, at].astype(F32)).astype(BF16)
            left[places[slot], beside] = (grad * factors[held, 1, :, at].astype(F32)).astype(BF16)

    def follow(between):
        outer_tiles(
            [
                (
                    seen_ref,
                    [
                        (0, width, lambda: left[:, pl.ds(0, width)]),
                        (width, width, lambda: left[:, pl.ds(width, width)]),
                    ],
                )
            ],
            [(weight_gate, 0, width), (weight_up, width, width)],
            outer[:1],
            *outer[1:],
            between,
        )

    return fill, follow


def plane_product_back(grads, down, by_gate, by_up, gate_w, up_w, seen, name, ride):
    total, depth = grads.shape
    width = gate_w.shape[1]
    block = total // 8
    operands = [by_gate, gate_w, by_up, up_w, grads, down, seen]
    anywhere = pl.BlockSpec(memory_space=pltpu.HBM)
    got = communicate(
        functools.partial(product_body, hidden_back, [0, 0]),
        operands,
        [anywhere] * len(operands),
        [jax.ShapeDtypeStruct((block, depth), F32)]
        + [jax.ShapeDtypeStruct((depth, width), BF16)] * 2,
        [pl.BlockSpec(memory_space=pltpu.VMEM), anywhere, anywhere],
        product_scratch(total, 2 * width, depth, 2)
        + [
            pltpu.VMEM((depth, width), BF16),
            pltpu.VMEM((2, block, depth), BF16),
            pltpu.VMEM((2, 2, block, width), BF16),
            pltpu.SemaphoreType.DMA(()),
            pltpu.SemaphoreType.DMA((3, 2)),
        ]
        + outer_scratch(total, 1, 2 * width, 2),
        name,
        ride,
        flops=10 * total * depth * width,
    )
    return got[:3], got[3:]


def plane_product(pairs, name, ride=None):
    total = pairs[0][0].shape[0]
    inner = sum(rows.shape[1] for rows, _, _ in pairs)
    width = pairs[0][1].shape[0]
    operands = []
    for rows, weight, _ in pairs:
        operands += [rows, weight]
    got = communicate(
        functools.partial(product_body, None, [start for _, _, start in pairs]),
        operands,
        [pl.BlockSpec(memory_space=pltpu.HBM)] * len(operands),
        [jax.ShapeDtypeStruct((total // 8, width), F32)],
        [pl.BlockSpec(memory_space=pltpu.VMEM)],
        product_scratch(total, inner, width, len(pairs)),
        name,
        ride,
        flops=2 * total * inner * width,
    )
    return got[0], got[1:]


def ring_next(values):
    total = lax.axis_size("z")
    return lax.ppermute(values, "z", [(i, (i + 1) % total) for i in range(total)])


def ring_rows(whole, owner):
    rows = whole.shape[0] // lax.axis_size("z")
    return lax.dynamic_slice(whole, (owner * rows, 0), (rows, whole.shape[1]))


class Gathered:
    def __init__(self, whole, step=0):
        self.whole, self.step = whole, step

    def ride(self, count):
        count = min(count, lax.axis_size("z") - 1 - self.step)
        item = (self.whole, self.step, count)
        self.step += count
        return item

    def land(self, whole):
        self.whole = whole

    def walk(self, count):
        total = lax.axis_size("z")
        rows = self.whole.shape[0] // total
        last = min(self.step + count, total - 1)
        current = ring_rows(self.whole, owner_at(self.step)) if self.step < last else None
        while self.step < last:
            self.step += 1
            current = ring_next(current)
            self.whole = lax.dynamic_update_slice(self.whole, current, (owner_at(self.step) * rows, 0))

    def finish(self):
        self.walk(lax.axis_size("z"))
        return self.whole


class Summed:
    def __init__(self, whole):
        self.whole, self.step, self.running = whole, 0, None

    def ride(self, count):
        count = min(count, lax.axis_size("z") - 1 - self.step)
        item = (self.running, self.whole, self.step, count)
        self.step += count
        return item

    def land(self, running):
        self.running = running

    def walk(self, count):
        total = lax.axis_size("z")
        for _ in range(min(count, total - 1 - self.step)):
            running = ring_rows(self.whole, owner_at(1)) if self.running is None else self.running
            own = ring_rows(self.whole, owner_at((self.step + 2) % total))
            self.running = (ring_next(running).astype(F32) + own.astype(F32)).astype(BF16)
            self.step += 1

    def finish(self):
        self.walk(lax.axis_size("z"))
        return self.running


def from_plane(block):
    rows = block.shape[0] // 4
    me_y, me_x = lax.axis_index("y"), lax.axis_index("x")

    def piece(y, x):
        return lax.dynamic_slice(block, ((y * 2 + x) * rows, 0), (rows, block.shape[1]))

    own = piece(me_y, me_x)
    by_x = lax.ppermute(piece(me_y, 1 - me_x), "x", ((0, 1), (1, 0)))
    by_y = lax.ppermute(piece(1 - me_y, me_x), "y", ((0, 1), (1, 0)))
    far = lax.ppermute(piece(1 - me_y, 1 - me_x), ("y", "x"), ((0, 3), (1, 2), (2, 1), (3, 0)))

    def chosen(y, x):
        same_y, same_x = me_y == y, me_x == x
        return jnp.where(
            same_y, jnp.where(same_x, own, by_x), jnp.where(same_x, by_y, far)
        )

    return [chosen(y, x) for y in range(2) for x in range(2)]


def side_by_side(pieces, start=0, stop=None):
    return jnp.concatenate([piece[:, start:stop].astype(F32) for piece in pieces], axis=1)


def turn(values, cos_rows, sin_rows):
    return values * cos_rows + pltpu.roll(values, HEAD_DIM // 2, 1) * sin_rows


def visible_of(places):
    size = places.shape[0]
    row = lax.broadcasted_iota(jnp.int32, (size, size), 0)
    column = lax.broadcasted_iota(jnp.int32, (size, size), 1)
    return (column <= row) & (row - column <= places)


def soft_of(queries, keys, visible):
    scores = project_t(queries, keys) * (1.0 / math.sqrt(HEAD_DIM))
    scores = jnp.where(visible, scores, NEG_LARGE)
    weights = jnp.exp(scores - jnp.max(scores, axis=1, keepdims=True))
    return weights / jnp.sum(weights, axis=1, keepdims=True)


def attend_body(inputs, outputs):
    seen_ref, weight_ref, cos_ref, sin_ref, place_ref = inputs
    low_ref, out_ref = outputs
    width = out_ref.shape[1]
    cos_rows, sin_rows = cos_ref[...], sin_ref[...]
    visible = visible_of(place_ref[...])
    lin = project(seen_ref[...], weight_ref[...])
    for start in range(0, width, HEAD_DIM):
        here = slice(start, start + HEAD_DIM)
        key_at = slice(width + start, width + start + HEAD_DIM)
        value_at = slice(2 * width + start, 2 * width + start + HEAD_DIM)
        queries = turn(lin[:, here], cos_rows, sin_rows).astype(BF16)
        keys = turn(lin[:, key_at], cos_rows, sin_rows).astype(BF16)
        values = lin[:, value_at].astype(BF16)
        low_ref[:, here] = queries
        low_ref[:, key_at] = keys
        low_ref[:, value_at] = values
        soft = soft_of(queries, keys, visible).astype(BF16)
        out_ref[:, here] = project(soft, values).astype(BF16)


def attend_back_body(blocks, inputs, outputs, grads_held):
    low_ref, seen_ref, weight_ref, cos_ref, sin_ref, place_ref = inputs[:6]
    seen_tile, grad_tile, attended_ref = inputs[6:]
    out_ref, outer_ref = outputs
    step = pl.program_id(0)
    block = out_ref.shape[0]

    @pl.when(step < blocks)
    def _():
        attend_back_block(inputs[:6], out_ref)
        grads_held[pl.ds(pl.multiple_of(step * block, block), block), :] = out_ref[...]

    @pl.when(step >= blocks)
    def _():
        width = out_ref.shape[1]
        outer_ref[:, :width] = outer_sum(seen_tile[...], grads_held[...]).astype(BF16)
        outer_ref[:, width:] = outer_sum(grad_tile[...], attended_ref[...]).astype(BF16)


def attend_back_block(inputs, out_ref):
    low_ref, seen_ref, weight_ref, cos_ref, sin_ref, place_ref = inputs
    width = weight_ref.shape[1]
    cos_rows, sin_rows = cos_ref[...], -sin_ref[...]
    visible = visible_of(place_ref[...])
    scale = 1.0 / math.sqrt(HEAD_DIM)
    grad_all = project(seen_ref[...], weight_ref[...]).astype(BF16)
    for start in range(0, width, HEAD_DIM):
        here = slice(start, start + HEAD_DIM)
        key_at = slice(width + start, width + start + HEAD_DIM)
        value_at = slice(2 * width + start, 2 * width + start + HEAD_DIM)
        queries, keys, values = low_ref[:, here], low_ref[:, key_at], low_ref[:, value_at]
        grad = grad_all[:, here]
        soft = soft_of(queries, keys, visible)
        grad_soft = project_t(grad, values)
        inner = jnp.sum(soft * grad_soft, axis=1, keepdims=True)
        grad_scores = (soft * (grad_soft - inner)).astype(BF16)
        grad_query = project(grad_scores, keys) * scale
        grad_key = outer_sum(grad_scores, queries) * scale
        out_ref[:, here] = turn(grad_query, cos_rows, sin_rows).astype(BF16)
        out_ref[:, key_at] = turn(grad_key, cos_rows, sin_rows).astype(BF16)
        out_ref[:, value_at] = outer_sum(soft.astype(BF16), grad).astype(BF16)


def plane_peers():
    me_y, me_x = lax.axis_index("y"), lax.axis_index("x")
    return (
        (("x",), me_y * 2 + 1 - me_x),
        (("y",), (1 - me_y) * 2 + me_x),
        (("y", "x"), (1 - me_y) * 2 + 1 - me_x),
    )


def collect_copies(blocks, outs, send, recv, local):
    rank = lax.axis_index("y") * 2 + lax.axis_index("x")
    keeps, copies = [], []
    for index, (block, out) in enumerate(zip(blocks, outs)):
        rows = block.shape[0] // 4

        def piece(owner, block=block, rows=rows):
            return block.at[pl.ds(pl.multiple_of(owner * rows, rows), rows)]

        keeps.append(pltpu.make_async_copy(piece(rank), out.at[rank], local.at[index]))
        for number, (axes, owner) in enumerate(plane_peers()):
            copies.append(
                pltpu.make_async_remote_copy(
                    src_ref=piece(owner),
                    dst_ref=out.at[rank],
                    send_sem=send.at[3 * index + number],
                    recv_sem=recv.at[3 * index + number],
                    device_id=flip(*axes),
                    device_id_type=MESH,
                )
            )
    return keeps, copies


def collected_shape(block):
    return jax.ShapeDtypeStruct((4, block.shape[0] // 4, block.shape[1]), block.dtype)


def by_blocks(
    body, operands, specs, shapes, out_specs, blocks, name, ride, flops, collect=(), own_scratch=(), advances=()
):
    extra = len(collect)
    operands, shapes = list(operands) + list(collect), list(shapes)
    shapes += [collected_shape(block) for block in collect]
    anywhere = pl.BlockSpec(memory_space=pltpu.HBM)
    specs, out_specs = list(specs) + [anywhere] * extra, list(out_specs) + [anywhere] * extra
    scratch = list(own_scratch)
    if extra:
        scratch += [
            pltpu.SemaphoreType.DMA((3 * extra,)),
            pltpu.SemaphoreType.DMA((3 * extra,)),
            pltpu.SemaphoreType.DMA((extra,)),
        ]
    count_in, count_out = len(operands), len(shapes)
    all_in = count_in + len(ride.operands)
    all_out = count_out + len(ride.shapes)

    def kernel(*refs):
        inputs, outputs, held = refs[:all_in], refs[all_in : all_in + all_out], refs[all_in + all_out :]
        step = pl.program_id(0)
        ride.board(inputs[count_in:], outputs[count_out:], held[len(scratch) :])
        keeps, copies = [], []
        if extra:
            keeps, copies = collect_copies(
                inputs[count_in - extra : count_in], outputs[count_out - extra : count_out], *held[len(scratch) - 3 : len(scratch)]
            )
        if ride.copies or extra:

            @pl.when(step == 0)
            def _():
                greet([axes for axes, _ in plane_peers()] if extra else (), bool(ride.copies))
                ride.begin()
                for copy in keeps + copies:
                    copy.start()

        body(inputs[: count_in - extra], outputs[: count_out - extra], *held[: len(own_scratch)])
        for number in advances:
            pl.when(step == number)(ride.advance)
        if ride.copies or extra:

            @pl.when(step == blocks - 1)
            def _():
                for copy in keeps:
                    copy.wait()
                for copy in copies:
                    copy.wait()
                ride.finish()

    params = {"collective_id": IDS.index(name), "has_side_effects": True} if ride.steps or extra else {}
    got = pl.pallas_call(
        kernel,
        grid=(blocks,),
        in_specs=list(specs) + [anywhere] * len(ride.operands),
        out_specs=list(out_specs) + [anywhere] * len(ride.shapes),
        out_shape=list(shapes) + ride.shapes,
        scratch_shapes=scratch + ride.scratch,
        input_output_aliases={count_in + k: count_out + v for k, v in ride.aliases.items()},
        compiler_params=pltpu.CompilerParams(vmem_limit_bytes=VMEM_BYTES, **params),
        cost_estimate=pl.CostEstimate(flops=flops, bytes_accessed=40 << 20, transcendentals=0),
        name=name,
    )(*operands, *ride.operands)
    return list(got)


def row_spec(rows, columns):
    return pl.BlockSpec((rows, columns), lambda i: (i, 0))


def attend(seen, weight, cos_rows, sin_rows, places, block, ride):
    rows, depth = seen.shape
    width = weight.shape[1] // 4
    got = by_blocks(
        attend_body,
        [seen, weight, cos_rows, sin_rows, places],
        [
            row_spec(block, depth),
            pl.BlockSpec((depth, 3 * width), lambda i: (0, 0)),
            row_spec(block, HEAD_DIM),
            row_spec(block, HEAD_DIM),
            row_spec(block, 1),
        ],
        [
            jax.ShapeDtypeStruct((rows, 3 * width), BF16),
            jax.ShapeDtypeStruct((rows, width), BF16),
        ],
        [row_spec(block, 3 * width), row_spec(block, width)],
        rows // block,
        "attend",
        ride,
        4 * rows * block * width + 6 * rows * depth * width,
    )
    return got[:2], got[2:]


def attend_back(low, grad_all, weight, cos_rows, sin_rows, places, seen, attended, block, ride, collect):
    rows, depth = grad_all.shape
    width = weight.shape[1] // 4
    blocks = rows // block
    tile = 256

    def early(columns):
        return pl.BlockSpec((block, columns), lambda i: (jnp.minimum(i, blocks - 1), 0))

    def late(i):
        return jnp.maximum(i - blocks, 0)

    got = by_blocks(
        functools.partial(attend_back_body, blocks),
        [low, grad_all, weight, cos_rows, sin_rows, places, seen, grad_all, attended],
        [
            early(3 * width),
            early(depth),
            pl.BlockSpec((depth, width), lambda i: (0, 3)),
            early(HEAD_DIM),
            early(HEAD_DIM),
            early(1),
            pl.BlockSpec((rows, tile), lambda i: (0, late(i))),
            pl.BlockSpec((rows, tile), lambda i: (0, late(i))),
            pl.BlockSpec((rows, width), lambda i: (0, 0)),
        ],
        [
            jax.ShapeDtypeStruct((rows, 3 * width), BF16),
            jax.ShapeDtypeStruct((depth, 4 * width), BF16),
        ],
        [early(3 * width), pl.BlockSpec((tile, 4 * width), lambda i: (late(i), 0))],
        blocks + depth // tile,
        "attend_back",
        ride,
        10 * rows * block * width + 10 * rows * depth * width,
        collect,
        [pltpu.VMEM((rows, 3 * width), BF16)],
        (blocks - 2, blocks + depth // tile - 3),
    )
    last = 2 + len(collect)
    return got[:last], got[last:]


def plane_places(segments):
    groups, size = segments.shape
    numbers = jnp.arange(SEGS, dtype=jnp.int32)
    starts = jnp.sum((segments[:, :, None] < numbers).astype(jnp.int32), axis=1)
    onehot = segments[:, :, None] == numbers
    offset = jnp.sum(jnp.where(onehot, starts[:, None, :], 0), axis=2)
    places = jnp.arange(size, dtype=jnp.int32)[None, :] - offset
    return places.reshape(-1, 1)


def after(values, *gates):
    return lax.optimization_barrier((values,) + gates)[0]


EVERY = ("z", "y", "x", "c")


def exchange(rows):
    return lax.all_to_all(rows, EVERY, split_axis=0, concat_axis=0, tiled=True)


def on_device(
    tokens_in,
    cotangent,
    segment_ids,
    destination,
    source,
    w_query,
    w_key,
    w_value,
    w_out,
    w_gate,
    w_up,
    w_down,
):
    tok_rows = tokens_in.shape[0]
    devices = lax.axis_size(EVERY)
    per_peer = tok_rows // devices
    row_index = jnp.arange(tok_rows, dtype=jnp.int32)
    peer_to = destination // tok_rows
    ahead_rows = (peer_to[None, :] == peer_to[:, None]) & (
        destination[None, :] < destination[:, None]
    )
    send_slot = peer_to * per_peer + jnp.sum(ahead_rows.astype(jnp.int32), axis=1)
    peer_from = source // tok_rows
    before = (peer_from[None, :] == peer_from[:, None]) & (row_index[None, :] < row_index[:, None])
    recv_slot = peer_from * per_peer + jnp.sum(before.astype(jnp.int32), axis=1)
    send_pick = (send_slot[:, None] == row_index[None, :]).astype(BF16)
    recv_pick = (recv_slot[:, None] == row_index[None, :]).astype(BF16)

    packed = outer_sum(send_pick, tokens_in).astype(BF16)
    weights = [w_query, w_key, w_value, w_out.T, w_gate, w_up, w_down.T]
    attention_whole, gate_whole, up_whole, down_whole, segments, landed = dispatch(
        [weight.astype(BF16) for weight in weights],
        4,
        segment_ids.reshape(-1, 128),
        packed.reshape(devices, per_peer, -1),
        2,
        "dispatch",
    )
    arrived = project(recv_pick, landed.reshape(tok_rows, -1))
    attention_w, gate_w = Gathered(attention_whole, 2), Gathered(gate_whole)
    up_w, down_w = Gathered(up_whole), Gathered(down_whole)
    head_width = w_query.shape[1] // 4
    places = plane_places(segments.reshape(4, -1))
    half_dim = HEAD_DIM // 2
    frequency = jnp.exp(
        -jnp.arange(half_dim, dtype=F32) * (2.0 * math.log(10000.0) / HEAD_DIM)
    )
    angles = places.astype(F32) * frequency[None, :]
    cos_half, sin_half = jnp.cos(angles), jnp.sin(angles)
    cos_rows = jnp.concatenate([cos_half, cos_half], axis=1)
    sin_rows = jnp.concatenate([-sin_half, sin_half], axis=1)

    normed_one, scale_one = norm_parts(arrived)
    def send_back(rows):
        return exchange(outer_sum(recv_pick, rows.astype(BF16)).astype(BF16))

    def riding(call, gathers=(), sums=()):
        ride = Ride(
            [weight.ride(count) for weight, count in gathers],
            [gradient.ride(count) for gradient, count in sums],
        )
        result, landed = call(ride)
        for (item, _), value in zip(tuple(gathers) + tuple(sums), landed):
            item.land(value)
        return result

    seen_one = riding(
        lambda ride: plane_gather(normed_one.astype(BF16), "gather_one", ride),
        [(attention_w, 1), (gate_w, 1)],
    )
    attention = attention_w.finish()
    upstream_low = project(
        recv_pick,
        exchange(outer_sum(send_pick, after(cotangent, seen_one)).astype(BF16)),
    ).astype(BF16)
    upstream = upstream_low.astype(F32)
    qkv_low, attended = riding(
        lambda ride: attend(seen_one, attention, cos_rows, sin_rows, places, tok_rows, ride),
        [(gate_w, 1)],
    )
    middle = arrived + riding(
        lambda ride: plane_product([(attended, attention, 3 * head_width)], "product_out", ride),
        [(gate_w, 1), (up_w, 1)],
    )
    normed_two, scale_two = norm_parts(middle)
    seen_two = riding(
        lambda ride: plane_gather(normed_two.astype(BF16), "gather_two", ride), [(up_w, 2)]
    )
    gate_whole, up_whole = gate_w.finish(), up_w.finish()
    grad_two_all, hidden, by_gate, by_up, weight_down = riding(
        lambda ride: plane_gather_hidden(
            upstream_low, seen_two, gate_whole, up_whole, "gather_up", ride
        ),
        [(down_w, 3)],
    )
    down_whole = down_w.finish()
    summed_down = Summed(weight_down)
    grad_normed_two, weight_gate, weight_up = riding(
        lambda ride: plane_product_back(
            grad_two_all,
            down_whole,
            by_gate,
            by_up,
            gate_whole,
            up_whole,
            seen_two,
            "product_forward",
            ride,
        ),
        (),
        [(summed_down, 3)],
    )
    summed_gate, summed_up = Summed(weight_gate), Summed(weight_up)
    output = middle + riding(
        lambda ride: plane_product(
            [(after(hidden, grad_normed_two), down_whole, 0)], "product_down", ride
        ),
        (),
        [(summed_gate, 2)],
    )
    returned_out = send_back(output)
    grad_middle = upstream + norm_back(normed_two, scale_two, grad_normed_two)
    grad_one_all = riding(
        lambda ride: plane_gather(
            after(grad_middle.astype(BF16), output), "gather_middle", ride
        ),
        (),
        [(summed_gate, 1)],
    )
    grad_qkv, weight_attention, own_down, own_gate = riding(
        lambda ride: attend_back(
            after(qkv_low, returned_out),
            grad_one_all,
            attention,
            cos_rows,
            sin_rows,
            places,
            seen_one,
            attended,
            tok_rows,
            ride,
            (summed_down.finish(), summed_gate.finish()),
        ),
        (),
        [(summed_up, 3)],
    )
    summed_attention = Summed(weight_attention)
    grad_normed_one = riding(
        lambda ride: plane_product([(grad_qkv, attention, 0)], "product_qkv", ride),
        (),
        [(summed_attention, 2)],
    )
    grad_inputs = grad_middle + norm_back(normed_one, scale_one, grad_normed_one)
    own_up, last_attention = from_plane(summed_up.finish()), summed_attention.finish()
    own_attention = from_plane(last_attention)
    own_down, own_gate, own_up = [
        after(own, last_attention) for own in (own_down, own_gate, jnp.stack(own_up))
    ]

    return (
        project(send_pick, after(returned_out, grad_normed_one)),
        project(send_pick, send_back(grad_inputs)),
        side_by_side(own_attention, 0, head_width),
        side_by_side(own_attention, head_width, 2 * head_width),
        side_by_side(own_attention, 2 * head_width, 3 * head_width),
        side_by_side(own_attention, 3 * head_width).T,
        side_by_side(own_gate),
        side_by_side(own_up),
        side_by_side(own_down).T,
    )


def solution(mesh):
    groups, cores = mesh.shape["dp"], mesh.shape["tensor"]
    whole = Mesh(mesh.devices.reshape(groups // 4, 2, 2, cores), EVERY)
    rows = P(EVERY, None)
    tall = P(("z", "y", "x"), "c")
    wide = P("c", ("z", "y", "x"))
    in_specs = (
        rows,
        rows,
        P(("z", "y", "x")),
        P(EVERY),
        P(EVERY),
        tall,
        tall,
        tall,
        wide,
        tall,
        tall,
        wide,
    )
    out_specs = (rows, rows, tall, tall, tall, wide, tall, tall, wide)
    return jax.shard_map(
        on_device, mesh=whole, in_specs=in_specs, out_specs=out_specs, check_vma=False
    )
```

```python
import functools
import math

import jax
import jax.numpy as jnp
from jax import lax
from jax.experimental import pallas as pl
from jax.experimental.pallas import tpu as pltpu
from jax.sharding import Mesh
from jax.sharding import PartitionSpec as P

HEAD_DIM = 128
SEGS = 4
EPSILON = 1e-05
NEG_LARGE = -1e30
VMEM_BYTES = 60 << 20
F32 = jnp.float32
BF16 = jnp.bfloat16
MESH = pl.DeviceIdType.MESH
IDS = (
    "dispatch",
    "gather_one",
    "gather_two",
    "gather_middle",
    "product_out",
    "product_forward",
    "product_qkv",
    "product_down",
    "gather_up",
    "attend",
    "attend_back",
)


def project(left, right):
    return jnp.dot(left, right, preferred_element_type=F32)


def project_t(left, right):
    return lax.dot_general(left, right, (((1,), (1,)), ((), ())), preferred_element_type=F32)


def outer_sum(left, right):
    return lax.dot_general(left, right, (((0,), (0,)), ((), ())), preferred_element_type=F32)


def norm_parts(values):
    center = values - jnp.mean(values, axis=-1, keepdims=True)
    spread = jnp.mean(center * center, axis=-1, keepdims=True)
    scale = lax.rsqrt(spread + EPSILON)
    return center * scale, scale


def norm_back(normed, scale, gradient):
    mean_grad = jnp.mean(gradient, axis=-1, keepdims=True)
    mean_both = jnp.mean(gradient * normed, axis=-1, keepdims=True)
    return (gradient - mean_grad - normed * mean_both) * scale


def flip(*axes):
    return {axis: 1 - lax.axis_index(axis) for axis in axes}


def owner_at(step):
    total = lax.axis_size("z")
    return lax.rem(lax.axis_index("z") + total - step, total)


def greet(peers, ring):
    barrier = pltpu.get_barrier_semaphore()
    for axes in peers:
        pl.semaphore_signal(barrier, inc=1, device_id=flip(*axes), device_id_type=MESH)
    count = len(peers)
    if ring:
        pl.semaphore_signal(barrier, inc=1, device_id={"z": owner_at(1)}, device_id_type=MESH)
        count += 1
    pl.semaphore_wait(barrier, count)


def push(axes, source, target, send, recv):
    copy = pltpu.make_async_remote_copy(
        src_ref=source,
        dst_ref=target,
        send_sem=send,
        recv_sem=recv,
        device_id=flip(*axes),
        device_id_type=MESH,
    )
    copy.start()
    return copy


class Ride:
    def __init__(self, gathers=(), sums=()):
        self.gathers, self.sums = tuple(gathers), tuple(sums)
        self.operands, self.shapes, self.scratch = [], [], []
        self.aliases = {}
        self.steps = 0
        for whole, first, count in self.gathers:
            self.aliases[len(self.operands)] = len(self.shapes)
            self.operands.append(whole)
            self.shapes.append(jax.ShapeDtypeStruct(whole.shape, whole.dtype))
            self.steps += count
        for running, whole, first, count in self.sums:
            self.operands += [whole] if running is None else [running, whole]
            block = (whole.shape[0] // lax.axis_size("z"), whole.shape[1])
            self.shapes.append(jax.ShapeDtypeStruct(block, whole.dtype))
            self.steps += count
            self.scratch += [
                pltpu.VMEM((count, *block), whole.dtype),
                pltpu.VMEM((count, *block), whole.dtype),
                pltpu.SemaphoreType.DMA((count + 1,)),
            ]
        if self.steps:
            self.scratch += [
                pltpu.SemaphoreType.DMA((self.steps,)),
                pltpu.SemaphoreType.DMA((self.steps,)),
            ]

    def board(self, inputs, outputs, scratch):
        inputs, outputs, scratch = list(inputs), list(outputs), list(scratch)
        self.loads, self.copies, self.prepares, self.begun = [], [], [], 0
        self.ends = []
        if not self.steps:
            return
        total = lax.axis_size("z")
        send, recv = scratch[-2], scratch[-1]
        ahead = {"z": owner_at(total - 1)}

        def rows_of(whole, step):
            rows = whole.shape[0] // total
            return whole.at[pl.ds(pl.multiple_of(owner_at(step % total) * rows, rows), rows)]

        def plan(source, target, prepare=None):
            slot = len(self.copies)
            self.copies.append(
                pltpu.make_async_remote_copy(
                    src_ref=source,
                    dst_ref=target,
                    send_sem=send.at[slot],
                    recv_sem=recv.at[slot],
                    device_id=ahead,
                    device_id_type=MESH,
                )
            )
            self.prepares.append(prepare)

        def adding(load, landed, own):
            def prepare():
                load.wait()
                height = 64

                @pl.loop(0, own.shape[0] // height)
                def _(index):
                    at = pl.ds(pl.multiple_of(index * height, height), height)
                    own[at, :] = (own[at, :].astype(F32) + landed[at, :].astype(F32)).astype(BF16)

            return prepare

        for _, first, count in self.gathers:
            inputs.pop(0)
            whole = outputs.pop(0)
            for step in range(first, first + count):
                plan(rows_of(whole, step), rows_of(whole, step))
        for running, _, first, count in self.sums:
            source = None if running is None else inputs.pop(0)
            whole, final = inputs.pop(0), outputs.pop(0)
            landed, own, loaded = scratch[:3]
            scratch = scratch[3:]
            if source is None:
                source = rows_of(whole, 1)
            prepare = None
            for k in range(count):
                load = pltpu.make_async_copy(rows_of(whole, first + 2 + k), own.at[k], loaded.at[k])
                self.loads.append(load)
                plan(source, landed.at[k], prepare)
                prepare, source = adding(load, landed.at[k], own.at[k]), own.at[k]
            last = len(self.copies) - 1
            keep = pltpu.make_async_copy(own.at[count - 1], final, loaded.at[count])
            self.ends.append((last, prepare, keep))

    def start(self, number):
        if self.prepares[number]:
            self.prepares[number]()
        self.copies[number].start()
        self.begun = number + 1

    def begin(self):
        for load in self.loads:
            load.start()
        if self.copies:
            self.start(0)

    def advance(self):
        if 0 < self.begun < len(self.copies):
            self.copies[self.begun - 1].wait_recv()
            self.start(self.begun)

    def finish(self):
        while self.begun < len(self.copies):
            self.advance()
        if self.copies:
            self.copies[-1].wait_recv()
        for _, prepare, keep in self.ends:
            prepare()
            keep.start()
        for copy in self.copies:
            copy.wait_send()
        for _, _, keep in self.ends:
            keep.wait()


def block_at(core, y, x):
    def moved(axis, offset):
        here = lax.axis_index(axis)
        return 1 - here if offset else here

    return (moved("y", y) * 2 + moved("x", x)) * 2 + moved("c", core)


def communicate(body, operands, specs, shapes, out_specs, scratch, name, ride, flops=0):
    ride = ride or Ride()
    count_in, count_out, count_scratch = len(operands), len(shapes), len(scratch)
    all_in = count_in + len(ride.operands)
    all_out = count_out + len(ride.shapes)

    def kernel(*refs):
        inputs, outputs, held = refs[:all_in], refs[all_in : all_in + all_out], refs[all_in + all_out :]
        ride.board(inputs[count_in:], outputs[count_out:], held[count_scratch:])
        body(inputs[:count_in], outputs[:count_out], held[:count_scratch], ride)

    anywhere = pl.BlockSpec(memory_space=pltpu.HBM)
    got = pl.pallas_call(
        kernel,
        in_specs=list(specs) + [anywhere] * len(ride.operands),
        out_specs=list(out_specs) + [anywhere] * len(ride.shapes),
        out_shape=list(shapes) + ride.shapes,
        scratch_shapes=list(scratch) + ride.scratch,
        input_output_aliases={count_in + k: count_out + v for k, v in ride.aliases.items()},
        compiler_params=pltpu.CompilerParams(
            collective_id=IDS.index(name), has_side_effects=True, vmem_limit_bytes=VMEM_BYTES
        ),
        cost_estimate=pl.CostEstimate(
            flops=flops, bytes_accessed=120 << 20, transcendentals=0
        ),
        name=name,
    )(*operands, *ride.operands)
    return list(got)


class OwnRide(Ride):
    def __init__(self, count):
        super().__init__()
        self.steps = count

    def take(self, whole, semaphores):
        self.gathers = ((None, 0, self.steps),)
        super().board([None], [whole], semaphores)


def dispatch_kernel(turned, narrow, steps, *refs):
    count = len(turned)
    inputs, refs = refs[:count], refs[count:]
    places, packed, refs = refs[0], refs[1], refs[2:]
    wholes, refs = refs[: count - narrow + 1], refs[count - narrow + 1 :]
    all_places, landed, send, recv, local, rows_send, rows_recv, step_send, step_recv = refs[:9]
    loaded, refs = refs[9], refs[10:]
    wide, low = refs[:count], refs[count:]
    ride = OwnRide(steps)
    ride.take(wholes[0], (step_send, step_recv))
    loads = [
        pltpu.make_async_copy(source, held, loaded.at[index])
        for index, (source, held) in enumerate(zip(inputs, wide))
    ]
    for load in loads:
        load.start()
    me_y, me_x = lax.axis_index("y"), lax.axis_index("x")
    me_z, me_c = lax.axis_index("z"), lax.axis_index("c")
    rank = me_y * 2 + me_x
    rows = low[0].shape[0]
    at = pl.ds(pl.multiple_of(me_z * (4 * rows) + rank * rows, rows), rows)
    peers = ((("x",), me_y * 2 + 1 - me_x), (("y",), (1 - me_y) * 2 + me_x))
    peers += ((("y", "x"), (1 - me_y) * 2 + 1 - me_x),)

    def piece(index, owner):
        width = low[index].shape[1] // 4
        return low[index].at[:, pl.ds(pl.multiple_of(owner * width, width), width)]

    def fill(index):
        loads[index].wait()
        size = 512

        @pl.loop(0, low[index].shape[1] // size)
        def _(step):
            here = pl.ds(pl.multiple_of(step * size, size), size)
            if turned[index]:
                low[index][:, here] = wide[index][here, :].T.astype(BF16)
            else:
                low[index][:, here] = wide[index][:, here].astype(BF16)

        keeps[index].start()

    def target(index):
        width = low[index].shape[1] // 4
        if index < narrow:
            return wholes[0].at[at, pl.ds(index * width, width)]
        return wholes[index - narrow + 1].at[at]

    devices = packed.shape[0]
    me = (me_z * 4 + rank) * 2 + me_c
    keeps = [
        pltpu.make_async_copy(piece(index, rank), target(index), local.at[index])
        for index in range(count)
    ]
    keeps.append(pltpu.make_async_copy(places, all_places.at[rank], local.at[count]))
    keeps.append(pltpu.make_async_copy(packed.at[me], landed.at[me], local.at[count + 1]))
    for keep in keeps[count:]:
        keep.start()

    def device(shift):
        other = lax.rem(me + shift, devices)
        chip = other // 2
        return {"z": chip // 4, "y": lax.rem(chip // 2, 2), "x": lax.rem(chip, 2), "c": lax.rem(other, 2)}

    barrier = pltpu.get_barrier_semaphore()

    @pl.loop(1, devices)
    def _(shift):
        pl.semaphore_signal(barrier, inc=1, device_id=device(shift), device_id_type=MESH)

    for index in range(narrow):
        fill(index)
    pl.semaphore_wait(barrier, devices - 1)
    copies = {}

    def share(index, source_of, goal):
        for number, (axes, owner) in enumerate(peers):
            slot = 3 * index + number
            copies[index, number] = push(axes, source_of(owner), goal, send.at[slot], recv.at[slot])

    def arrive(index):
        keeps[index].wait()
        for number in range(3):
            copies[index, number].wait_recv()

    for index in range(narrow):
        share(index, functools.partial(piece, index), target(index))
    share(count, lambda owner: places, all_places.at[rank])

    @pl.loop(1, devices)
    def _(shift):
        other = lax.rem(me + shift, devices)
        pltpu.make_async_remote_copy(
            src_ref=packed.at[other],
            dst_ref=landed.at[me],
            send_sem=rows_send,
            recv_sem=rows_recv,
            device_id=device(shift),
            device_id_type=MESH,
        ).start()

    for index in range(narrow, count):
        fill(index)
    for index in range(narrow):
        arrive(index)
    ride.begin()
    for index in range(narrow, count):
        share(index, functools.partial(piece, index), target(index))
    most = pl.ds(0, devices - 1)
    pltpu.make_async_copy(packed.at[most], landed.at[most], rows_recv).wait()
    ride.advance()
    for index in range(narrow, count + 1):
        arrive(index)
    keeps[count + 1].wait()
    ride.finish()
    for copy in copies.values():
        copy.wait_send()
    pltpu.make_async_copy(packed.at[most], packed.at[most], rows_send).wait()


def dispatch(weights, turned, narrow, places, packed, steps, name):
    flat = [w.shape[::-1] if flip_it else w.shape for w, flip_it in zip(weights, turned)]
    rows = flat[0][0]
    total = lax.axis_size("z")
    anywhere = pl.BlockSpec(memory_space=pltpu.HBM)
    count = len(weights)
    widths = [sum(shape[1] // 4 for shape in flat[:narrow])]
    widths += [shape[1] // 4 for shape in flat[narrow:]]
    shapes = [jax.ShapeDtypeStruct((total * 4 * rows, width), BF16) for width in widths]
    shapes.append(jax.ShapeDtypeStruct((4, *places.shape), places.dtype))
    shapes.append(jax.ShapeDtypeStruct(packed.shape, packed.dtype))
    return pl.pallas_call(
        functools.partial(dispatch_kernel, tuple(turned), narrow, steps),
        in_specs=[anywhere] * (count + 2),
        out_specs=[anywhere] * len(shapes),
        out_shape=shapes,
        scratch_shapes=[
            pltpu.SemaphoreType.DMA((3 * count + 3,)),
            pltpu.SemaphoreType.DMA((3 * count + 3,)),
            pltpu.SemaphoreType.DMA((count + 2,)),
            pltpu.SemaphoreType.DMA(()),
            pltpu.SemaphoreType.DMA(()),
            pltpu.SemaphoreType.DMA((steps,)),
            pltpu.SemaphoreType.DMA((steps,)),
            pltpu.SemaphoreType.DMA((count,)),
        ]
        + [pltpu.VMEM(weight.shape, F32) for weight in weights]
        + [pltpu.VMEM(shape, BF16) for shape in flat],
        compiler_params=pltpu.CompilerParams(
            collective_id=IDS.index(name), has_side_effects=True, vmem_limit_bytes=VMEM_BYTES
        ),
        cost_estimate=pl.CostEstimate(flops=0, bytes_accessed=120 << 20, transcendentals=0),
        name=name,
    )(*weights, places, packed)


def gather_stages(own, out, send, recv, local, ride):
    rows = own.shape[0]
    half = rows // 2

    def part(core, y, x, side):
        start = block_at(core, y, x) * rows + side * half
        return out.at[pl.ds(pl.multiple_of(start, half), half)]

    def over(axis, source, target, slot):
        return push((axis,), source, target, send.at[slot], recv.at[slot])

    def across(y, x, side, slot):
        here = part(0, y, x, side)
        return over("c", here, here, slot)

    whole = out.at[pl.ds(pl.multiple_of(block_at(0, 0, 0) * rows, rows), rows)]
    keep = pltpu.make_async_copy(own, whole, local)
    keep.start()
    greet((("x",), ("y",), ("c",)), ride.steps > 0)
    first, second = own.at[pl.ds(0, half)], own.at[pl.ds(half, half)]
    x_first = over("x", first, part(0, 0, 0, 0), 0)
    y_second = over("y", second, part(0, 0, 0, 1), 1)
    x_second = over("x", second, part(0, 0, 0, 1), 2)
    y_first = over("y", first, part(0, 0, 0, 0), 3)
    ride.begin()
    crossed = [over("c", own, whole, 4)]
    yield
    x_first.wait_recv()
    far_first = over("y", part(0, 0, 1, 0), part(0, 0, 1, 0), 5)
    crossed.append(across(0, 1, 0, 6))
    y_second.wait_recv()
    far_second = over("x", part(0, 1, 0, 1), part(0, 1, 0, 1), 7)
    crossed.append(across(1, 0, 1, 8))
    yield
    x_second.wait_recv()
    crossed.append(across(0, 1, 1, 9))
    y_first.wait_recv()
    crossed.append(across(1, 0, 0, 10))
    ride.advance()
    yield
    far_first.wait_recv()
    crossed.append(across(1, 1, 0, 11))
    far_second.wait_recv()
    crossed.append(across(1, 1, 1, 12))
    for copy in crossed:
        copy.wait_recv()
    keep.wait()
    ride.advance()
    yield
    ride.finish()
    for copy in crossed + [x_first, y_second, x_second, y_first, far_first, far_second]:
        copy.wait_send()
    yield


def gather_body(inputs, outputs, scratch, ride):
    for _ in gather_stages(inputs[0], outputs[0], *scratch, ride):
        pass


def gather_turns_body(inputs, outputs, scratch, ride):
    own, table_ref, places_ref = inputs
    out, cos_ref, sin_ref = outputs
    stages = gather_stages(own, out, *scratch, ride)
    next(stages)
    size, width = table_ref.shape[0], 2 * HEAD_DIM
    count, _, block = places_ref.shape
    for index in range(count):
        at = pl.ds(index * block, block)
        entry = lax.broadcasted_iota(jnp.int32, (size, block), 0)
        pick = (entry == places_ref[index]).astype(F32).astype(BF16)
        rows = outer_sum(pick, table_ref[:, :width])
        rows += outer_sum(pick, table_ref[:, width : 2 * width])
        rows += outer_sum(pick, table_ref[:, 2 * width :])
        cos_ref[at, :] = rows[:, :HEAD_DIM]
        sin_ref[at, :] = rows[:, HEAD_DIM:]

    for _ in stages:
        pass


def rotation_table(size):
    half_dim = HEAD_DIM // 2
    frequency = jnp.exp(-jnp.arange(half_dim, dtype=F32) * (2.0 * math.log(10000.0) / HEAD_DIM))
    angles = jnp.arange(size, dtype=jnp.int32).astype(F32)[:, None] * frequency[None, :]
    cos_half, sin_half = jnp.cos(angles), jnp.sin(angles)
    rest = jnp.concatenate([cos_half, cos_half, -sin_half, sin_half], axis=1)
    terms = []
    for _ in range(3):
        term = lax.reduce_precision(rest, 8, 7)
        terms.append(term.astype(BF16))
        rest = rest - term
    return jnp.concatenate(terms, axis=1)


def plane_gather_turns(rows, table, places, name, ride):
    anywhere = pl.BlockSpec(memory_space=pltpu.HBM)
    near = pl.BlockSpec(memory_space=pltpu.VMEM)
    total = 8 * rows.shape[0]
    got = communicate(
        gather_turns_body,
        [rows, table, places],
        [anywhere, near, near],
        [jax.ShapeDtypeStruct((total, rows.shape[1]), rows.dtype)]
        + [jax.ShapeDtypeStruct((total, HEAD_DIM), F32)] * 2,
        [anywhere, near, near],
        [
            pltpu.SemaphoreType.DMA((13,)),
            pltpu.SemaphoreType.DMA((13,)),
            pltpu.SemaphoreType.DMA(()),
        ],
        name,
        ride,
    )
    return got[:3], got[3:]


def outer_tiles(sources, targets, tiles, stage, loads, stores, between=lambda: None):
    count = tiles[0].shape[0]
    tile = tiles[0].shape[2]
    total = sources[0][0].shape[1] // tile

    def fetch(index, slot):
        at = pl.ds(pl.multiple_of(index * tile, tile), tile)
        return [
            pltpu.make_async_copy(source.at[:, at], held.at[slot], loads.at[number, slot])
            for number, ((source, _), held) in enumerate(zip(sources, tiles))
        ]

    def keep(index, slot):
        at = pl.ds(pl.multiple_of(index * tile, tile), tile)
        return [
            pltpu.make_async_copy(
                stage.at[slot, :, pl.ds(start, size)], target.at[at], stores.at[number, slot]
            )
            for number, (target, start, size) in enumerate(targets)
        ]

    for copy in fetch(0, 0):
        copy.start()

    def multiply(index):
        slot = lax.rem(index, count)

        @pl.when(index + 1 < total)
        def _():
            for copy in fetch(index + 1, lax.rem(index + 1, count)):
                copy.start()

        @pl.when(index >= count)
        def _():
            for copy in keep(index - count, slot):
                copy.wait()

        for copy in fetch(index, slot):
            copy.wait()
        for (_, parts), held in zip(sources, tiles):
            left = held[slot]
            for start, size, right in parts:
                stage[slot, :, pl.ds(start, size)] = outer_sum(left, right()).astype(BF16)
        for copy in keep(index, slot):
            copy.start()

    pl.loop(0, total // 2)(multiply)
    between()
    pl.loop(total // 2, total)(multiply)
    for index in range(max(total - count, 0), total):
        for copy in keep(index, index % count):
            copy.wait()


def outer_scratch(rows, sources, columns, targets, tile=256):
    return [pltpu.VMEM((2, rows, tile), BF16)] * sources + [
        pltpu.VMEM((2, tile, columns), BF16),
        pltpu.SemaphoreType.DMA((sources, 2)),
        pltpu.SemaphoreType.DMA((targets, 2)),
    ]


def gather_hidden_body(inputs, outputs, scratch, ride):
    own, seen_ref, gate_ref, up_ref = inputs
    out, hidden_ref, by_gate_ref, by_up_ref, weight_ref = outputs
    seen, gate_w, up_w, hidden, by_gate, by_up, loads, stores, *outer = scratch[3:]
    blocks, block = seen.shape[0], seen.shape[1]
    width = gate_w.shape[1]
    tile = 512
    fetch = [
        pltpu.make_async_copy(gate_ref, gate_w, loads.at[0]),
        pltpu.make_async_copy(up_ref, up_w, loads.at[1]),
    ]
    for index in range(blocks):
        at = pl.ds(index * block, block)
        fetch.append(pltpu.make_async_copy(seen_ref.at[at], seen.at[index], loads.at[2 + index]))
    for index in (0, 2, 1, *range(3, len(fetch))):
        fetch[index].start()
    stages = gather_stages(own, out, *scratch[:3], ride)
    next(stages)
    fetch[0].wait()
    fetch[1].wait()
    kept = []
    for index in range(blocks):
        fetch[2 + index].wait()

        @pl.loop(0, width // tile)
        def _(step):
            at = pl.ds(pl.multiple_of(step * tile, tile), tile)
            here = seen[index]
            gate = project(here, gate_w[:, at])
            up = project(here, up_w[:, at])
            turned = 1.0 / (1.0 + jnp.exp(-gate))
            silu = gate * turned
            hidden[pl.ds(index * block, block), at] = (silu * up).astype(BF16)
            by_up[pl.ds(index * block, block), at] = silu.astype(BF16)
            by_gate[pl.ds(index * block, block), at] = (up * (turned * (1.0 + gate * (1.0 - turned)))).astype(BF16)

        rows_at = pl.ds(index * block, block)
        pairs = ((hidden, hidden_ref), (by_gate, by_gate_ref), (by_up, by_up_ref))
        for number, (held, target) in enumerate(pairs):
            copy = pltpu.make_async_copy(
                held.at[rows_at], target.at[rows_at], stores.at[number, index]
            )
            copy.start()
            kept.append(copy)
        if index in (3, 6):
            next(stages)
    next(stages)
    outer_tiles(
        [(out, [(0, width, lambda: hidden[...])])],
        [(weight_ref, 0, width)],
        outer[:1],
        *outer[1:],
    )
    next(stages)
    for copy in kept:
        copy.wait()


def plane_gather_hidden(rows, seen, gate_w, up_w, name, ride=None):
    total, depth = seen.shape
    width = gate_w.shape[1]
    block = rows.shape[0]
    blocks = total // block
    anywhere = pl.BlockSpec(memory_space=pltpu.HBM)
    got = communicate(
        gather_hidden_body,
        [rows, seen, gate_w, up_w],
        [anywhere] * 4,
        [jax.ShapeDtypeStruct((8 * rows.shape[0], rows.shape[1]), rows.dtype)]
        + [jax.ShapeDtypeStruct((total, width), BF16)] * 3
        + [jax.ShapeDtypeStruct((rows.shape[1], width), BF16)],
        [anywhere] * 5,
        [
            pltpu.SemaphoreType.DMA((13,)),
            pltpu.SemaphoreType.DMA((13,)),
            pltpu.SemaphoreType.DMA(()),
            pltpu.VMEM((blocks, block, depth), BF16),
            pltpu.VMEM((depth, width), BF16),
            pltpu.VMEM((depth, width), BF16),
            pltpu.VMEM((total, width), BF16),
            pltpu.VMEM((total, width), BF16),
            pltpu.VMEM((total, width), BF16),
            pltpu.SemaphoreType.DMA((2 + blocks,)),
            pltpu.SemaphoreType.DMA((3, blocks)),
        ]
        + outer_scratch(total, 1, width, 1),
        name,
        ride,
        flops=6 * total * depth * width,
    )
    return got[:5], got[5:]


def plane_gather(rows, name, ride=None):
    got = communicate(
        gather_body,
        [rows],
        [pl.BlockSpec(memory_space=pltpu.HBM)],
        [jax.ShapeDtypeStruct((8 * rows.shape[0], rows.shape[1]), rows.dtype)],
        [pl.BlockSpec(memory_space=pltpu.HBM)],
        [
            pltpu.SemaphoreType.DMA((13,)),
            pltpu.SemaphoreType.DMA((13,)),
            pltpu.SemaphoreType.DMA(()),
        ],
        name,
        ride,
    )
    return got[0], got[1:]


def product_body(make, starts, inputs, outputs, scratch, ride):
    out_ref = outputs[0]
    left, weight, away, got, near, by_y, by_x, end_y, end_x, send, recv, local = scratch[:12]
    block, width = out_ref.shape
    half = block // 2
    tile = 1024
    pairs = [(inputs[2 * i], inputs[2 * i + 1], start) for i, start in enumerate(starts)]

    def over(axis, source, target, slot):
        return push((axis,), source, target, send.at[slot], recv.at[slot])

    waits = {"weight": []}
    column = 0
    for index, (rows_ref, weight_ref, start) in enumerate(pairs):
        inner = weight_ref.shape[1] if make else rows_ref.shape[1]
        copy = pltpu.make_async_copy(
            weight_ref.at[:, pl.ds(start, inner)],
            weight.at[:, pl.ds(column, inner)],
            local.at[index, 8],
        )
        copy.start()
        waits["weight"].append(copy)
        column += inner
    order = ((1, 1, 1), (1, 1, 0), (0, 1, 1), (1, 0, 1), (0, 1, 0), (1, 0, 0), (0, 0, 1), (0, 0, 0))
    places = [pl.ds(pl.multiple_of(block_at(*key) * block, block), block) for key in order]
    if make:
        fill, follow = make(inputs, outputs, scratch[12:], left, places)
    else:
        for slot, key in enumerate(order):
            waits[key] = []
            column = 0
            for index, (rows_ref, _, _) in enumerate(pairs):
                inner = rows_ref.shape[1]
                copy = pltpu.make_async_copy(
                    rows_ref.at[places[slot]],
                    left.at[places[slot], pl.ds(column, inner)],
                    local.at[index, slot],
                )
                copy.start()
                waits[key].append(copy)
                column += inner
    greet((("x",), ("y",), ("c",)), ride.steps > 0)
    ride.begin()
    for copy in waits["weight"]:
        copy.wait()

    def multiply(key, store):
        slot = order.index(key)
        if make:
            fill(slot)
        else:
            for copy in waits[key]:
                copy.wait()
        here = left[places[slot], :]
        for start in range(0, width, tile):
            at = pl.ds(start, tile)
            store(at, project_t(here, weight[at, :]))

    crossing = {}

    def compute_far(y, x):
        index = 2 * y + x

        def store(at, value):
            away[index, :, at] = value.astype(BF16)

        multiply((1, y, x), store)
        crossing[index] = over("c", away.at[index], got.at[index], index)

    def compute_near(y, x):
        index = 2 * y + x
        crossing[index].wait_recv()

        def store(at, value):
            near[index, :, at] = (value + got[index, :, at].astype(F32)).astype(BF16)

        multiply((0, y, x), store)

    lower, upper = pl.ds(0, half), pl.ds(half, half)
    compute_far(1, 1)
    compute_far(1, 0)
    compute_near(1, 1)
    y_far = over("y", near.at[3, lower], by_y.at[1], 4)
    x_far = over("x", near.at[3, upper], by_x.at[1], 5)
    compute_far(0, 1)
    compute_near(1, 0)
    y_near = over("y", near.at[2, lower], by_y.at[0], 6)
    if make:
        ride.advance()
    compute_far(0, 0)
    compute_near(0, 1)
    x_near = over("x", near.at[1, upper], by_x.at[0], 7)
    y_far.wait_recv()
    near[1, lower, :] = (near[1, lower, :].astype(F32) + by_y[1].astype(F32)).astype(BF16)
    x_last = over("x", near.at[1, lower], end_x, 8)
    x_far.wait_recv()
    near[2, upper, :] = (near[2, upper, :].astype(F32) + by_x[1].astype(F32)).astype(BF16)
    y_last = over("y", near.at[2, upper], end_y, 9)
    if not make:
        ride.advance()
    compute_near(0, 0)
    if make:
        follow(ride.advance)
    y_near.wait_recv()
    out_ref[lower, :] = near[0, lower, :].astype(F32) + by_y[0].astype(F32)
    x_near.wait_recv()
    out_ref[upper, :] = near[0, upper, :].astype(F32) + by_x[0].astype(F32)
    x_last.wait_recv()
    out_ref[lower, :] += end_x[...].astype(F32)
    y_last.wait_recv()
    out_ref[upper, :] += end_y[...].astype(F32)
    ride.finish()
    for copy in list(crossing.values()) + [y_far, x_far, y_near, x_near, x_last, y_last]:
        copy.wait_send()


def product_scratch(total, inner, width, pairs):
    block = total // 8
    half = block // 2
    return [
        pltpu.VMEM((total, inner), BF16),
        pltpu.VMEM((width, inner), BF16),
        pltpu.VMEM((4, block, width), BF16),
        pltpu.VMEM((4, block, width), BF16),
        pltpu.VMEM((4, block, width), BF16),
        pltpu.VMEM((2, half, width), BF16),
        pltpu.VMEM((2, half, width), BF16),
        pltpu.VMEM((half, width), BF16),
        pltpu.VMEM((half, width), BF16),
        pltpu.SemaphoreType.DMA((10,)),
        pltpu.SemaphoreType.DMA((10,)),
        pltpu.SemaphoreType.DMA((pairs, 9)),
    ]


def hidden_back(inputs, outputs, scratch, left, places):
    by_gate_ref, gate_w, by_up_ref, up_w, grad_ref, down_ref, seen_ref = inputs
    weight_gate, weight_up = outputs[1:]
    down, rows, factors, down_load, row_loads, *outer = scratch
    width = down.shape[1]
    tile = 1024
    fetch_down = pltpu.make_async_copy(down_ref, down, down_load)
    fetch_down.start()

    def fetch(slot):
        at, held = places[slot], slot % 2
        return [
            pltpu.make_async_copy(grad_ref.at[at], rows.at[held], row_loads.at[0, held]),
            pltpu.make_async_copy(by_gate_ref.at[at], factors.at[held, 0], row_loads.at[1, held]),
            pltpu.make_async_copy(by_up_ref.at[at], factors.at[held, 1], row_loads.at[2, held]),
        ]

    for copy in fetch(0):
        copy.start()

    def fill(slot):
        if slot == 0:
            fetch_down.wait()
        for copy in fetch(slot):
            copy.wait()
        if slot + 1 < len(places):
            for copy in fetch(slot + 1):
                copy.start()
        held = slot % 2

        for start in range(0, width, tile):
            at, beside = pl.ds(start, tile), pl.ds(width + start, tile)
            grad = project(rows[held], down[:, at])
            left[places[slot], at] = (grad * factors[held, 0, :, at].astype(F32)).astype(BF16)
            left[places[slot], beside] = (grad * factors[held, 1, :, at].astype(F32)).astype(BF16)

    def follow(between):
        outer_tiles(
            [
                (
                    seen_ref,
                    [
                        (0, width, lambda: left[:, pl.ds(0, width)]),
                        (width, width, lambda: left[:, pl.ds(width, width)]),
                    ],
                )
            ],
            [(weight_gate, 0, width), (weight_up, width, width)],
            outer[:1],
            *outer[1:],
            between,
        )

    return fill, follow


def plane_product_back(grads, down, by_gate, by_up, gate_w, up_w, seen, name, ride):
    total, depth = grads.shape
    width = gate_w.shape[1]
    block = total // 8
    operands = [by_gate, gate_w, by_up, up_w, grads, down, seen]
    anywhere = pl.BlockSpec(memory_space=pltpu.HBM)
    got = communicate(
        functools.partial(product_body, hidden_back, [0, 0]),
        operands,
        [anywhere] * len(operands),
        [jax.ShapeDtypeStruct((block, depth), F32)]
        + [jax.ShapeDtypeStruct((depth, width), BF16)] * 2,
        [pl.BlockSpec(memory_space=pltpu.VMEM), anywhere, anywhere],
        product_scratch(total, 2 * width, depth, 2)
        + [
            pltpu.VMEM((depth, width), BF16),
            pltpu.VMEM((2, block, depth), BF16),
            pltpu.VMEM((2, 2, block, width), BF16),
            pltpu.SemaphoreType.DMA(()),
            pltpu.SemaphoreType.DMA((3, 2)),
        ]
        + outer_scratch(total, 1, 2 * width, 2),
        name,
        ride,
        flops=10 * total * depth * width,
    )
    return got[:3], got[3:]


def plane_product(pairs, name, ride=None):
    total = pairs[0][0].shape[0]
    inner = sum(rows.shape[1] for rows, _, _ in pairs)
    width = pairs[0][1].shape[0]
    operands = []
    for rows, weight, _ in pairs:
        operands += [rows, weight]
    got = communicate(
        functools.partial(product_body, None, [start for _, _, start in pairs]),
        operands,
        [pl.BlockSpec(memory_space=pltpu.HBM)] * len(operands),
        [jax.ShapeDtypeStruct((total // 8, width), F32)],
        [pl.BlockSpec(memory_space=pltpu.VMEM)],
        product_scratch(total, inner, width, len(pairs)),
        name,
        ride,
        flops=2 * total * inner * width,
    )
    return got[0], got[1:]


def ring_next(values):
    total = lax.axis_size("z")
    return lax.ppermute(values, "z", [(i, (i + 1) % total) for i in range(total)])


def ring_rows(whole, owner):
    rows = whole.shape[0] // lax.axis_size("z")
    return lax.dynamic_slice(whole, (owner * rows, 0), (rows, whole.shape[1]))


class Gathered:
    def __init__(self, whole, step=0):
        self.whole, self.step = whole, step

    def ride(self, count):
        count = min(count, lax.axis_size("z") - 1 - self.step)
        item = (self.whole, self.step, count)
        self.step += count
        return item

    def land(self, whole):
        self.whole = whole

    def walk(self, count):
        total = lax.axis_size("z")
        rows = self.whole.shape[0] // total
        last = min(self.step + count, total - 1)
        current = ring_rows(self.whole, owner_at(self.step)) if self.step < last else None
        while self.step < last:
            self.step += 1
            current = ring_next(current)
            self.whole = lax.dynamic_update_slice(self.whole, current, (owner_at(self.step) * rows, 0))

    def finish(self):
        self.walk(lax.axis_size("z"))
        return self.whole


class Summed:
    def __init__(self, whole):
        self.whole, self.step, self.running = whole, 0, None

    def ride(self, count):
        count = min(count, lax.axis_size("z") - 1 - self.step)
        item = (self.running, self.whole, self.step, count)
        self.step += count
        return item

    def land(self, running):
        self.running = running

    def walk(self, count):
        total = lax.axis_size("z")
        for _ in range(min(count, total - 1 - self.step)):
            running = ring_rows(self.whole, owner_at(1)) if self.running is None else self.running
            own = ring_rows(self.whole, owner_at((self.step + 2) % total))
            self.running = (ring_next(running).astype(F32) + own.astype(F32)).astype(BF16)
            self.step += 1

    def finish(self):
        self.walk(lax.axis_size("z"))
        return self.running


def from_plane(block):
    rows = block.shape[0] // 4
    me_y, me_x = lax.axis_index("y"), lax.axis_index("x")

    def piece(y, x):
        return lax.dynamic_slice(block, ((y * 2 + x) * rows, 0), (rows, block.shape[1]))

    own = piece(me_y, me_x)
    by_x = lax.ppermute(piece(me_y, 1 - me_x), "x", ((0, 1), (1, 0)))
    by_y = lax.ppermute(piece(1 - me_y, me_x), "y", ((0, 1), (1, 0)))
    far = lax.ppermute(piece(1 - me_y, 1 - me_x), ("y", "x"), ((0, 3), (1, 2), (2, 1), (3, 0)))

    def chosen(y, x):
        same_y, same_x = me_y == y, me_x == x
        return jnp.where(
            same_y, jnp.where(same_x, own, by_x), jnp.where(same_x, by_y, far)
        )

    return [chosen(y, x) for y in range(2) for x in range(2)]


def side_by_side(pieces, start=0, stop=None):
    return jnp.concatenate([piece[:, start:stop].astype(F32) for piece in pieces], axis=1)


def turn(values, cos_rows, sin_rows):
    return values * cos_rows + pltpu.roll(values, HEAD_DIM // 2, 1) * sin_rows


def visible_of(follow):
    size = follow.shape[1]
    row = lax.broadcasted_iota(jnp.int32, (size, size), 0)
    column = lax.broadcasted_iota(jnp.int32, (size, size), 1)
    return (column <= row) & (row - column <= follow)


def soft_of(queries, keys, visible):
    scores = project_t(queries, keys) * (1.0 / math.sqrt(HEAD_DIM))
    scores = jnp.where(visible, scores, NEG_LARGE)
    weights = jnp.exp(scores - jnp.max(scores, axis=1, keepdims=True))
    return weights / jnp.sum(weights, axis=1, keepdims=True)


def attend_body(inputs, outputs):
    seen_ref, weight_ref, cos_ref, sin_ref, follow_ref = inputs
    low_ref, out_ref = outputs
    width = out_ref.shape[1]
    cos_rows, sin_rows = cos_ref[...], sin_ref[...]
    visible = visible_of(follow_ref[0])
    lin = project(seen_ref[...], weight_ref[...])
    for start in range(0, width, HEAD_DIM):
        here = slice(start, start + HEAD_DIM)
        key_at = slice(width + start, width + start + HEAD_DIM)
        value_at = slice(2 * width + start, 2 * width + start + HEAD_DIM)
        queries = turn(lin[:, here], cos_rows, sin_rows).astype(BF16)
        keys = turn(lin[:, key_at], cos_rows, sin_rows).astype(BF16)
        values = lin[:, value_at].astype(BF16)
        low_ref[:, here] = queries
        low_ref[:, key_at] = keys
        low_ref[:, value_at] = values
        soft = soft_of(queries, keys, visible).astype(BF16)
        out_ref[:, here] = project(soft, values).astype(BF16)


def attend_back_body(blocks, inputs, outputs, grads_held):
    low_ref, seen_ref, weight_ref, cos_ref, sin_ref, follow_ref = inputs[:6]
    seen_tile, grad_tile, attended_ref = inputs[6:]
    out_ref, outer_ref = outputs
    step = pl.program_id(0)
    block = out_ref.shape[0]

    @pl.when(step < blocks)
    def _():
        attend_back_block(inputs[:6], out_ref)
        grads_held[pl.ds(pl.multiple_of(step * block, block), block), :] = out_ref[...]

    @pl.when(step >= blocks)
    def _():
        width = out_ref.shape[1]
        outer_ref[:, :width] = outer_sum(seen_tile[...], grads_held[...]).astype(BF16)
        outer_ref[:, width:] = outer_sum(grad_tile[...], attended_ref[...]).astype(BF16)


def attend_back_block(inputs, out_ref):
    low_ref, seen_ref, weight_ref, cos_ref, sin_ref, follow_ref = inputs
    width = weight_ref.shape[1]
    cos_rows, sin_rows = cos_ref[...], -sin_ref[...]
    visible = visible_of(follow_ref[0])
    scale = 1.0 / math.sqrt(HEAD_DIM)
    grad_all = project(seen_ref[...], weight_ref[...]).astype(BF16)
    for start in range(0, width, HEAD_DIM):
        here = slice(start, start + HEAD_DIM)
        key_at = slice(width + start, width + start + HEAD_DIM)
        value_at = slice(2 * width + start, 2 * width + start + HEAD_DIM)
        queries, keys, values = low_ref[:, here], low_ref[:, key_at], low_ref[:, value_at]
        grad = grad_all[:, here]
        soft = soft_of(queries, keys, visible)
        grad_soft = project_t(grad, values)
        inner = jnp.sum(soft * grad_soft, axis=1, keepdims=True)
        grad_scores = (soft * (grad_soft - inner)).astype(BF16)
        grad_query = project(grad_scores, keys) * scale
        grad_key = outer_sum(grad_scores, queries) * scale
        out_ref[:, here] = turn(grad_query, cos_rows, sin_rows).astype(BF16)
        out_ref[:, key_at] = turn(grad_key, cos_rows, sin_rows).astype(BF16)
        out_ref[:, value_at] = outer_sum(soft.astype(BF16), grad).astype(BF16)


def plane_peers():
    me_y, me_x = lax.axis_index("y"), lax.axis_index("x")
    return (
        (("x",), me_y * 2 + 1 - me_x),
        (("y",), (1 - me_y) * 2 + me_x),
        (("y", "x"), (1 - me_y) * 2 + 1 - me_x),
    )


def collect_copies(blocks, outs, send, recv, local):
    rank = lax.axis_index("y") * 2 + lax.axis_index("x")
    keeps, copies = [], []
    for index, (block, out) in enumerate(zip(blocks, outs)):
        rows = block.shape[0] // 4

        def piece(owner, block=block, rows=rows):
            return block.at[pl.ds(pl.multiple_of(owner * rows, rows), rows)]

        keeps.append(pltpu.make_async_copy(piece(rank), out.at[rank], local.at[index]))
        for number, (axes, owner) in enumerate(plane_peers()):
            copies.append(
                pltpu.make_async_remote_copy(
                    src_ref=piece(owner),
                    dst_ref=out.at[rank],
                    send_sem=send.at[3 * index + number],
                    recv_sem=recv.at[3 * index + number],
                    device_id=flip(*axes),
                    device_id_type=MESH,
                )
            )
    return keeps, copies


def collected_shape(block):
    return jax.ShapeDtypeStruct((4, block.shape[0] // 4, block.shape[1]), block.dtype)


def by_blocks(
    body, operands, specs, shapes, out_specs, blocks, name, ride, flops, collect=(), own_scratch=(), advances=()
):
    extra = len(collect)
    operands, shapes = list(operands) + list(collect), list(shapes)
    shapes += [collected_shape(block) for block in collect]
    anywhere = pl.BlockSpec(memory_space=pltpu.HBM)
    specs, out_specs = list(specs) + [anywhere] * extra, list(out_specs) + [anywhere] * extra
    scratch = list(own_scratch)
    if extra:
        scratch += [
            pltpu.SemaphoreType.DMA((3 * extra,)),
            pltpu.SemaphoreType.DMA((3 * extra,)),
            pltpu.SemaphoreType.DMA((extra,)),
        ]
    count_in, count_out = len(operands), len(shapes)
    all_in = count_in + len(ride.operands)
    all_out = count_out + len(ride.shapes)

    def kernel(*refs):
        inputs, outputs, held = refs[:all_in], refs[all_in : all_in + all_out], refs[all_in + all_out :]
        step = pl.program_id(0)
        ride.board(inputs[count_in:], outputs[count_out:], held[len(scratch) :])
        keeps, copies = [], []
        if extra:
            keeps, copies = collect_copies(
                inputs[count_in - extra : count_in], outputs[count_out - extra : count_out], *held[len(scratch) - 3 : len(scratch)]
            )
        if ride.copies or extra:

            @pl.when(step == 0)
            def _():
                greet([axes for axes, _ in plane_peers()] if extra else (), bool(ride.copies))
                ride.begin()
                for copy in keeps + copies:
                    copy.start()

        body(inputs[: count_in - extra], outputs[: count_out - extra], *held[: len(own_scratch)])
        for number in advances:
            pl.when(step == number)(ride.advance)
        if ride.copies or extra:

            @pl.when(step == blocks - 1)
            def _():
                for copy in keeps:
                    copy.wait()
                for copy in copies:
                    copy.wait()
                ride.finish()

    params = {"collective_id": IDS.index(name), "has_side_effects": True} if ride.steps or extra else {}
    got = pl.pallas_call(
        kernel,
        grid=(blocks,),
        in_specs=list(specs) + [anywhere] * len(ride.operands),
        out_specs=list(out_specs) + [anywhere] * len(ride.shapes),
        out_shape=list(shapes) + ride.shapes,
        scratch_shapes=scratch + ride.scratch,
        input_output_aliases={count_in + k: count_out + v for k, v in ride.aliases.items()},
        compiler_params=pltpu.CompilerParams(vmem_limit_bytes=VMEM_BYTES, **params),
        cost_estimate=pl.CostEstimate(flops=flops, bytes_accessed=40 << 20, transcendentals=0),
        name=name,
    )(*operands, *ride.operands)
    return list(got)


def row_spec(rows, columns):
    return pl.BlockSpec((rows, columns), lambda i: (i, 0))


def attend(seen, weight, cos_rows, sin_rows, places, block, ride):
    rows, depth = seen.shape
    width = weight.shape[1] // 4
    got = by_blocks(
        attend_body,
        [seen, weight, cos_rows, sin_rows, places],
        [
            row_spec(block, depth),
            pl.BlockSpec((depth, 3 * width), lambda i: (0, 0)),
            row_spec(block, HEAD_DIM),
            row_spec(block, HEAD_DIM),
            pl.BlockSpec((1, 1, block), lambda i: (i, 0, 0)),
        ],
        [
            jax.ShapeDtypeStruct((rows, 3 * width), BF16),
            jax.ShapeDtypeStruct((rows, width), BF16),
        ],
        [row_spec(block, 3 * width), row_spec(block, width)],
        rows // block,
        "attend",
        ride,
        4 * rows * block * width + 6 * rows * depth * width,
    )
    return got[:2], got[2:]


def attend_back(low, grad_all, weight, cos_rows, sin_rows, places, seen, attended, block, ride, collect):
    rows, depth = grad_all.shape
    width = weight.shape[1] // 4
    blocks = rows // block
    tile = 256

    def early(columns):
        return pl.BlockSpec((block, columns), lambda i: (jnp.minimum(i, blocks - 1), 0))

    def late(i):
        return jnp.maximum(i - blocks, 0)

    got = by_blocks(
        functools.partial(attend_back_body, blocks),
        [low, grad_all, weight, cos_rows, sin_rows, places, seen, grad_all, attended],
        [
            early(3 * width),
            early(depth),
            pl.BlockSpec((depth, width), lambda i: (0, 3)),
            early(HEAD_DIM),
            early(HEAD_DIM),
            pl.BlockSpec((1, 1, block), lambda i: (jnp.minimum(i, blocks - 1), 0, 0)),
            pl.BlockSpec((rows, tile), lambda i: (0, late(i))),
            pl.BlockSpec((rows, tile), lambda i: (0, late(i))),
            pl.BlockSpec((rows, width), lambda i: (0, 0)),
        ],
        [
            jax.ShapeDtypeStruct((rows, 3 * width), BF16),
            jax.ShapeDtypeStruct((depth, 4 * width), BF16),
        ],
        [early(3 * width), pl.BlockSpec((tile, 4 * width), lambda i: (late(i), 0))],
        blocks + depth // tile,
        "attend_back",
        ride,
        10 * rows * block * width + 10 * rows * depth * width,
        collect,
        [pltpu.VMEM((rows, 3 * width), BF16)],
        (blocks - 2, blocks + depth // tile - 3),
    )
    last = 2 + len(collect)
    return got[:last], got[last:]


def plane_places(segments, block):
    groups, size = segments.shape
    numbers = jnp.arange(SEGS, dtype=jnp.int32)
    starts = jnp.sum((segments[:, :, None] < numbers).astype(jnp.int32), axis=1)
    ends = jnp.sum((segments[:, :, None] <= numbers).astype(jnp.int32), axis=1)
    onehot = segments[:, :, None] == numbers
    row = jnp.arange(size, dtype=jnp.int32)[None, :]
    places = row - jnp.sum(jnp.where(onehot, starts[:, None, :], 0), axis=2)
    follow = jnp.sum(jnp.where(onehot, ends[:, None, :], 0), axis=2) - 1 - row
    return places.reshape(-1, 1, block), follow.reshape(-1, 1, block)


def after(values, *gates):
    return lax.optimization_barrier((values,) + gates)[0]


EVERY = ("z", "y", "x", "c")


def exchange(rows):
    return lax.all_to_all(rows, EVERY, split_axis=0, concat_axis=0, tiled=True)


def on_device(
    tokens_in,
    cotangent,
    segment_ids,
    destination,
    source,
    w_query,
    w_key,
    w_value,
    w_out,
    w_gate,
    w_up,
    w_down,
):
    tok_rows = tokens_in.shape[0]
    devices = lax.axis_size(EVERY)
    per_peer = tok_rows // devices
    row_index = jnp.arange(tok_rows, dtype=jnp.int32)
    peer_to = destination // tok_rows
    ahead_rows = (peer_to[None, :] == peer_to[:, None]) & (
        destination[None, :] < destination[:, None]
    )
    send_slot = peer_to * per_peer + jnp.sum(ahead_rows.astype(jnp.int32), axis=1)
    peer_from = source // tok_rows
    before = (peer_from[None, :] == peer_from[:, None]) & (row_index[None, :] < row_index[:, None])
    recv_slot = peer_from * per_peer + jnp.sum(before.astype(jnp.int32), axis=1)
    send_pick = (send_slot[:, None] == row_index[None, :]).astype(BF16)
    recv_pick = (recv_slot[:, None] == row_index[None, :]).astype(BF16)

    packed = outer_sum(send_pick, tokens_in).astype(BF16)
    table = rotation_table(tok_rows)
    weights = [w_query, w_key, w_value, w_out, w_gate, w_up, w_down]
    attention_whole, gate_whole, up_whole, down_whole, segments, landed = dispatch(
        weights,
        [False, False, False, True, False, False, True],
        4,
        segment_ids.reshape(-1, 128),
        packed.reshape(devices, per_peer, -1),
        2,
        "dispatch",
    )
    arrived = project(recv_pick, landed.reshape(tok_rows, -1))
    attention_w, gate_w = Gathered(attention_whole, 2), Gathered(gate_whole)
    up_w, down_w = Gathered(up_whole), Gathered(down_whole)
    head_width = w_query.shape[1] // 4
    places, follow = plane_places(segments.reshape(4, -1), tok_rows)
    normed_one, scale_one = norm_parts(arrived)
    def send_back(rows):
        return exchange(outer_sum(recv_pick, rows.astype(BF16)).astype(BF16))

    def riding(call, gathers=(), sums=()):
        ride = Ride(
            [weight.ride(count) for weight, count in gathers],
            [gradient.ride(count) for gradient, count in sums],
        )
        result, landed = call(ride)
        for (item, _), value in zip(tuple(gathers) + tuple(sums), landed):
            item.land(value)
        return result

    seen_one, cos_rows, sin_rows = riding(
        lambda ride: plane_gather_turns(
            normed_one.astype(BF16), table, places, "gather_one", ride
        ),
        [(attention_w, 1), (gate_w, 1)],
    )
    attention = attention_w.finish()
    upstream_low = project(
        recv_pick,
        exchange(outer_sum(send_pick, after(cotangent, seen_one)).astype(BF16)),
    ).astype(BF16)
    upstream = upstream_low.astype(F32)
    qkv_low, attended = riding(
        lambda ride: attend(seen_one, attention, cos_rows, sin_rows, follow, tok_rows, ride),
        [(gate_w, 1)],
    )
    middle = arrived + riding(
        lambda ride: plane_product([(attended, attention, 3 * head_width)], "product_out", ride),
        [(gate_w, 1), (up_w, 1)],
    )
    normed_two, scale_two = norm_parts(middle)
    seen_two = riding(
        lambda ride: plane_gather(normed_two.astype(BF16), "gather_two", ride), [(up_w, 2)]
    )
    gate_whole, up_whole = gate_w.finish(), up_w.finish()
    grad_two_all, hidden, by_gate, by_up, weight_down = riding(
        lambda ride: plane_gather_hidden(
            upstream_low, seen_two, gate_whole, up_whole, "gather_up", ride
        ),
        [(down_w, 3)],
    )
    down_whole = down_w.finish()
    summed_down = Summed(weight_down)
    grad_normed_two, weight_gate, weight_up = riding(
        lambda ride: plane_product_back(
            grad_two_all,
            down_whole,
            by_gate,
            by_up,
            gate_whole,
            up_whole,
            seen_two,
            "product_forward",
            ride,
        ),
        (),
        [(summed_down, 3)],
    )
    summed_gate, summed_up = Summed(weight_gate), Summed(weight_up)
    output = middle + riding(
        lambda ride: plane_product(
            [(after(hidden, grad_normed_two), down_whole, 0)], "product_down", ride
        ),
        (),
        [(summed_gate, 2)],
    )
    returned_out = send_back(output)
    grad_middle = upstream + norm_back(normed_two, scale_two, grad_normed_two)
    grad_one_all = riding(
        lambda ride: plane_gather(
            after(grad_middle.astype(BF16), output), "gather_middle", ride
        ),
        (),
        [(summed_gate, 1), (summed_up, 1)],
    )
    grad_qkv, weight_attention, own_down, own_gate = riding(
        lambda ride: attend_back(
            after(qkv_low, returned_out),
            grad_one_all,
            attention,
            cos_rows,
            sin_rows,
            follow,
            seen_one,
            attended,
            tok_rows,
            ride,
            (summed_down.finish(), summed_gate.finish()),
        ),
        (),
        [(summed_up, 2)],
    )
    summed_attention = Summed(weight_attention)
    grad_normed_one = riding(
        lambda ride: plane_product([(grad_qkv, attention, 0)], "product_qkv", ride),
        (),
        [(summed_attention, 2)],
    )
    grad_inputs = grad_middle + norm_back(normed_one, scale_one, grad_normed_one)
    own_up, last_attention = from_plane(summed_up.finish()), summed_attention.finish()
    own_attention = from_plane(last_attention)
    own_down, own_gate, own_up = [
        after(own, last_attention) for own in (own_down, own_gate, jnp.stack(own_up))
    ]

    return (
        project(send_pick, after(returned_out, grad_normed_one)),
        project(send_pick, send_back(grad_inputs)),
        side_by_side(own_attention, 0, head_width),
        side_by_side(own_attention, head_width, 2 * head_width),
        side_by_side(own_attention, 2 * head_width, 3 * head_width),
        side_by_side(own_attention, 3 * head_width).T,
        side_by_side(own_gate),
        side_by_side(own_up),
        side_by_side(own_down).T,
    )


def solution(mesh):
    groups, cores = mesh.shape["dp"], mesh.shape["tensor"]
    whole = Mesh(mesh.devices.reshape(groups // 4, 2, 2, cores), EVERY)
    rows = P(EVERY, None)
    tall = P(("z", "y", "x"), "c")
    wide = P("c", ("z", "y", "x"))
    in_specs = (
        rows,
        rows,
        P(("z", "y", "x")),
        P(EVERY),
        P(EVERY),
        tall,
        tall,
        tall,
        wide,
        tall,
        tall,
        wide,
    )
    out_specs = (rows, rows, tall, tall, tall, wide, tall, tall, wide)
    return jax.shard_map(
        on_device, mesh=whole, in_specs=in_specs, out_specs=out_specs, check_vma=False
    )
```

```python
import functools
import math

import jax
import jax.numpy as jnp
from jax import lax
from jax.experimental import pallas as pl
from jax.experimental.pallas import tpu as pltpu
from jax.sharding import Mesh
from jax.sharding import PartitionSpec as P

HEAD_DIM = 128
SEGS = 4
EPSILON = 1e-05
NEG_LARGE = -1e30
VMEM_BYTES = 60 << 20
F32 = jnp.float32
BF16 = jnp.bfloat16
MESH = pl.DeviceIdType.MESH
IDS = (
    "dispatch",
    "gather_one",
    "gather_two",
    "gather_middle",
    "product_out",
    "product_forward",
    "product_qkv",
    "product_down",
    "gather_up",
    "attend",
    "attend_back",
)


def project(left, right):
    return jnp.dot(left, right, preferred_element_type=F32)


def project_t(left, right):
    return lax.dot_general(left, right, (((1,), (1,)), ((), ())), preferred_element_type=F32)


def outer_sum(left, right):
    return lax.dot_general(left, right, (((0,), (0,)), ((), ())), preferred_element_type=F32)


def norm_parts(values):
    center = values - jnp.mean(values, axis=-1, keepdims=True)
    spread = jnp.mean(center * center, axis=-1, keepdims=True)
    scale = lax.rsqrt(spread + EPSILON)
    return center * scale, scale


def norm_back(normed, scale, gradient):
    mean_grad = jnp.mean(gradient, axis=-1, keepdims=True)
    mean_both = jnp.mean(gradient * normed, axis=-1, keepdims=True)
    return (gradient - mean_grad - normed * mean_both) * scale


def flip(*axes):
    return {axis: 1 - lax.axis_index(axis) for axis in axes}


def owner_at(step):
    total = lax.axis_size("z")
    return lax.rem(lax.axis_index("z") + total - step, total)


def greet(peers, ring):
    barrier = pltpu.get_barrier_semaphore()
    for axes in peers:
        pl.semaphore_signal(barrier, inc=1, device_id=flip(*axes), device_id_type=MESH)
    count = len(peers)
    if ring:
        pl.semaphore_signal(barrier, inc=1, device_id={"z": owner_at(1)}, device_id_type=MESH)
        count += 1
    pl.semaphore_wait(barrier, count)


def push(axes, source, target, send, recv):
    copy = pltpu.make_async_remote_copy(
        src_ref=source,
        dst_ref=target,
        send_sem=send,
        recv_sem=recv,
        device_id=flip(*axes),
        device_id_type=MESH,
    )
    copy.start()
    return copy


class Ride:
    sides = 2

    def __init__(self, gathers=(), sums=()):
        self.gathers, self.sums = tuple(gathers), tuple(sums)
        self.operands, self.shapes, self.scratch = [], [], []
        self.aliases = {}
        self.steps = 0
        for whole, first, count in self.gathers:
            self.aliases[len(self.operands)] = len(self.shapes)
            self.operands.append(whole)
            self.shapes.append(jax.ShapeDtypeStruct(whole.shape, whole.dtype))
            self.steps += count
        for running, whole, first, count in self.sums:
            self.operands += [whole] if running is None else [running, whole]
            block = (whole.shape[0] // lax.axis_size("z"), whole.shape[1])
            self.shapes.append(jax.ShapeDtypeStruct(block, whole.dtype))
            self.steps += count
            self.scratch += [
                pltpu.VMEM((count, *block), whole.dtype),
                pltpu.VMEM((count, *block), whole.dtype),
                pltpu.SemaphoreType.DMA((count + 1,)),
            ]
        if self.steps:
            self.scratch += [
                pltpu.SemaphoreType.DMA((2 * self.steps,)),
                pltpu.SemaphoreType.DMA((2 * self.steps,)),
            ]

    def board(self, inputs, outputs, scratch):
        inputs, outputs, scratch = list(inputs), list(outputs), list(scratch)
        self.loads, self.copies, self.prepares, self.begun = [], [], [], 0
        self.ends = []
        if not self.steps:
            return
        total = lax.axis_size("z")
        send, recv = scratch[-2], scratch[-1]
        ahead = {"z": owner_at(total - 1)}

        def rows_of(whole, step):
            rows = whole.shape[0] // total
            return whole.at[pl.ds(pl.multiple_of(owner_at(step % total) * rows, rows), rows)]

        def plan(source, target, prepare=None):
            half = source.shape[0] // self.sides
            slot = self.sides * len(self.copies)
            self.copies.append(
                [
                    pltpu.make_async_remote_copy(
                        src_ref=source.at[pl.ds(side * half, half)],
                        dst_ref=target.at[pl.ds(side * half, half)],
                        send_sem=send.at[slot + side],
                        recv_sem=recv.at[slot + side],
                        device_id=ahead,
                        device_id_type=MESH,
                    )
                    for side in range(self.sides)
                ]
            )
            self.prepares.append(prepare)

        def adding(load, landed, own):
            def prepare(side):
                if side == 0:
                    load.wait()
                height = 64
                count = own.shape[0] // (2 * height)

                @pl.loop(side * count, side * count + count)
                def _(index):
                    at = pl.ds(pl.multiple_of(index * height, height), height)
                    own[at, :] = (own[at, :].astype(F32) + landed[at, :].astype(F32)).astype(BF16)

            return prepare

        for _, first, count in self.gathers:
            inputs.pop(0)
            whole = outputs.pop(0)
            for step in range(first, first + count):
                plan(rows_of(whole, step), rows_of(whole, step))
        for running, _, first, count in self.sums:
            source = None if running is None else inputs.pop(0)
            whole, final = inputs.pop(0), outputs.pop(0)
            landed, own, loaded = scratch[:3]
            scratch = scratch[3:]
            if source is None:
                source = rows_of(whole, 1)
            prepare = None
            for k in range(count):
                load = pltpu.make_async_copy(rows_of(whole, first + 2 + k), own.at[k], loaded.at[k])
                self.loads.append(load)
                plan(source, landed.at[k], prepare)
                prepare, source = adding(load, landed.at[k], own.at[k]), own.at[k]
            last = len(self.copies) - 1
            keep = pltpu.make_async_copy(own.at[count - 1], final, loaded.at[count])
            self.ends.append((last, prepare, keep))

    def start(self, number, side):
        if self.prepares[number]:
            self.prepares[number](side)
        self.copies[number][side].start()

    def begin(self):
        for load in self.loads:
            load.start()
        if self.copies:
            for side in range(self.sides):
                self.start(0, side)
            self.begun = 1

    def advance(self):
        if 0 < self.begun < len(self.copies):
            for side in range(self.sides):
                self.copies[self.begun - 1][side].wait_recv()
                self.start(self.begun, side)
            self.begun += 1

    def finish(self):
        while self.begun < len(self.copies):
            self.advance()
        for side in range(self.sides):
            if self.copies:
                self.copies[-1][side].wait_recv()
            for number, prepare, _ in self.ends:
                if side == 0 and number < len(self.copies) - 1:
                    prepare(0)
                    prepare(1)
                elif number == len(self.copies) - 1:
                    prepare(side)
        for _, _, keep in self.ends:
            keep.start()
        for pair in self.copies:
            for copy in pair:
                copy.wait_send()
        for _, _, keep in self.ends:
            keep.wait()


def block_at(core, y, x):
    def moved(axis, offset):
        here = lax.axis_index(axis)
        return 1 - here if offset else here

    return (moved("y", y) * 2 + moved("x", x)) * 2 + moved("c", core)


def communicate(body, operands, specs, shapes, out_specs, scratch, name, ride, flops=0):
    ride = ride or Ride()
    count_in, count_out, count_scratch = len(operands), len(shapes), len(scratch)
    all_in = count_in + len(ride.operands)
    all_out = count_out + len(ride.shapes)

    def kernel(*refs):
        inputs, outputs, held = refs[:all_in], refs[all_in : all_in + all_out], refs[all_in + all_out :]
        ride.board(inputs[count_in:], outputs[count_out:], held[count_scratch:])
        body(inputs[:count_in], outputs[:count_out], held[:count_scratch], ride)

    anywhere = pl.BlockSpec(memory_space=pltpu.HBM)
    got = pl.pallas_call(
        kernel,
        in_specs=list(specs) + [anywhere] * len(ride.operands),
        out_specs=list(out_specs) + [anywhere] * len(ride.shapes),
        out_shape=list(shapes) + ride.shapes,
        scratch_shapes=list(scratch) + ride.scratch,
        input_output_aliases={count_in + k: count_out + v for k, v in ride.aliases.items()},
        compiler_params=pltpu.CompilerParams(
            collective_id=IDS.index(name), has_side_effects=True, vmem_limit_bytes=VMEM_BYTES
        ),
        cost_estimate=pl.CostEstimate(
            flops=flops, bytes_accessed=120 << 20, transcendentals=0
        ),
        name=name,
    )(*operands, *ride.operands)
    return list(got)


class OwnRide(Ride):
    sides = 1

    def __init__(self, count):
        super().__init__()
        self.steps = count

    def take(self, whole, semaphores):
        self.gathers = ((None, 0, self.steps),)
        super().board([None], [whole], semaphores)


def dispatch_kernel(turned, narrow, steps, *refs):
    count = len(turned)
    inputs, refs = refs[:count], refs[count:]
    places, packed, refs = refs[0], refs[1], refs[2:]
    wholes, refs = refs[: count - narrow + 1], refs[count - narrow + 1 :]
    all_places, landed, send, recv, local, rows_send, rows_recv, step_send, step_recv = refs[:9]
    loaded, refs = refs[9], refs[10:]
    wide, low = refs[:count], refs[count:]
    ride = OwnRide(steps)
    ride.take(wholes[0], (step_send, step_recv))
    loads = [
        pltpu.make_async_copy(source, held, loaded.at[index])
        for index, (source, held) in enumerate(zip(inputs, wide))
    ]
    for load in loads:
        load.start()
    me_y, me_x = lax.axis_index("y"), lax.axis_index("x")
    me_z, me_c = lax.axis_index("z"), lax.axis_index("c")
    rank = me_y * 2 + me_x
    rows = low[0].shape[0]
    at = pl.ds(pl.multiple_of(me_z * (4 * rows) + rank * rows, rows), rows)
    peers = ((("x",), me_y * 2 + 1 - me_x), (("y",), (1 - me_y) * 2 + me_x))
    peers += ((("y", "x"), (1 - me_y) * 2 + 1 - me_x),)

    def piece(index, owner):
        width = low[index].shape[1] // 4
        return low[index].at[:, pl.ds(pl.multiple_of(owner * width, width), width)]

    def fill(index):
        loads[index].wait()
        size = 512

        @pl.loop(0, low[index].shape[1] // size)
        def _(step):
            here = pl.ds(pl.multiple_of(step * size, size), size)
            if turned[index]:
                low[index][:, here] = wide[index][here, :].T.astype(BF16)
            else:
                low[index][:, here] = wide[index][:, here].astype(BF16)

        keeps[index].start()

    def target(index):
        width = low[index].shape[1] // 4
        if index < narrow:
            return wholes[0].at[at, pl.ds(index * width, width)]
        return wholes[index - narrow + 1].at[at]

    devices = packed.shape[0]
    me = (me_z * 4 + rank) * 2 + me_c
    keeps = [
        pltpu.make_async_copy(piece(index, rank), target(index), local.at[index])
        for index in range(count)
    ]
    keeps.append(pltpu.make_async_copy(places, all_places.at[rank], local.at[count]))
    keeps.append(pltpu.make_async_copy(packed.at[me], landed.at[me], local.at[count + 1]))
    for keep in keeps[count:]:
        keep.start()

    def device(shift):
        other = lax.rem(me + shift, devices)
        chip = other // 2
        return {"z": chip // 4, "y": lax.rem(chip // 2, 2), "x": lax.rem(chip, 2), "c": lax.rem(other, 2)}

    barrier = pltpu.get_barrier_semaphore()

    @pl.loop(1, devices)
    def _(shift):
        pl.semaphore_signal(barrier, inc=1, device_id=device(shift), device_id_type=MESH)

    for index in range(narrow):
        fill(index)
    pl.semaphore_wait(barrier, devices - 1)
    copies = {}

    def share(index, source_of, goal):
        for number, (axes, owner) in enumerate(peers):
            slot = 3 * index + number
            copies[index, number] = push(axes, source_of(owner), goal, send.at[slot], recv.at[slot])

    def arrive(index):
        keeps[index].wait()
        for number in range(3):
            copies[index, number].wait_recv()

    for index in range(narrow):
        share(index, functools.partial(piece, index), target(index))
    share(count, lambda owner: places, all_places.at[rank])

    @pl.loop(1, devices)
    def _(shift):
        other = lax.rem(me + shift, devices)
        pltpu.make_async_remote_copy(
            src_ref=packed.at[other],
            dst_ref=landed.at[me],
            send_sem=rows_send,
            recv_sem=rows_recv,
            device_id=device(shift),
            device_id_type=MESH,
        ).start()

    for index in range(narrow, count):
        fill(index)
    for index in range(narrow):
        arrive(index)
    ride.begin()
    for index in range(narrow, count):
        share(index, functools.partial(piece, index), target(index))
    most = pl.ds(0, devices - 1)
    pltpu.make_async_copy(packed.at[most], landed.at[most], rows_recv).wait()
    ride.advance()
    for index in range(narrow, count + 1):
        arrive(index)
    keeps[count + 1].wait()
    ride.finish()
    for copy in copies.values():
        copy.wait_send()
    pltpu.make_async_copy(packed.at[most], packed.at[most], rows_send).wait()


def dispatch(weights, turned, narrow, places, packed, steps, name):
    flat = [w.shape[::-1] if flip_it else w.shape for w, flip_it in zip(weights, turned)]
    rows = flat[0][0]
    total = lax.axis_size("z")
    anywhere = pl.BlockSpec(memory_space=pltpu.HBM)
    count = len(weights)
    widths = [sum(shape[1] // 4 for shape in flat[:narrow])]
    widths += [shape[1] // 4 for shape in flat[narrow:]]
    shapes = [jax.ShapeDtypeStruct((total * 4 * rows, width), BF16) for width in widths]
    shapes.append(jax.ShapeDtypeStruct((4, *places.shape), places.dtype))
    shapes.append(jax.ShapeDtypeStruct(packed.shape, packed.dtype))
    return pl.pallas_call(
        functools.partial(dispatch_kernel, tuple(turned), narrow, steps),
        in_specs=[anywhere] * (count + 2),
        out_specs=[anywhere] * len(shapes),
        out_shape=shapes,
        scratch_shapes=[
            pltpu.SemaphoreType.DMA((3 * count + 3,)),
            pltpu.SemaphoreType.DMA((3 * count + 3,)),
            pltpu.SemaphoreType.DMA((count + 2,)),
            pltpu.SemaphoreType.DMA(()),
            pltpu.SemaphoreType.DMA(()),
            pltpu.SemaphoreType.DMA((2 * steps,)),
            pltpu.SemaphoreType.DMA((2 * steps,)),
            pltpu.SemaphoreType.DMA((count,)),
        ]
        + [pltpu.VMEM(weight.shape, F32) for weight in weights]
        + [pltpu.VMEM(shape, BF16) for shape in flat],
        compiler_params=pltpu.CompilerParams(
            collective_id=IDS.index(name), has_side_effects=True, vmem_limit_bytes=VMEM_BYTES
        ),
        cost_estimate=pl.CostEstimate(flops=0, bytes_accessed=120 << 20, transcendentals=0),
        name=name,
    )(*weights, places, packed)


def gather_stages(own, out, send, recv, local, ride):
    rows = own.shape[0]
    half = rows // 2

    def part(core, y, x, side):
        start = block_at(core, y, x) * rows + side * half
        return out.at[pl.ds(pl.multiple_of(start, half), half)]

    def over(axis, source, target, slot):
        return push((axis,), source, target, send.at[slot], recv.at[slot])

    def across(y, x, side, slot):
        here = part(0, y, x, side)
        return over("c", here, here, slot)

    whole = out.at[pl.ds(pl.multiple_of(block_at(0, 0, 0) * rows, rows), rows)]
    keep = pltpu.make_async_copy(own, whole, local)
    keep.start()
    greet((("x",), ("y",), ("c",)), ride.steps > 0)
    first, second = own.at[pl.ds(0, half)], own.at[pl.ds(half, half)]
    x_first = over("x", first, part(0, 0, 0, 0), 0)
    y_second = over("y", second, part(0, 0, 0, 1), 1)
    x_second = over("x", second, part(0, 0, 0, 1), 2)
    y_first = over("y", first, part(0, 0, 0, 0), 3)
    ride.begin()
    crossed = [over("c", own, whole, 4)]
    yield
    x_first.wait_recv()
    far_first = over("y", part(0, 0, 1, 0), part(0, 0, 1, 0), 5)
    crossed.append(across(0, 1, 0, 6))
    y_second.wait_recv()
    far_second = over("x", part(0, 1, 0, 1), part(0, 1, 0, 1), 7)
    crossed.append(across(1, 0, 1, 8))
    yield
    x_second.wait_recv()
    crossed.append(across(0, 1, 1, 9))
    y_first.wait_recv()
    crossed.append(across(1, 0, 0, 10))
    ride.advance()
    yield
    far_first.wait_recv()
    crossed.append(across(1, 1, 0, 11))
    far_second.wait_recv()
    crossed.append(across(1, 1, 1, 12))
    for copy in crossed:
        copy.wait_recv()
    keep.wait()
    ride.advance()
    yield
    ride.finish()
    for copy in crossed + [x_first, y_second, x_second, y_first, far_first, far_second]:
        copy.wait_send()
    yield


def gather_body(inputs, outputs, scratch, ride):
    for _ in gather_stages(inputs[0], outputs[0], *scratch, ride):
        pass


def gather_turns_body(inputs, outputs, scratch, ride):
    own, table_ref, places_ref = inputs
    out, cos_ref, sin_ref = outputs
    stages = gather_stages(own, out, *scratch, ride)
    next(stages)
    size, width = table_ref.shape[0], 2 * HEAD_DIM
    count, _, block = places_ref.shape
    for index in range(count):
        at = pl.ds(index * block, block)
        entry = lax.broadcasted_iota(jnp.int32, (size, block), 0)
        pick = (entry == places_ref[index]).astype(F32).astype(BF16)
        rows = outer_sum(pick, table_ref[:, :width])
        rows += outer_sum(pick, table_ref[:, width : 2 * width])
        rows += outer_sum(pick, table_ref[:, 2 * width :])
        cos_ref[at, :] = rows[:, :HEAD_DIM]
        sin_ref[at, :] = rows[:, HEAD_DIM:]

    for _ in stages:
        pass


def rotation_table(size):
    half_dim = HEAD_DIM // 2
    frequency = jnp.exp(-jnp.arange(half_dim, dtype=F32) * (2.0 * math.log(10000.0) / HEAD_DIM))
    angles = jnp.arange(size, dtype=jnp.int32).astype(F32)[:, None] * frequency[None, :]
    cos_half, sin_half = jnp.cos(angles), jnp.sin(angles)
    rest = jnp.concatenate([cos_half, cos_half, -sin_half, sin_half], axis=1)
    terms = []
    for _ in range(3):
        term = lax.reduce_precision(rest, 8, 7)
        terms.append(term.astype(BF16))
        rest = rest - term
    return jnp.concatenate(terms, axis=1)


def plane_gather_turns(rows, table, places, name, ride):
    anywhere = pl.BlockSpec(memory_space=pltpu.HBM)
    near = pl.BlockSpec(memory_space=pltpu.VMEM)
    total = 8 * rows.shape[0]
    got = communicate(
        gather_turns_body,
        [rows, table, places],
        [anywhere, near, near],
        [jax.ShapeDtypeStruct((total, rows.shape[1]), rows.dtype)]
        + [jax.ShapeDtypeStruct((total, HEAD_DIM), F32)] * 2,
        [anywhere, near, near],
        [
            pltpu.SemaphoreType.DMA((13,)),
            pltpu.SemaphoreType.DMA((13,)),
            pltpu.SemaphoreType.DMA(()),
        ],
        name,
        ride,
    )
    return got[:3], got[3:]


def outer_tiles(sources, targets, tiles, stage, loads, stores, between=lambda: None):
    count = tiles[0].shape[0]
    tile = tiles[0].shape[2]
    total = sources[0][0].shape[1] // tile

    def fetch(index, slot):
        at = pl.ds(pl.multiple_of(index * tile, tile), tile)
        return [
            pltpu.make_async_copy(source.at[:, at], held.at[slot], loads.at[number, slot])
            for number, ((source, _), held) in enumerate(zip(sources, tiles))
        ]

    def keep(index, slot):
        at = pl.ds(pl.multiple_of(index * tile, tile), tile)
        return [
            pltpu.make_async_copy(
                stage.at[slot, :, pl.ds(start, size)], target.at[at], stores.at[number, slot]
            )
            for number, (target, start, size) in enumerate(targets)
        ]

    for copy in fetch(0, 0):
        copy.start()

    def multiply(index):
        slot = lax.rem(index, count)

        @pl.when(index + 1 < total)
        def _():
            for copy in fetch(index + 1, lax.rem(index + 1, count)):
                copy.start()

        @pl.when(index >= count)
        def _():
            for copy in keep(index - count, slot):
                copy.wait()

        for copy in fetch(index, slot):
            copy.wait()
        for (_, parts), held in zip(sources, tiles):
            left = held[slot]
            for start, size, right in parts:
                stage[slot, :, pl.ds(start, size)] = outer_sum(left, right()).astype(BF16)
        for copy in keep(index, slot):
            copy.start()

    pl.loop(0, total // 2)(multiply)
    between()
    pl.loop(total // 2, total)(multiply)
    for index in range(max(total - count, 0), total):
        for copy in keep(index, index % count):
            copy.wait()


def outer_scratch(rows, sources, columns, targets, tile=256):
    return [pltpu.VMEM((2, rows, tile), BF16)] * sources + [
        pltpu.VMEM((2, tile, columns), BF16),
        pltpu.SemaphoreType.DMA((sources, 2)),
        pltpu.SemaphoreType.DMA((targets, 2)),
    ]


def gather_hidden_body(inputs, outputs, scratch, ride):
    own, seen_ref, gate_ref, up_ref = inputs
    out, hidden_ref, by_gate_ref, by_up_ref, weight_ref = outputs
    seen, gate_w, up_w, hidden, by_gate, by_up, loads, stores, *outer = scratch[3:]
    blocks, block = seen.shape[0], seen.shape[1]
    width = gate_w.shape[1]
    tile = 512
    fetch = [
        pltpu.make_async_copy(gate_ref, gate_w, loads.at[0]),
        pltpu.make_async_copy(up_ref, up_w, loads.at[1]),
    ]
    for index in range(blocks):
        at = pl.ds(index * block, block)
        fetch.append(pltpu.make_async_copy(seen_ref.at[at], seen.at[index], loads.at[2 + index]))
    for index in (0, 2, 1, *range(3, len(fetch))):
        fetch[index].start()
    stages = gather_stages(own, out, *scratch[:3], ride)
    next(stages)
    fetch[0].wait()
    fetch[1].wait()
    kept = []
    for index in range(blocks):
        fetch[2 + index].wait()

        @pl.loop(0, width // tile)
        def _(step):
            at = pl.ds(pl.multiple_of(step * tile, tile), tile)
            here = seen[index]
            gate = project(here, gate_w[:, at])
            up = project(here, up_w[:, at])
            turned = 1.0 / (1.0 + jnp.exp(-gate))
            silu = gate * turned
            hidden[pl.ds(index * block, block), at] = (silu * up).astype(BF16)
            by_up[pl.ds(index * block, block), at] = silu.astype(BF16)
            by_gate[pl.ds(index * block, block), at] = (up * (turned * (1.0 + gate * (1.0 - turned)))).astype(BF16)

        rows_at = pl.ds(index * block, block)
        pairs = ((hidden, hidden_ref), (by_gate, by_gate_ref), (by_up, by_up_ref))
        for number, (held, target) in enumerate(pairs):
            copy = pltpu.make_async_copy(
                held.at[rows_at], target.at[rows_at], stores.at[number, index]
            )
            copy.start()
            kept.append(copy)
        if index in (3, 6):
            next(stages)
    next(stages)
    outer_tiles(
        [(out, [(0, width, lambda: hidden[...])])],
        [(weight_ref, 0, width)],
        outer[:1],
        *outer[1:],
    )
    next(stages)
    for copy in kept:
        copy.wait()


def plane_gather_hidden(rows, seen, gate_w, up_w, name, ride=None):
    total, depth = seen.shape
    width = gate_w.shape[1]
    block = rows.shape[0]
    blocks = total // block
    anywhere = pl.BlockSpec(memory_space=pltpu.HBM)
    got = communicate(
        gather_hidden_body,
        [rows, seen, gate_w, up_w],
        [anywhere] * 4,
        [jax.ShapeDtypeStruct((8 * rows.shape[0], rows.shape[1]), rows.dtype)]
        + [jax.ShapeDtypeStruct((total, width), BF16)] * 3
        + [jax.ShapeDtypeStruct((rows.shape[1], width), BF16)],
        [anywhere] * 5,
        [
            pltpu.SemaphoreType.DMA((13,)),
            pltpu.SemaphoreType.DMA((13,)),
            pltpu.SemaphoreType.DMA(()),
            pltpu.VMEM((blocks, block, depth), BF16),
            pltpu.VMEM((depth, width), BF16),
            pltpu.VMEM((depth, width), BF16),
            pltpu.VMEM((total, width), BF16),
            pltpu.VMEM((total, width), BF16),
            pltpu.VMEM((total, width), BF16),
            pltpu.SemaphoreType.DMA((2 + blocks,)),
            pltpu.SemaphoreType.DMA((3, blocks)),
        ]
        + outer_scratch(total, 1, width, 1),
        name,
        ride,
        flops=6 * total * depth * width,
    )
    return got[:5], got[5:]


def plane_gather(rows, name, ride=None):
    got = communicate(
        gather_body,
        [rows],
        [pl.BlockSpec(memory_space=pltpu.HBM)],
        [jax.ShapeDtypeStruct((8 * rows.shape[0], rows.shape[1]), rows.dtype)],
        [pl.BlockSpec(memory_space=pltpu.HBM)],
        [
            pltpu.SemaphoreType.DMA((13,)),
            pltpu.SemaphoreType.DMA((13,)),
            pltpu.SemaphoreType.DMA(()),
        ],
        name,
        ride,
    )
    return got[0], got[1:]


def product_body(make, starts, inputs, outputs, scratch, ride):
    out_ref = outputs[0]
    left, weight, away, got, near, by_y, by_x, end_y, end_x, send, recv, local = scratch[:12]
    block, width = out_ref.shape
    half = block // 2
    tile = 1024
    pairs = [(inputs[2 * i], inputs[2 * i + 1], start) for i, start in enumerate(starts)]

    def over(axis, source, target, slot):
        return push((axis,), source, target, send.at[slot], recv.at[slot])

    waits = {"weight": []}
    column = 0
    for index, (rows_ref, weight_ref, start) in enumerate(pairs):
        inner = weight_ref.shape[1] if make else rows_ref.shape[1]
        copy = pltpu.make_async_copy(
            weight_ref.at[:, pl.ds(start, inner)],
            weight.at[:, pl.ds(column, inner)],
            local.at[index, 8],
        )
        copy.start()
        waits["weight"].append(copy)
        column += inner
    order = ((1, 1, 1), (1, 1, 0), (0, 1, 1), (1, 0, 1), (0, 1, 0), (1, 0, 0), (0, 0, 1), (0, 0, 0))
    places = [pl.ds(pl.multiple_of(block_at(*key) * block, block), block) for key in order]
    if make:
        fill, follow = make(inputs, outputs, scratch[12:], left, places)
    else:
        for slot, key in enumerate(order):
            waits[key] = []
            column = 0
            for index, (rows_ref, _, _) in enumerate(pairs):
                inner = rows_ref.shape[1]
                copy = pltpu.make_async_copy(
                    rows_ref.at[places[slot]],
                    left.at[places[slot], pl.ds(column, inner)],
                    local.at[index, slot],
                )
                copy.start()
                waits[key].append(copy)
                column += inner
    greet((("x",), ("y",), ("c",)), ride.steps > 0)
    ride.begin()
    for copy in waits["weight"]:
        copy.wait()

    def multiply(key, store):
        slot = order.index(key)
        if make:
            fill(slot)
        else:
            for copy in waits[key]:
                copy.wait()
        here = left[places[slot], :]
        for start in range(0, width, tile):
            at = pl.ds(start, tile)
            store(at, project_t(here, weight[at, :]))

    crossing = {}

    def compute_far(y, x):
        index = 2 * y + x

        def store(at, value):
            away[index, :, at] = value.astype(BF16)

        multiply((1, y, x), store)
        crossing[index] = over("c", away.at[index], got.at[index], index)

    def compute_near(y, x):
        index = 2 * y + x
        crossing[index].wait_recv()

        def store(at, value):
            near[index, :, at] = (value + got[index, :, at].astype(F32)).astype(BF16)

        multiply((0, y, x), store)

    lower, upper = pl.ds(0, half), pl.ds(half, half)
    compute_far(1, 1)
    compute_far(1, 0)
    compute_near(1, 1)
    y_far = over("y", near.at[3, lower], by_y.at[1], 4)
    x_far = over("x", near.at[3, upper], by_x.at[1], 5)
    compute_far(0, 1)
    compute_near(1, 0)
    y_near = over("y", near.at[2, lower], by_y.at[0], 6)
    if make:
        ride.advance()
    compute_far(0, 0)
    compute_near(0, 1)
    x_near = over("x", near.at[1, upper], by_x.at[0], 7)
    y_far.wait_recv()
    near[1, lower, :] = (near[1, lower, :].astype(F32) + by_y[1].astype(F32)).astype(BF16)
    x_last = over("x", near.at[1, lower], end_x, 8)
    x_far.wait_recv()
    near[2, upper, :] = (near[2, upper, :].astype(F32) + by_x[1].astype(F32)).astype(BF16)
    y_last = over("y", near.at[2, upper], end_y, 9)
    if not make:
        ride.advance()
    compute_near(0, 0)
    if make:
        follow(ride.advance)
    y_near.wait_recv()
    out_ref[lower, :] = near[0, lower, :].astype(F32) + by_y[0].astype(F32)
    x_near.wait_recv()
    out_ref[upper, :] = near[0, upper, :].astype(F32) + by_x[0].astype(F32)
    x_last.wait_recv()
    out_ref[lower, :] += end_x[...].astype(F32)
    y_last.wait_recv()
    out_ref[upper, :] += end_y[...].astype(F32)
    ride.finish()
    for copy in list(crossing.values()) + [y_far, x_far, y_near, x_near, x_last, y_last]:
        copy.wait_send()


def product_scratch(total, inner, width, pairs):
    block = total // 8
    half = block // 2
    return [
        pltpu.VMEM((total, inner), BF16),
        pltpu.VMEM((width, inner), BF16),
        pltpu.VMEM((4, block, width), BF16),
        pltpu.VMEM((4, block, width), BF16),
        pltpu.VMEM((4, block, width), BF16),
        pltpu.VMEM((2, half, width), BF16),
        pltpu.VMEM((2, half, width), BF16),
        pltpu.VMEM((half, width), BF16),
        pltpu.VMEM((half, width), BF16),
        pltpu.SemaphoreType.DMA((10,)),
        pltpu.SemaphoreType.DMA((10,)),
        pltpu.SemaphoreType.DMA((pairs, 9)),
    ]


def hidden_back(inputs, outputs, scratch, left, places):
    by_gate_ref, gate_w, by_up_ref, up_w, grad_ref, down_ref, seen_ref = inputs
    weight_gate, weight_up = outputs[1:]
    down, rows, factors, down_load, row_loads, *outer = scratch
    width = down.shape[1]
    tile = 1024
    fetch_down = pltpu.make_async_copy(down_ref, down, down_load)
    fetch_down.start()

    def fetch(slot):
        at, held = places[slot], slot % 2
        return [
            pltpu.make_async_copy(grad_ref.at[at], rows.at[held], row_loads.at[0, held]),
            pltpu.make_async_copy(by_gate_ref.at[at], factors.at[held, 0], row_loads.at[1, held]),
            pltpu.make_async_copy(by_up_ref.at[at], factors.at[held, 1], row_loads.at[2, held]),
        ]

    for copy in fetch(0):
        copy.start()

    def fill(slot):
        if slot == 0:
            fetch_down.wait()
        for copy in fetch(slot):
            copy.wait()
        if slot + 1 < len(places):
            for copy in fetch(slot + 1):
                copy.start()
        held = slot % 2

        for start in range(0, width, tile):
            at, beside = pl.ds(start, tile), pl.ds(width + start, tile)
            grad = project(rows[held], down[:, at])
            left[places[slot], at] = (grad * factors[held, 0, :, at].astype(F32)).astype(BF16)
            left[places[slot], beside] = (grad * factors[held, 1, :, at].astype(F32)).astype(BF16)

    def follow(between):
        outer_tiles(
            [
                (
                    seen_ref,
                    [
                        (0, width, lambda: left[:, pl.ds(0, width)]),
                        (width, width, lambda: left[:, pl.ds(width, width)]),
                    ],
                )
            ],
            [(weight_gate, 0, width), (weight_up, width, width)],
            outer[:1],
            *outer[1:],
            between,
        )

    return fill, follow


def plane_product_back(grads, down, by_gate, by_up, gate_w, up_w, seen, name, ride):
    total, depth = grads.shape
    width = gate_w.shape[1]
    block = total // 8
    operands = [by_gate, gate_w, by_up, up_w, grads, down, seen]
    anywhere = pl.BlockSpec(memory_space=pltpu.HBM)
    got = communicate(
        functools.partial(product_body, hidden_back, [0, 0]),
        operands,
        [anywhere] * len(operands),
        [jax.ShapeDtypeStruct((block, depth), F32)]
        + [jax.ShapeDtypeStruct((depth, width), BF16)] * 2,
        [pl.BlockSpec(memory_space=pltpu.VMEM), anywhere, anywhere],
        product_scratch(total, 2 * width, depth, 2)
        + [
            pltpu.VMEM((depth, width), BF16),
            pltpu.VMEM((2, block, depth), BF16),
            pltpu.VMEM((2, 2, block, width), BF16),
            pltpu.SemaphoreType.DMA(()),
            pltpu.SemaphoreType.DMA((3, 2)),
        ]
        + outer_scratch(total, 1, 2 * width, 2),
        name,
        ride,
        flops=10 * total * depth * width,
    )
    return got[:3], got[3:]


def plane_product(pairs, name, ride=None):
    total = pairs[0][0].shape[0]
    inner = sum(rows.shape[1] for rows, _, _ in pairs)
    width = pairs[0][1].shape[0]
    operands = []
    for rows, weight, _ in pairs:
        operands += [rows, weight]
    got = communicate(
        functools.partial(product_body, None, [start for _, _, start in pairs]),
        operands,
        [pl.BlockSpec(memory_space=pltpu.HBM)] * len(operands),
        [jax.ShapeDtypeStruct((total // 8, width), F32)],
        [pl.BlockSpec(memory_space=pltpu.VMEM)],
        product_scratch(total, inner, width, len(pairs)),
        name,
        ride,
        flops=2 * total * inner * width,
    )
    return got[0], got[1:]


def ring_next(values):
    total = lax.axis_size("z")
    return lax.ppermute(values, "z", [(i, (i + 1) % total) for i in range(total)])


def ring_rows(whole, owner):
    rows = whole.shape[0] // lax.axis_size("z")
    return lax.dynamic_slice(whole, (owner * rows, 0), (rows, whole.shape[1]))


class Gathered:
    def __init__(self, whole, step=0):
        self.whole, self.step = whole, step

    def ride(self, count):
        count = min(count, lax.axis_size("z") - 1 - self.step)
        item = (self.whole, self.step, count)
        self.step += count
        return item

    def land(self, whole):
        self.whole = whole

    def walk(self, count):
        total = lax.axis_size("z")
        rows = self.whole.shape[0] // total
        last = min(self.step + count, total - 1)
        current = ring_rows(self.whole, owner_at(self.step)) if self.step < last else None
        while self.step < last:
            self.step += 1
            current = ring_next(current)
            self.whole = lax.dynamic_update_slice(self.whole, current, (owner_at(self.step) * rows, 0))

    def finish(self):
        self.walk(lax.axis_size("z"))
        return self.whole


class Summed:
    def __init__(self, whole):
        self.whole, self.step, self.running = whole, 0, None

    def ride(self, count):
        count = min(count, lax.axis_size("z") - 1 - self.step)
        item = (self.running, self.whole, self.step, count)
        self.step += count
        return item

    def land(self, running):
        self.running = running

    def walk(self, count):
        total = lax.axis_size("z")
        for _ in range(min(count, total - 1 - self.step)):
            running = ring_rows(self.whole, owner_at(1)) if self.running is None else self.running
            own = ring_rows(self.whole, owner_at((self.step + 2) % total))
            self.running = (ring_next(running).astype(F32) + own.astype(F32)).astype(BF16)
            self.step += 1

    def finish(self):
        self.walk(lax.axis_size("z"))
        return self.running


def from_plane(block):
    rows = block.shape[0] // 4
    me_y, me_x = lax.axis_index("y"), lax.axis_index("x")

    def piece(y, x):
        return lax.dynamic_slice(block, ((y * 2 + x) * rows, 0), (rows, block.shape[1]))

    own = piece(me_y, me_x)
    by_x = lax.ppermute(piece(me_y, 1 - me_x), "x", ((0, 1), (1, 0)))
    by_y = lax.ppermute(piece(1 - me_y, me_x), "y", ((0, 1), (1, 0)))
    far = lax.ppermute(piece(1 - me_y, 1 - me_x), ("y", "x"), ((0, 3), (1, 2), (2, 1), (3, 0)))

    def chosen(y, x):
        same_y, same_x = me_y == y, me_x == x
        return jnp.where(
            same_y, jnp.where(same_x, own, by_x), jnp.where(same_x, by_y, far)
        )

    return [chosen(y, x) for y in range(2) for x in range(2)]


def side_by_side(pieces, start=0, stop=None):
    return jnp.concatenate([piece[:, start:stop].astype(F32) for piece in pieces], axis=1)


def turn(values, cos_rows, sin_rows):
    return values * cos_rows + pltpu.roll(values, HEAD_DIM // 2, 1) * sin_rows


def visible_of(follow):
    size = follow.shape[1]
    row = lax.broadcasted_iota(jnp.int32, (size, size), 0)
    column = lax.broadcasted_iota(jnp.int32, (size, size), 1)
    return (column <= row) & (row - column <= follow)


def soft_of(queries, keys, visible):
    scores = project_t(queries, keys) * (1.0 / math.sqrt(HEAD_DIM))
    scores = jnp.where(visible, scores, NEG_LARGE)
    weights = jnp.exp(scores - jnp.max(scores, axis=1, keepdims=True))
    return weights / jnp.sum(weights, axis=1, keepdims=True)


def attend_body(inputs, outputs):
    seen_ref, weight_ref, cos_ref, sin_ref, follow_ref = inputs
    low_ref, out_ref = outputs
    width = out_ref.shape[1]
    cos_rows, sin_rows = cos_ref[...], sin_ref[...]
    visible = visible_of(follow_ref[0])
    lin = project(seen_ref[...], weight_ref[...])
    for start in range(0, width, HEAD_DIM):
        here = slice(start, start + HEAD_DIM)
        key_at = slice(width + start, width + start + HEAD_DIM)
        value_at = slice(2 * width + start, 2 * width + start + HEAD_DIM)
        queries = turn(lin[:, here], cos_rows, sin_rows).astype(BF16)
        keys = turn(lin[:, key_at], cos_rows, sin_rows).astype(BF16)
        values = lin[:, value_at].astype(BF16)
        low_ref[:, here] = queries
        low_ref[:, key_at] = keys
        low_ref[:, value_at] = values
        soft = soft_of(queries, keys, visible).astype(BF16)
        out_ref[:, here] = project(soft, values).astype(BF16)


def attend_back_body(blocks, inputs, outputs, grads_held):
    low_ref, seen_ref, weight_ref, cos_ref, sin_ref, follow_ref = inputs[:6]
    seen_tile, grad_tile, attended_ref = inputs[6:]
    out_ref, outer_ref = outputs
    step = pl.program_id(0)
    block = out_ref.shape[0]

    @pl.when(step < blocks)
    def _():
        attend_back_block(inputs[:6], out_ref)
        grads_held[pl.ds(pl.multiple_of(step * block, block), block), :] = out_ref[...]

    @pl.when(step >= blocks)
    def _():
        width = out_ref.shape[1]
        outer_ref[:, :width] = outer_sum(seen_tile[...], grads_held[...]).astype(BF16)
        outer_ref[:, width:] = outer_sum(grad_tile[...], attended_ref[...]).astype(BF16)


def attend_back_block(inputs, out_ref):
    low_ref, seen_ref, weight_ref, cos_ref, sin_ref, follow_ref = inputs
    width = weight_ref.shape[1]
    cos_rows, sin_rows = cos_ref[...], -sin_ref[...]
    visible = visible_of(follow_ref[0])
    scale = 1.0 / math.sqrt(HEAD_DIM)
    grad_all = project(seen_ref[...], weight_ref[...]).astype(BF16)
    for start in range(0, width, HEAD_DIM):
        here = slice(start, start + HEAD_DIM)
        key_at = slice(width + start, width + start + HEAD_DIM)
        value_at = slice(2 * width + start, 2 * width + start + HEAD_DIM)
        queries, keys, values = low_ref[:, here], low_ref[:, key_at], low_ref[:, value_at]
        grad = grad_all[:, here]
        soft = soft_of(queries, keys, visible)
        grad_soft = project_t(grad, values)
        inner = jnp.sum(soft * grad_soft, axis=1, keepdims=True)
        grad_scores = (soft * (grad_soft - inner)).astype(BF16)
        grad_query = project(grad_scores, keys) * scale
        grad_key = outer_sum(grad_scores, queries) * scale
        out_ref[:, here] = turn(grad_query, cos_rows, sin_rows).astype(BF16)
        out_ref[:, key_at] = turn(grad_key, cos_rows, sin_rows).astype(BF16)
        out_ref[:, value_at] = outer_sum(soft.astype(BF16), grad).astype(BF16)


def plane_peers():
    me_y, me_x = lax.axis_index("y"), lax.axis_index("x")
    return (
        (("x",), me_y * 2 + 1 - me_x),
        (("y",), (1 - me_y) * 2 + me_x),
        (("y", "x"), (1 - me_y) * 2 + 1 - me_x),
    )


def collect_copies(blocks, outs, send, recv, local):
    rank = lax.axis_index("y") * 2 + lax.axis_index("x")
    keeps, copies = [], []
    for index, (block, out) in enumerate(zip(blocks, outs)):
        rows = block.shape[0] // 4

        def piece(owner, block=block, rows=rows):
            return block.at[pl.ds(pl.multiple_of(owner * rows, rows), rows)]

        keeps.append(pltpu.make_async_copy(piece(rank), out.at[rank], local.at[index]))
        for number, (axes, owner) in enumerate(plane_peers()):
            copies.append(
                pltpu.make_async_remote_copy(
                    src_ref=piece(owner),
                    dst_ref=out.at[rank],
                    send_sem=send.at[3 * index + number],
                    recv_sem=recv.at[3 * index + number],
                    device_id=flip(*axes),
                    device_id_type=MESH,
                )
            )
    return keeps, copies


def collected_shape(block):
    return jax.ShapeDtypeStruct((4, block.shape[0] // 4, block.shape[1]), block.dtype)


def by_blocks(
    body, operands, specs, shapes, out_specs, blocks, name, ride, flops, collect=(), own_scratch=(), advances=()
):
    extra = len(collect)
    operands, shapes = list(operands) + list(collect), list(shapes)
    shapes += [collected_shape(block) for block in collect]
    anywhere = pl.BlockSpec(memory_space=pltpu.HBM)
    specs, out_specs = list(specs) + [anywhere] * extra, list(out_specs) + [anywhere] * extra
    scratch = list(own_scratch)
    if extra:
        scratch += [
            pltpu.SemaphoreType.DMA((3 * extra,)),
            pltpu.SemaphoreType.DMA((3 * extra,)),
            pltpu.SemaphoreType.DMA((extra,)),
        ]
    count_in, count_out = len(operands), len(shapes)
    all_in = count_in + len(ride.operands)
    all_out = count_out + len(ride.shapes)

    def kernel(*refs):
        inputs, outputs, held = refs[:all_in], refs[all_in : all_in + all_out], refs[all_in + all_out :]
        step = pl.program_id(0)
        ride.board(inputs[count_in:], outputs[count_out:], held[len(scratch) :])
        keeps, copies = [], []
        if extra:
            keeps, copies = collect_copies(
                inputs[count_in - extra : count_in], outputs[count_out - extra : count_out], *held[len(scratch) - 3 : len(scratch)]
            )
        if ride.copies or extra:

            @pl.when(step == 0)
            def _():
                greet([axes for axes, _ in plane_peers()] if extra else (), bool(ride.copies))
                ride.begin()
                for copy in keeps + copies:
                    copy.start()

        body(inputs[: count_in - extra], outputs[: count_out - extra], *held[: len(own_scratch)])
        for number in advances:
            pl.when(step == number)(ride.advance)
        if ride.copies or extra:

            @pl.when(step == blocks - 1)
            def _():
                for copy in keeps:
                    copy.wait()
                for copy in copies:
                    copy.wait()
                ride.finish()

    params = {"collective_id": IDS.index(name), "has_side_effects": True} if ride.steps or extra else {}
    got = pl.pallas_call(
        kernel,
        grid=(blocks,),
        in_specs=list(specs) + [anywhere] * len(ride.operands),
        out_specs=list(out_specs) + [anywhere] * len(ride.shapes),
        out_shape=list(shapes) + ride.shapes,
        scratch_shapes=scratch + ride.scratch,
        input_output_aliases={count_in + k: count_out + v for k, v in ride.aliases.items()},
        compiler_params=pltpu.CompilerParams(vmem_limit_bytes=VMEM_BYTES, **params),
        cost_estimate=pl.CostEstimate(flops=flops, bytes_accessed=40 << 20, transcendentals=0),
        name=name,
    )(*operands, *ride.operands)
    return list(got)


def row_spec(rows, columns):
    return pl.BlockSpec((rows, columns), lambda i: (i, 0))


def attend(seen, weight, cos_rows, sin_rows, places, block, ride):
    rows, depth = seen.shape
    width = weight.shape[1] // 4
    got = by_blocks(
        attend_body,
        [seen, weight, cos_rows, sin_rows, places],
        [
            row_spec(block, depth),
            pl.BlockSpec((depth, 3 * width), lambda i: (0, 0)),
            row_spec(block, HEAD_DIM),
            row_spec(block, HEAD_DIM),
            pl.BlockSpec((1, 1, block), lambda i: (i, 0, 0)),
        ],
        [
            jax.ShapeDtypeStruct((rows, 3 * width), BF16),
            jax.ShapeDtypeStruct((rows, width), BF16),
        ],
        [row_spec(block, 3 * width), row_spec(block, width)],
        rows // block,
        "attend",
        ride,
        4 * rows * block * width + 6 * rows * depth * width,
    )
    return got[:2], got[2:]


def attend_back(low, grad_all, weight, cos_rows, sin_rows, places, seen, attended, block, ride, collect):
    rows, depth = grad_all.shape
    width = weight.shape[1] // 4
    blocks = rows // block
    tile = 256

    def early(columns):
        return pl.BlockSpec((block, columns), lambda i: (jnp.minimum(i, blocks - 1), 0))

    def late(i):
        return jnp.maximum(i - blocks, 0)

    got = by_blocks(
        functools.partial(attend_back_body, blocks),
        [low, grad_all, weight, cos_rows, sin_rows, places, seen, grad_all, attended],
        [
            early(3 * width),
            early(depth),
            pl.BlockSpec((depth, width), lambda i: (0, 3)),
            early(HEAD_DIM),
            early(HEAD_DIM),
            pl.BlockSpec((1, 1, block), lambda i: (jnp.minimum(i, blocks - 1), 0, 0)),
            pl.BlockSpec((rows, tile), lambda i: (0, late(i))),
            pl.BlockSpec((rows, tile), lambda i: (0, late(i))),
            pl.BlockSpec((rows, width), lambda i: (0, 0)),
        ],
        [
            jax.ShapeDtypeStruct((rows, 3 * width), BF16),
            jax.ShapeDtypeStruct((depth, 4 * width), BF16),
        ],
        [early(3 * width), pl.BlockSpec((tile, 4 * width), lambda i: (late(i), 0))],
        blocks + depth // tile,
        "attend_back",
        ride,
        10 * rows * block * width + 10 * rows * depth * width,
        collect,
        [pltpu.VMEM((rows, 3 * width), BF16)],
        (blocks - 2, blocks + depth // tile - 3),
    )
    last = 2 + len(collect)
    return got[:last], got[last:]


def plane_places(segments, block):
    groups, size = segments.shape
    numbers = jnp.arange(SEGS, dtype=jnp.int32)
    starts = jnp.sum((segments[:, :, None] < numbers).astype(jnp.int32), axis=1)
    ends = jnp.sum((segments[:, :, None] <= numbers).astype(jnp.int32), axis=1)
    onehot = segments[:, :, None] == numbers
    row = jnp.arange(size, dtype=jnp.int32)[None, :]
    places = row - jnp.sum(jnp.where(onehot, starts[:, None, :], 0), axis=2)
    follow = jnp.sum(jnp.where(onehot, ends[:, None, :], 0), axis=2) - 1 - row
    return places.reshape(-1, 1, block), follow.reshape(-1, 1, block)


def after(values, *gates):
    return lax.optimization_barrier((values,) + gates)[0]


EVERY = ("z", "y", "x", "c")


def exchange(rows):
    return lax.all_to_all(rows, EVERY, split_axis=0, concat_axis=0, tiled=True)


def on_device(
    tokens_in,
    cotangent,
    segment_ids,
    destination,
    source,
    w_query,
    w_key,
    w_value,
    w_out,
    w_gate,
    w_up,
    w_down,
):
    tok_rows = tokens_in.shape[0]
    devices = lax.axis_size(EVERY)
    per_peer = tok_rows // devices
    row_index = jnp.arange(tok_rows, dtype=jnp.int32)
    peer_to = destination // tok_rows
    ahead_rows = (peer_to[None, :] == peer_to[:, None]) & (
        destination[None, :] < destination[:, None]
    )
    send_slot = peer_to * per_peer + jnp.sum(ahead_rows.astype(jnp.int32), axis=1)
    peer_from = source // tok_rows
    before = (peer_from[None, :] == peer_from[:, None]) & (row_index[None, :] < row_index[:, None])
    recv_slot = peer_from * per_peer + jnp.sum(before.astype(jnp.int32), axis=1)
    send_pick = (send_slot[:, None] == row_index[None, :]).astype(BF16)
    recv_pick = (recv_slot[:, None] == row_index[None, :]).astype(BF16)

    packed = outer_sum(send_pick, tokens_in).astype(BF16)
    table = rotation_table(tok_rows)
    weights = [w_query, w_key, w_value, w_out, w_gate, w_up, w_down]
    attention_whole, gate_whole, up_whole, down_whole, segments, landed = dispatch(
        weights,
        [False, False, False, True, False, False, True],
        4,
        segment_ids.reshape(-1, 128),
        packed.reshape(devices, per_peer, -1),
        2,
        "dispatch",
    )
    arrived = project(recv_pick, landed.reshape(tok_rows, -1))
    attention_w, gate_w = Gathered(attention_whole, 2), Gathered(gate_whole)
    up_w, down_w = Gathered(up_whole), Gathered(down_whole)
    head_width = w_query.shape[1] // 4
    places, follow = plane_places(segments.reshape(4, -1), tok_rows)
    normed_one, scale_one = norm_parts(arrived)
    def send_back(rows):
        return exchange(outer_sum(recv_pick, rows.astype(BF16)).astype(BF16))

    def riding(call, gathers=(), sums=()):
        ride = Ride(
            [weight.ride(count) for weight, count in gathers],
            [gradient.ride(count) for gradient, count in sums],
        )
        result, landed = call(ride)
        for (item, _), value in zip(tuple(gathers) + tuple(sums), landed):
            item.land(value)
        return result

    seen_one, cos_rows, sin_rows = riding(
        lambda ride: plane_gather_turns(
            normed_one.astype(BF16), table, places, "gather_one", ride
        ),
        [(attention_w, 1), (gate_w, 1)],
    )
    attention = attention_w.finish()
    upstream_low = project(
        recv_pick,
        exchange(outer_sum(send_pick, after(cotangent, seen_one)).astype(BF16)),
    ).astype(BF16)
    upstream = upstream_low.astype(F32)
    qkv_low, attended = riding(
        lambda ride: attend(seen_one, attention, cos_rows, sin_rows, follow, tok_rows, ride),
        [(gate_w, 1)],
    )
    middle = arrived + riding(
        lambda ride: plane_product([(attended, attention, 3 * head_width)], "product_out", ride),
        [(gate_w, 1), (up_w, 1)],
    )
    normed_two, scale_two = norm_parts(middle)
    seen_two = riding(
        lambda ride: plane_gather(normed_two.astype(BF16), "gather_two", ride), [(up_w, 2)]
    )
    gate_whole, up_whole = gate_w.finish(), up_w.finish()
    grad_two_all, hidden, by_gate, by_up, weight_down = riding(
        lambda ride: plane_gather_hidden(
            upstream_low, seen_two, gate_whole, up_whole, "gather_up", ride
        ),
        [(down_w, 3)],
    )
    down_whole = down_w.finish()
    summed_down = Summed(weight_down)
    grad_normed_two, weight_gate, weight_up = riding(
        lambda ride: plane_product_back(
            grad_two_all,
            down_whole,
            by_gate,
            by_up,
            gate_whole,
            up_whole,
            seen_two,
            "product_forward",
            ride,
        ),
        (),
        [(summed_down, 3)],
    )
    summed_gate, summed_up = Summed(weight_gate), Summed(weight_up)
    output = middle + riding(
        lambda ride: plane_product(
            [(after(hidden, grad_normed_two), down_whole, 0)], "product_down", ride
        ),
        (),
        [(summed_gate, 2)],
    )
    returned_out = send_back(output)
    grad_middle = upstream + norm_back(normed_two, scale_two, grad_normed_two)
    grad_one_all = riding(
        lambda ride: plane_gather(
            after(grad_middle.astype(BF16), output), "gather_middle", ride
        ),
        (),
        [(summed_gate, 1), (summed_up, 1)],
    )
    grad_qkv, weight_attention, own_down, own_gate = riding(
        lambda ride: attend_back(
            after(qkv_low, returned_out),
            grad_one_all,
            attention,
            cos_rows,
            sin_rows,
            follow,
            seen_one,
            attended,
            tok_rows,
            ride,
            (summed_down.finish(), summed_gate.finish()),
        ),
        (),
        [(summed_up, 2)],
    )
    summed_attention = Summed(weight_attention)
    grad_normed_one = riding(
        lambda ride: plane_product([(grad_qkv, attention, 0)], "product_qkv", ride),
        (),
        [(summed_attention, 2)],
    )
    grad_inputs = grad_middle + norm_back(normed_one, scale_one, grad_normed_one)
    own_up, last_attention = from_plane(summed_up.finish()), summed_attention.finish()
    own_attention = from_plane(last_attention)
    own_down, own_gate, own_up = [
        after(own, last_attention) for own in (own_down, own_gate, jnp.stack(own_up))
    ]

    return (
        project(send_pick, after(returned_out, grad_normed_one)),
        project(send_pick, send_back(grad_inputs)),
        side_by_side(own_attention, 0, head_width),
        side_by_side(own_attention, head_width, 2 * head_width),
        side_by_side(own_attention, 2 * head_width, 3 * head_width),
        side_by_side(own_attention, 3 * head_width).T,
        side_by_side(own_gate),
        side_by_side(own_up),
        side_by_side(own_down).T,
    )


def solution(mesh):
    groups, cores = mesh.shape["dp"], mesh.shape["tensor"]
    whole = Mesh(mesh.devices.reshape(groups // 4, 2, 2, cores), EVERY)
    rows = P(EVERY, None)
    tall = P(("z", "y", "x"), "c")
    wide = P("c", ("z", "y", "x"))
    in_specs = (
        rows,
        rows,
        P(("z", "y", "x")),
        P(EVERY),
        P(EVERY),
        tall,
        tall,
        tall,
        wide,
        tall,
        tall,
        wide,
    )
    out_specs = (rows, rows, tall, tall, tall, wide, tall, tall, wide)
    return jax.shard_map(
        on_device, mesh=whole, in_specs=in_specs, out_specs=out_specs, check_vma=False
    )
```

```python
import functools
import math

import jax
import jax.numpy as jnp
import numpy as np
from jax import lax
from jax.experimental import pallas as pl
from jax.experimental.pallas import tpu as pltpu
from jax.sharding import Mesh
from jax.sharding import PartitionSpec as P

HEAD_DIM = 128
SEGS = 4
EPSILON = 1e-05
NEG_LARGE = -1e30
VMEM_BYTES = 60 << 20
F32 = jnp.float32
BF16 = jnp.bfloat16
MESH = pl.DeviceIdType.MESH
IDS = (
    "dispatch",
    "gather_one",
    "gather_two",
    "gather_middle",
    "product_out",
    "product_forward",
    "product_qkv",
    "product_down",
    "gather_up",
    "attend",
    "attend_back",
)


def project(left, right):
    return jnp.dot(left, right, preferred_element_type=F32)


def project_t(left, right):
    return lax.dot_general(left, right, (((1,), (1,)), ((), ())), preferred_element_type=F32)


def outer_sum(left, right):
    return lax.dot_general(left, right, (((0,), (0,)), ((), ())), preferred_element_type=F32)


def norm_parts(values):
    center = values - jnp.mean(values, axis=-1, keepdims=True)
    spread = jnp.mean(center * center, axis=-1, keepdims=True)
    scale = lax.rsqrt(spread + EPSILON)
    return center * scale, scale


def norm_back(normed, scale, gradient):
    mean_grad = jnp.mean(gradient, axis=-1, keepdims=True)
    mean_both = jnp.mean(gradient * normed, axis=-1, keepdims=True)
    return (gradient - mean_grad - normed * mean_both) * scale


def flip(*axes):
    return {axis: 1 - lax.axis_index(axis) for axis in axes}


def owner_at(step):
    total = lax.axis_size("z")
    return lax.rem(lax.axis_index("z") + total - step, total)


def greet(peers, ring):
    barrier = pltpu.get_barrier_semaphore()
    for axes in peers:
        pl.semaphore_signal(barrier, inc=1, device_id=flip(*axes), device_id_type=MESH)
    count = len(peers)
    if ring:
        pl.semaphore_signal(barrier, inc=1, device_id={"z": owner_at(1)}, device_id_type=MESH)
        count += 1
    pl.semaphore_wait(barrier, count)


def push(axes, source, target, send, recv):
    copy = pltpu.make_async_remote_copy(
        src_ref=source,
        dst_ref=target,
        send_sem=send,
        recv_sem=recv,
        device_id=flip(*axes),
        device_id_type=MESH,
    )
    copy.start()
    return copy


class Ride:
    sides = 2

    def __init__(self, gathers=(), sums=()):
        self.gathers, self.sums = tuple(gathers), tuple(sums)
        self.operands, self.shapes, self.scratch = [], [], []
        self.aliases = {}
        self.steps = 0
        for whole, first, count in self.gathers:
            self.aliases[len(self.operands)] = len(self.shapes)
            self.operands.append(whole)
            self.shapes.append(jax.ShapeDtypeStruct(whole.shape, whole.dtype))
            self.steps += count
        for running, whole, first, count in self.sums:
            self.operands += [whole] if running is None else [running, whole]
            block = (whole.shape[0] // lax.axis_size("z"), whole.shape[1])
            self.shapes.append(jax.ShapeDtypeStruct(block, whole.dtype))
            self.steps += count
            self.scratch += [
                pltpu.VMEM((count, *block), whole.dtype),
                pltpu.VMEM((count, *block), whole.dtype),
                pltpu.SemaphoreType.DMA((count + 1,)),
            ]
        if self.steps:
            self.scratch += [
                pltpu.SemaphoreType.DMA((2 * self.steps,)),
                pltpu.SemaphoreType.DMA((2 * self.steps,)),
            ]

    def board(self, inputs, outputs, scratch):
        inputs, outputs, scratch = list(inputs), list(outputs), list(scratch)
        self.loads, self.copies, self.prepares, self.begun = [], [], [], 0
        self.ends = []
        if not self.steps:
            return
        total = lax.axis_size("z")
        send, recv = scratch[-2], scratch[-1]
        ahead = {"z": owner_at(total - 1)}

        def rows_of(whole, step):
            rows = whole.shape[0] // total
            return whole.at[pl.ds(pl.multiple_of(owner_at(step % total) * rows, rows), rows)]

        def plan(source, target, prepare=None):
            half = source.shape[0] // self.sides
            slot = self.sides * len(self.copies)
            self.copies.append(
                [
                    pltpu.make_async_remote_copy(
                        src_ref=source.at[pl.ds(side * half, half)],
                        dst_ref=target.at[pl.ds(side * half, half)],
                        send_sem=send.at[slot + side],
                        recv_sem=recv.at[slot + side],
                        device_id=ahead,
                        device_id_type=MESH,
                    )
                    for side in range(self.sides)
                ]
            )
            self.prepares.append(prepare)

        def adding(load, landed, own):
            def prepare(side):
                if side == 0:
                    load.wait()
                height = 64
                count = own.shape[0] // (2 * height)

                @pl.loop(side * count, side * count + count)
                def _(index):
                    at = pl.ds(pl.multiple_of(index * height, height), height)
                    own[at, :] = (own[at, :].astype(F32) + landed[at, :].astype(F32)).astype(BF16)

            return prepare

        for _, first, count in self.gathers:
            inputs.pop(0)
            whole = outputs.pop(0)
            for step in range(first, first + count):
                plan(rows_of(whole, step), rows_of(whole, step))
        for running, _, first, count in self.sums:
            source = None if running is None else inputs.pop(0)
            whole, final = inputs.pop(0), outputs.pop(0)
            landed, own, loaded = scratch[:3]
            scratch = scratch[3:]
            if source is None:
                source = rows_of(whole, 1)
            prepare = None
            for k in range(count):
                load = pltpu.make_async_copy(rows_of(whole, first + 2 + k), own.at[k], loaded.at[k])
                self.loads.append(load)
                plan(source, landed.at[k], prepare)
                prepare, source = adding(load, landed.at[k], own.at[k]), own.at[k]
            last = len(self.copies) - 1
            keep = pltpu.make_async_copy(own.at[count - 1], final, loaded.at[count])
            self.ends.append((last, prepare, keep))

    def start(self, number, side):
        if self.prepares[number]:
            self.prepares[number](side)
        self.copies[number][side].start()

    def begin(self):
        for load in self.loads:
            load.start()
        if self.copies:
            for side in range(self.sides):
                self.start(0, side)
            self.begun = 1

    def advance(self):
        if 0 < self.begun < len(self.copies):
            for side in range(self.sides):
                self.copies[self.begun - 1][side].wait_recv()
                self.start(self.begun, side)
            self.begun += 1

    def finish(self):
        while self.begun < len(self.copies):
            self.advance()
        for side in range(self.sides):
            if self.copies:
                self.copies[-1][side].wait_recv()
            for number, prepare, _ in self.ends:
                if side == 0 and number < len(self.copies) - 1:
                    prepare(0)
                    prepare(1)
                elif number == len(self.copies) - 1:
                    prepare(side)
        for _, _, keep in self.ends:
            keep.start()
        for pair in self.copies:
            for copy in pair:
                copy.wait_send()
        for _, _, keep in self.ends:
            keep.wait()


def block_at(core, y, x):
    def moved(axis, offset):
        here = lax.axis_index(axis)
        return 1 - here if offset else here

    return (moved("y", y) * 2 + moved("x", x)) * 2 + moved("c", core)


def communicate(body, operands, specs, shapes, out_specs, scratch, name, ride, flops=0):
    ride = ride or Ride()
    count_in, count_out, count_scratch = len(operands), len(shapes), len(scratch)
    all_in = count_in + len(ride.operands)
    all_out = count_out + len(ride.shapes)

    def kernel(*refs):
        inputs, outputs, held = refs[:all_in], refs[all_in : all_in + all_out], refs[all_in + all_out :]
        ride.board(inputs[count_in:], outputs[count_out:], held[count_scratch:])
        body(inputs[:count_in], outputs[:count_out], held[:count_scratch], ride)

    anywhere = pl.BlockSpec(memory_space=pltpu.HBM)
    got = pl.pallas_call(
        kernel,
        in_specs=list(specs) + [anywhere] * len(ride.operands),
        out_specs=list(out_specs) + [anywhere] * len(ride.shapes),
        out_shape=list(shapes) + ride.shapes,
        scratch_shapes=list(scratch) + ride.scratch,
        input_output_aliases={count_in + k: count_out + v for k, v in ride.aliases.items()},
        compiler_params=pltpu.CompilerParams(
            collective_id=IDS.index(name), has_side_effects=True, vmem_limit_bytes=VMEM_BYTES
        ),
        cost_estimate=pl.CostEstimate(
            flops=flops, bytes_accessed=120 << 20, transcendentals=0
        ),
        name=name,
    )(*operands, *ride.operands)
    return list(got)


class OwnRide(Ride):
    sides = 1

    def __init__(self, count):
        super().__init__()
        self.steps = count

    def take(self, whole, semaphores):
        self.gathers = ((None, 0, self.steps),)
        super().board([None], [whole], semaphores)


def dispatch_kernel(turned, narrow, steps, *refs):
    count = len(turned)
    inputs, refs = refs[:count], refs[count:]
    places, packed, refs = refs[0], refs[1], refs[2:]
    wholes, refs = refs[: count - narrow + 1], refs[count - narrow + 1 :]
    all_places, landed, send, recv, local, rows_send, rows_recv, step_send, step_recv = refs[:9]
    loaded, refs = refs[9], refs[10:]
    wide, low = refs[:count], refs[count:]
    ride = OwnRide(steps)
    ride.take(wholes[0], (step_send, step_recv))
    loads = [
        pltpu.make_async_copy(source, held, loaded.at[index])
        for index, (source, held) in enumerate(zip(inputs, wide))
    ]
    for load in loads:
        load.start()
    me_y, me_x = lax.axis_index("y"), lax.axis_index("x")
    me_z, me_c = lax.axis_index("z"), lax.axis_index("c")
    rank = me_y * 2 + me_x
    rows = low[0].shape[0]
    at = pl.ds(pl.multiple_of(me_z * (4 * rows) + rank * rows, rows), rows)
    peers = ((("x",), me_y * 2 + 1 - me_x), (("y",), (1 - me_y) * 2 + me_x))
    peers += ((("y", "x"), (1 - me_y) * 2 + 1 - me_x),)

    def piece(index, owner):
        width = low[index].shape[1] // 4
        return low[index].at[:, pl.ds(pl.multiple_of(owner * width, width), width)]

    def fill(index):
        loads[index].wait()
        size = 512

        @pl.loop(0, low[index].shape[1] // size)
        def _(step):
            here = pl.ds(pl.multiple_of(step * size, size), size)
            if turned[index]:
                low[index][:, here] = wide[index][here, :].T.astype(BF16)
            else:
                low[index][:, here] = wide[index][:, here].astype(BF16)

        keeps[index].start()

    def target(index):
        width = low[index].shape[1] // 4
        if index < narrow:
            return wholes[0].at[at, pl.ds(index * width, width)]
        return wholes[index - narrow + 1].at[at]

    devices = packed.shape[0]
    me = (me_z * 4 + rank) * 2 + me_c
    keeps = [
        pltpu.make_async_copy(piece(index, rank), target(index), local.at[index])
        for index in range(count)
    ]
    keeps.append(pltpu.make_async_copy(places, all_places.at[rank], local.at[count]))
    keeps.append(pltpu.make_async_copy(packed.at[me], landed.at[me], local.at[count + 1]))
    for keep in keeps[count:]:
        keep.start()

    def device(shift):
        other = lax.rem(me + shift, devices)
        chip = other // 2
        return {"z": chip // 4, "y": lax.rem(chip // 2, 2), "x": lax.rem(chip, 2), "c": lax.rem(other, 2)}

    barrier = pltpu.get_barrier_semaphore()

    @pl.loop(1, devices)
    def _(shift):
        pl.semaphore_signal(barrier, inc=1, device_id=device(shift), device_id_type=MESH)

    for index in range(narrow):
        fill(index)
    pl.semaphore_wait(barrier, devices - 1)
    copies = {}

    def share(index, source_of, goal):
        for number, (axes, owner) in enumerate(peers):
            slot = 3 * index + number
            copies[index, number] = push(axes, source_of(owner), goal, send.at[slot], recv.at[slot])

    def arrive(index):
        keeps[index].wait()
        for number in range(3):
            copies[index, number].wait_recv()

    for index in range(narrow):
        share(index, functools.partial(piece, index), target(index))
    share(count, lambda owner: places, all_places.at[rank])

    @pl.loop(1, devices)
    def _(shift):
        other = lax.rem(me + shift, devices)
        pltpu.make_async_remote_copy(
            src_ref=packed.at[other],
            dst_ref=landed.at[me],
            send_sem=rows_send,
            recv_sem=rows_recv,
            device_id=device(shift),
            device_id_type=MESH,
        ).start()

    for index in range(narrow, count):
        fill(index)
    for index in range(narrow):
        arrive(index)
    ride.begin()
    for index in range(narrow, count):
        share(index, functools.partial(piece, index), target(index))
    most = pl.ds(0, devices - 1)
    ride.advance()
    pltpu.make_async_copy(packed.at[most], landed.at[most], rows_recv).wait()
    for index in range(narrow, count + 1):
        arrive(index)
    keeps[count + 1].wait()
    ride.finish()
    for copy in copies.values():
        copy.wait_send()
    pltpu.make_async_copy(packed.at[most], packed.at[most], rows_send).wait()


def dispatch(weights, turned, narrow, places, packed, steps, name):
    flat = [w.shape[::-1] if flip_it else w.shape for w, flip_it in zip(weights, turned)]
    rows = flat[0][0]
    total = lax.axis_size("z")
    anywhere = pl.BlockSpec(memory_space=pltpu.HBM)
    count = len(weights)
    widths = [sum(shape[1] // 4 for shape in flat[:narrow])]
    widths += [shape[1] // 4 for shape in flat[narrow:]]
    shapes = [jax.ShapeDtypeStruct((total * 4 * rows, width), BF16) for width in widths]
    shapes.append(jax.ShapeDtypeStruct((4, *places.shape), places.dtype))
    shapes.append(jax.ShapeDtypeStruct(packed.shape, packed.dtype))
    return pl.pallas_call(
        functools.partial(dispatch_kernel, tuple(turned), narrow, steps),
        in_specs=[anywhere] * (count + 2),
        out_specs=[anywhere] * len(shapes),
        out_shape=shapes,
        scratch_shapes=[
            pltpu.SemaphoreType.DMA((3 * count + 3,)),
            pltpu.SemaphoreType.DMA((3 * count + 3,)),
            pltpu.SemaphoreType.DMA((count + 2,)),
            pltpu.SemaphoreType.DMA(()),
            pltpu.SemaphoreType.DMA(()),
            pltpu.SemaphoreType.DMA((2 * steps,)),
            pltpu.SemaphoreType.DMA((2 * steps,)),
            pltpu.SemaphoreType.DMA((count,)),
        ]
        + [pltpu.VMEM(weight.shape, F32) for weight in weights]
        + [pltpu.VMEM(shape, BF16) for shape in flat],
        compiler_params=pltpu.CompilerParams(
            collective_id=IDS.index(name), has_side_effects=True, vmem_limit_bytes=VMEM_BYTES
        ),
        cost_estimate=pl.CostEstimate(flops=0, bytes_accessed=120 << 20, transcendentals=0),
        name=name,
    )(*weights, places, packed)


def gather_stages(own, out, send, recv, local, ride):
    rows = own.shape[0]
    half = rows // 2

    def part(core, y, x, side):
        start = block_at(core, y, x) * rows + side * half
        return out.at[pl.ds(pl.multiple_of(start, half), half)]

    def over(axis, source, target, slot):
        return push((axis,), source, target, send.at[slot], recv.at[slot])

    def across(y, x, side, slot):
        here = part(0, y, x, side)
        return over("c", here, here, slot)

    whole = out.at[pl.ds(pl.multiple_of(block_at(0, 0, 0) * rows, rows), rows)]
    keep = pltpu.make_async_copy(own, whole, local)
    keep.start()
    greet((("x",), ("y",), ("c",)), ride.steps > 0)
    first, second = own.at[pl.ds(0, half)], own.at[pl.ds(half, half)]
    x_first = over("x", first, part(0, 0, 0, 0), 0)
    y_second = over("y", second, part(0, 0, 0, 1), 1)
    x_second = over("x", second, part(0, 0, 0, 1), 2)
    y_first = over("y", first, part(0, 0, 0, 0), 3)
    ride.begin()
    crossed = [over("c", own, whole, 4)]
    yield
    x_first.wait_recv()
    far_first = over("y", part(0, 0, 1, 0), part(0, 0, 1, 0), 5)
    crossed.append(across(0, 1, 0, 6))
    y_second.wait_recv()
    far_second = over("x", part(0, 1, 0, 1), part(0, 1, 0, 1), 7)
    crossed.append(across(1, 0, 1, 8))
    yield
    x_second.wait_recv()
    crossed.append(across(0, 1, 1, 9))
    y_first.wait_recv()
    crossed.append(across(1, 0, 0, 10))
    ride.advance()
    yield
    far_first.wait_recv()
    crossed.append(across(1, 1, 0, 11))
    far_second.wait_recv()
    crossed.append(across(1, 1, 1, 12))
    for copy in crossed:
        copy.wait_recv()
    keep.wait()
    ride.advance()
    yield
    ride.finish()
    for copy in crossed + [x_first, y_second, x_second, y_first, far_first, far_second]:
        copy.wait_send()
    yield


def gather_body(inputs, outputs, scratch, ride):
    for _ in gather_stages(inputs[0], outputs[0], *scratch, ride):
        pass


def gather_turns_body(inputs, outputs, scratch, ride):
    own, table_ref, places_ref = inputs
    out, cos_ref, sin_ref = outputs
    stages = gather_stages(own, out, *scratch, ride)
    next(stages)
    size, width = table_ref.shape[0], 2 * HEAD_DIM
    count, _, block = places_ref.shape
    for index in range(count):
        at = pl.ds(index * block, block)
        entry = lax.broadcasted_iota(jnp.int32, (size, block), 0)
        pick = (entry == places_ref[index]).astype(F32).astype(BF16)
        rows = outer_sum(pick, table_ref[:, :width])
        rows += outer_sum(pick, table_ref[:, width : 2 * width])
        rows += outer_sum(pick, table_ref[:, 2 * width :])
        cos_ref[at, :] = rows[:, :HEAD_DIM]
        sin_ref[at, :] = rows[:, HEAD_DIM:]

    for _ in stages:
        pass


def rotation_table(size):
    half_dim = HEAD_DIM // 2
    steps = -np.arange(half_dim, dtype=np.float32) * np.float32(2.0 * math.log(10000.0) / HEAD_DIM)
    angles = np.arange(size, dtype=np.float32)[:, None] * np.exp(steps)[None, :]
    cos_half, sin_half = np.cos(angles), np.sin(angles)
    rest = np.concatenate([cos_half, cos_half, -sin_half, sin_half], axis=1)
    terms = []
    for _ in range(3):
        terms.append(rest.astype(BF16))
        rest = rest - terms[-1].astype(np.float32)
    return jnp.asarray(np.concatenate(terms, axis=1))


def plane_gather_turns(rows, table, places, name, ride):
    anywhere = pl.BlockSpec(memory_space=pltpu.HBM)
    near = pl.BlockSpec(memory_space=pltpu.VMEM)
    total = 8 * rows.shape[0]
    got = communicate(
        gather_turns_body,
        [rows, table, places],
        [anywhere, near, near],
        [jax.ShapeDtypeStruct((total, rows.shape[1]), rows.dtype)]
        + [jax.ShapeDtypeStruct((total, HEAD_DIM), F32)] * 2,
        [anywhere, near, near],
        [
            pltpu.SemaphoreType.DMA((13,)),
            pltpu.SemaphoreType.DMA((13,)),
            pltpu.SemaphoreType.DMA(()),
        ],
        name,
        ride,
    )
    return got[:3], got[3:]


def outer_tiles(sources, targets, tiles, stage, loads, stores, between=lambda: None):
    count = tiles[0].shape[0]
    tile = tiles[0].shape[2]
    total = sources[0][0].shape[1] // tile

    def fetch(index, slot):
        at = pl.ds(pl.multiple_of(index * tile, tile), tile)
        return [
            pltpu.make_async_copy(source.at[:, at], held.at[slot], loads.at[number, slot])
            for number, ((source, _), held) in enumerate(zip(sources, tiles))
        ]

    def keep(index, slot):
        at = pl.ds(pl.multiple_of(index * tile, tile), tile)
        return [
            pltpu.make_async_copy(
                stage.at[slot, :, pl.ds(start, size)], target.at[at], stores.at[number, slot]
            )
            for number, (target, start, size) in enumerate(targets)
        ]

    for copy in fetch(0, 0):
        copy.start()

    def multiply(index):
        slot = lax.rem(index, count)

        @pl.when(index + 1 < total)
        def _():
            for copy in fetch(index + 1, lax.rem(index + 1, count)):
                copy.start()

        @pl.when(index >= count)
        def _():
            for copy in keep(index - count, slot):
                copy.wait()

        for copy in fetch(index, slot):
            copy.wait()
        for (_, parts), held in zip(sources, tiles):
            left = held[slot]
            for start, size, right in parts:
                stage[slot, :, pl.ds(start, size)] = outer_sum(left, right()).astype(BF16)
        for copy in keep(index, slot):
            copy.start()

    pl.loop(0, total // 2)(multiply)
    between()
    pl.loop(total // 2, total)(multiply)
    for index in range(max(total - count, 0), total):
        for copy in keep(index, index % count):
            copy.wait()


def outer_scratch(rows, sources, columns, targets, tile=256):
    return [pltpu.VMEM((2, rows, tile), BF16)] * sources + [
        pltpu.VMEM((2, tile, columns), BF16),
        pltpu.SemaphoreType.DMA((sources, 2)),
        pltpu.SemaphoreType.DMA((targets, 2)),
    ]


def gather_hidden_body(inputs, outputs, scratch, ride):
    own, seen_ref, gate_ref, up_ref = inputs
    out, hidden_ref, by_gate_ref, by_up_ref, weight_ref = outputs
    seen, gate_w, up_w, hidden, by_gate, by_up, loads, stores, *outer = scratch[3:]
    blocks, block = seen.shape[0], seen.shape[1]
    width = gate_w.shape[1]
    tile = 512
    fetch = [
        pltpu.make_async_copy(gate_ref, gate_w, loads.at[0]),
        pltpu.make_async_copy(up_ref, up_w, loads.at[1]),
    ]
    for index in range(blocks):
        at = pl.ds(index * block, block)
        fetch.append(pltpu.make_async_copy(seen_ref.at[at], seen.at[index], loads.at[2 + index]))
    for index in (0, 2, 1, *range(3, len(fetch))):
        fetch[index].start()
    stages = gather_stages(own, out, *scratch[:3], ride)
    next(stages)
    fetch[0].wait()
    fetch[1].wait()
    kept = []
    for index in range(blocks):
        fetch[2 + index].wait()

        @pl.loop(0, width // tile)
        def _(step):
            at = pl.ds(pl.multiple_of(step * tile, tile), tile)
            here = seen[index]
            gate = project(here, gate_w[:, at])
            up = project(here, up_w[:, at])
            turned = 1.0 / (1.0 + jnp.exp(-gate))
            silu = gate * turned
            hidden[pl.ds(index * block, block), at] = (silu * up).astype(BF16)
            by_up[pl.ds(index * block, block), at] = silu.astype(BF16)
            by_gate[pl.ds(index * block, block), at] = (up * (turned * (1.0 + gate * (1.0 - turned)))).astype(BF16)

        rows_at = pl.ds(index * block, block)
        pairs = ((hidden, hidden_ref), (by_gate, by_gate_ref), (by_up, by_up_ref))
        for number, (held, target) in enumerate(pairs):
            copy = pltpu.make_async_copy(
                held.at[rows_at], target.at[rows_at], stores.at[number, index]
            )
            copy.start()
            kept.append(copy)
        if index in (3, 6):
            next(stages)
    next(stages)
    outer_tiles(
        [(out, [(0, width, lambda: hidden[...])])],
        [(weight_ref, 0, width)],
        outer[:1],
        *outer[1:],
    )
    next(stages)
    for copy in kept:
        copy.wait()


def plane_gather_hidden(rows, seen, gate_w, up_w, name, ride=None):
    total, depth = seen.shape
    width = gate_w.shape[1]
    block = rows.shape[0]
    blocks = total // block
    anywhere = pl.BlockSpec(memory_space=pltpu.HBM)
    got = communicate(
        gather_hidden_body,
        [rows, seen, gate_w, up_w],
        [anywhere] * 4,
        [jax.ShapeDtypeStruct((8 * rows.shape[0], rows.shape[1]), rows.dtype)]
        + [jax.ShapeDtypeStruct((total, width), BF16)] * 3
        + [jax.ShapeDtypeStruct((rows.shape[1], width), BF16)],
        [anywhere] * 5,
        [
            pltpu.SemaphoreType.DMA((13,)),
            pltpu.SemaphoreType.DMA((13,)),
            pltpu.SemaphoreType.DMA(()),
            pltpu.VMEM((blocks, block, depth), BF16),
            pltpu.VMEM((depth, width), BF16),
            pltpu.VMEM((depth, width), BF16),
            pltpu.VMEM((total, width), BF16),
            pltpu.VMEM((total, width), BF16),
            pltpu.VMEM((total, width), BF16),
            pltpu.SemaphoreType.DMA((2 + blocks,)),
            pltpu.SemaphoreType.DMA((3, blocks)),
        ]
        + outer_scratch(total, 1, width, 1),
        name,
        ride,
        flops=6 * total * depth * width,
    )
    return got[:5], got[5:]


def plane_gather(rows, name, ride=None):
    got = communicate(
        gather_body,
        [rows],
        [pl.BlockSpec(memory_space=pltpu.HBM)],
        [jax.ShapeDtypeStruct((8 * rows.shape[0], rows.shape[1]), rows.dtype)],
        [pl.BlockSpec(memory_space=pltpu.HBM)],
        [
            pltpu.SemaphoreType.DMA((13,)),
            pltpu.SemaphoreType.DMA((13,)),
            pltpu.SemaphoreType.DMA(()),
        ],
        name,
        ride,
    )
    return got[0], got[1:]


def product_body(make, starts, inputs, outputs, scratch, ride):
    out_ref = outputs[0]
    left, weight, away, got, near, by_y, by_x, end_y, end_x, send, recv, local = scratch[:12]
    block, width = out_ref.shape
    half = block // 2
    tile = 1024
    pairs = [(inputs[2 * i], inputs[2 * i + 1], start) for i, start in enumerate(starts)]

    def over(axis, source, target, slot):
        return push((axis,), source, target, send.at[slot], recv.at[slot])

    waits = {"weight": []}
    column = 0
    for index, (rows_ref, weight_ref, start) in enumerate(pairs):
        inner = weight_ref.shape[1] if make else rows_ref.shape[1]
        copy = pltpu.make_async_copy(
            weight_ref.at[:, pl.ds(start, inner)],
            weight.at[:, pl.ds(column, inner)],
            local.at[index, 8],
        )
        copy.start()
        waits["weight"].append(copy)
        column += inner
    order = ((1, 1, 1), (1, 1, 0), (0, 1, 1), (1, 0, 1), (0, 1, 0), (1, 0, 0), (0, 0, 1), (0, 0, 0))
    places = [pl.ds(pl.multiple_of(block_at(*key) * block, block), block) for key in order]
    if make:
        fill, follow = make(inputs, outputs, scratch[12:], left, places)
    else:
        for slot, key in enumerate(order):
            waits[key] = []
            column = 0
            for index, (rows_ref, _, _) in enumerate(pairs):
                inner = rows_ref.shape[1]
                copy = pltpu.make_async_copy(
                    rows_ref.at[places[slot]],
                    left.at[places[slot], pl.ds(column, inner)],
                    local.at[index, slot],
                )
                copy.start()
                waits[key].append(copy)
                column += inner
    greet((("x",), ("y",), ("c",)), ride.steps > 0)
    ride.begin()
    for copy in waits["weight"]:
        copy.wait()

    def multiply(key, store):
        slot = order.index(key)
        if make:
            fill(slot)
        else:
            for copy in waits[key]:
                copy.wait()
        here = left[places[slot], :]
        for start in range(0, width, tile):
            at = pl.ds(start, tile)
            store(at, project_t(here, weight[at, :]))

    crossing = {}

    def compute_far(y, x):
        index = 2 * y + x

        def store(at, value):
            away[index, :, at] = value.astype(BF16)

        multiply((1, y, x), store)
        crossing[index] = over("c", away.at[index], got.at[index], index)

    def compute_near(y, x):
        index = 2 * y + x
        crossing[index].wait_recv()

        def store(at, value):
            near[index, :, at] = (value + got[index, :, at].astype(F32)).astype(BF16)

        multiply((0, y, x), store)

    lower, upper = pl.ds(0, half), pl.ds(half, half)
    compute_far(1, 1)
    compute_far(1, 0)
    compute_near(1, 1)
    y_far = over("y", near.at[3, lower], by_y.at[1], 4)
    x_far = over("x", near.at[3, upper], by_x.at[1], 5)
    compute_far(0, 1)
    compute_near(1, 0)
    y_near = over("y", near.at[2, lower], by_y.at[0], 6)
    if make:
        ride.advance()
    compute_far(0, 0)
    compute_near(0, 1)
    x_near = over("x", near.at[1, upper], by_x.at[0], 7)
    y_far.wait_recv()
    near[1, lower, :] = (near[1, lower, :].astype(F32) + by_y[1].astype(F32)).astype(BF16)
    x_last = over("x", near.at[1, lower], end_x, 8)
    x_far.wait_recv()
    near[2, upper, :] = (near[2, upper, :].astype(F32) + by_x[1].astype(F32)).astype(BF16)
    y_last = over("y", near.at[2, upper], end_y, 9)
    if not make:
        ride.advance()
    compute_near(0, 0)
    if make:
        follow(ride.advance)
    y_near.wait_recv()
    out_ref[lower, :] = near[0, lower, :].astype(F32) + by_y[0].astype(F32)
    x_near.wait_recv()
    out_ref[upper, :] = near[0, upper, :].astype(F32) + by_x[0].astype(F32)
    x_last.wait_recv()
    out_ref[lower, :] += end_x[...].astype(F32)
    y_last.wait_recv()
    out_ref[upper, :] += end_y[...].astype(F32)
    ride.finish()
    for copy in list(crossing.values()) + [y_far, x_far, y_near, x_near, x_last, y_last]:
        copy.wait_send()


def product_scratch(total, inner, width, pairs):
    block = total // 8
    half = block // 2
    return [
        pltpu.VMEM((total, inner), BF16),
        pltpu.VMEM((width, inner), BF16),
        pltpu.VMEM((4, block, width), BF16),
        pltpu.VMEM((4, block, width), BF16),
        pltpu.VMEM((4, block, width), BF16),
        pltpu.VMEM((2, half, width), BF16),
        pltpu.VMEM((2, half, width), BF16),
        pltpu.VMEM((half, width), BF16),
        pltpu.VMEM((half, width), BF16),
        pltpu.SemaphoreType.DMA((10,)),
        pltpu.SemaphoreType.DMA((10,)),
        pltpu.SemaphoreType.DMA((pairs, 9)),
    ]


def hidden_back(inputs, outputs, scratch, left, places):
    by_gate_ref, gate_w, by_up_ref, up_w, grad_ref, down_ref, seen_ref = inputs
    weight_gate, weight_up = outputs[1:]
    down, rows, factors, down_load, row_loads, *outer = scratch
    width = down.shape[1]
    tile = 1024
    fetch_down = pltpu.make_async_copy(down_ref, down, down_load)
    fetch_down.start()

    def fetch(slot):
        at, held = places[slot], slot % 2
        return [
            pltpu.make_async_copy(grad_ref.at[at], rows.at[held], row_loads.at[0, held]),
            pltpu.make_async_copy(by_gate_ref.at[at], factors.at[held, 0], row_loads.at[1, held]),
            pltpu.make_async_copy(by_up_ref.at[at], factors.at[held, 1], row_loads.at[2, held]),
        ]

    for copy in fetch(0):
        copy.start()

    def fill(slot):
        if slot == 0:
            fetch_down.wait()
        for copy in fetch(slot):
            copy.wait()
        if slot + 1 < len(places):
            for copy in fetch(slot + 1):
                copy.start()
        held = slot % 2

        for start in range(0, width, tile):
            at, beside = pl.ds(start, tile), pl.ds(width + start, tile)
            grad = project(rows[held], down[:, at])
            left[places[slot], at] = (grad * factors[held, 0, :, at].astype(F32)).astype(BF16)
            left[places[slot], beside] = (grad * factors[held, 1, :, at].astype(F32)).astype(BF16)

    def follow(between):
        outer_tiles(
            [
                (
                    seen_ref,
                    [
                        (0, width, lambda: left[:, pl.ds(0, width)]),
                        (width, width, lambda: left[:, pl.ds(width, width)]),
                    ],
                )
            ],
            [(weight_gate, 0, width), (weight_up, width, width)],
            outer[:1],
            *outer[1:],
            between,
        )

    return fill, follow


def plane_product_back(grads, down, by_gate, by_up, gate_w, up_w, seen, name, ride):
    total, depth = grads.shape
    width = gate_w.shape[1]
    block = total // 8
    operands = [by_gate, gate_w, by_up, up_w, grads, down, seen]
    anywhere = pl.BlockSpec(memory_space=pltpu.HBM)
    got = communicate(
        functools.partial(product_body, hidden_back, [0, 0]),
        operands,
        [anywhere] * len(operands),
        [jax.ShapeDtypeStruct((block, depth), F32)]
        + [jax.ShapeDtypeStruct((depth, width), BF16)] * 2,
        [pl.BlockSpec(memory_space=pltpu.VMEM), anywhere, anywhere],
        product_scratch(total, 2 * width, depth, 2)
        + [
            pltpu.VMEM((depth, width), BF16),
            pltpu.VMEM((2, block, depth), BF16),
            pltpu.VMEM((2, 2, block, width), BF16),
            pltpu.SemaphoreType.DMA(()),
            pltpu.SemaphoreType.DMA((3, 2)),
        ]
        + outer_scratch(total, 1, 2 * width, 2),
        name,
        ride,
        flops=10 * total * depth * width,
    )
    return got[:3], got[3:]


def plane_product(pairs, name, ride=None):
    total = pairs[0][0].shape[0]
    inner = sum(rows.shape[1] for rows, _, _ in pairs)
    width = pairs[0][1].shape[0]
    operands = []
    for rows, weight, _ in pairs:
        operands += [rows, weight]
    got = communicate(
        functools.partial(product_body, None, [start for _, _, start in pairs]),
        operands,
        [pl.BlockSpec(memory_space=pltpu.HBM)] * len(operands),
        [jax.ShapeDtypeStruct((total // 8, width), F32)],
        [pl.BlockSpec(memory_space=pltpu.VMEM)],
        product_scratch(total, inner, width, len(pairs)),
        name,
        ride,
        flops=2 * total * inner * width,
    )
    return got[0], got[1:]


def ring_next(values):
    total = lax.axis_size("z")
    return lax.ppermute(values, "z", [(i, (i + 1) % total) for i in range(total)])


def ring_rows(whole, owner):
    rows = whole.shape[0] // lax.axis_size("z")
    return lax.dynamic_slice(whole, (owner * rows, 0), (rows, whole.shape[1]))


class Gathered:
    def __init__(self, whole, step=0):
        self.whole, self.step = whole, step

    def ride(self, count):
        count = min(count, lax.axis_size("z") - 1 - self.step)
        item = (self.whole, self.step, count)
        self.step += count
        return item

    def land(self, whole):
        self.whole = whole

    def walk(self, count):
        total = lax.axis_size("z")
        rows = self.whole.shape[0] // total
        last = min(self.step + count, total - 1)
        current = ring_rows(self.whole, owner_at(self.step)) if self.step < last else None
        while self.step < last:
            self.step += 1
            current = ring_next(current)
            self.whole = lax.dynamic_update_slice(self.whole, current, (owner_at(self.step) * rows, 0))

    def finish(self):
        self.walk(lax.axis_size("z"))
        return self.whole


class Summed:
    def __init__(self, whole):
        self.whole, self.step, self.running = whole, 0, None

    def ride(self, count):
        count = min(count, lax.axis_size("z") - 1 - self.step)
        item = (self.running, self.whole, self.step, count)
        self.step += count
        return item

    def land(self, running):
        self.running = running

    def walk(self, count):
        total = lax.axis_size("z")
        for _ in range(min(count, total - 1 - self.step)):
            running = ring_rows(self.whole, owner_at(1)) if self.running is None else self.running
            own = ring_rows(self.whole, owner_at((self.step + 2) % total))
            self.running = (ring_next(running).astype(F32) + own.astype(F32)).astype(BF16)
            self.step += 1

    def finish(self):
        self.walk(lax.axis_size("z"))
        return self.running


def from_plane(block):
    rows = block.shape[0] // 4
    me_y, me_x = lax.axis_index("y"), lax.axis_index("x")

    def piece(y, x):
        return lax.dynamic_slice(block, ((y * 2 + x) * rows, 0), (rows, block.shape[1]))

    own = piece(me_y, me_x)
    by_x = lax.ppermute(piece(me_y, 1 - me_x), "x", ((0, 1), (1, 0)))
    by_y = lax.ppermute(piece(1 - me_y, me_x), "y", ((0, 1), (1, 0)))
    far = lax.ppermute(piece(1 - me_y, 1 - me_x), ("y", "x"), ((0, 3), (1, 2), (2, 1), (3, 0)))

    def chosen(y, x):
        same_y, same_x = me_y == y, me_x == x
        return jnp.where(
            same_y, jnp.where(same_x, own, by_x), jnp.where(same_x, by_y, far)
        )

    return [chosen(y, x) for y in range(2) for x in range(2)]


def side_by_side(pieces, start=0, stop=None):
    return jnp.concatenate([piece[:, start:stop].astype(F32) for piece in pieces], axis=1)


def turn(values, cos_rows, sin_rows):
    return values * cos_rows + pltpu.roll(values, HEAD_DIM // 2, 1) * sin_rows


def visible_of(follow):
    size = follow.shape[1]
    row = lax.broadcasted_iota(jnp.int32, (size, size), 0)
    column = lax.broadcasted_iota(jnp.int32, (size, size), 1)
    return (column <= row) & (row - column <= follow)


def soft_of(queries, keys, visible):
    scores = project_t(queries, keys) * (1.0 / math.sqrt(HEAD_DIM))
    scores = jnp.where(visible, scores, NEG_LARGE)
    weights = jnp.exp(scores - jnp.max(scores, axis=1, keepdims=True))
    return weights / jnp.sum(weights, axis=1, keepdims=True)


def attend_body(inputs, outputs):
    seen_ref, weight_ref, cos_ref, sin_ref, follow_ref = inputs
    low_ref, out_ref = outputs
    width = out_ref.shape[1]
    cos_rows, sin_rows = cos_ref[...], sin_ref[...]
    visible = visible_of(follow_ref[0])
    lin = project(seen_ref[...], weight_ref[...])
    for start in range(0, width, HEAD_DIM):
        here = slice(start, start + HEAD_DIM)
        key_at = slice(width + start, width + start + HEAD_DIM)
        value_at = slice(2 * width + start, 2 * width + start + HEAD_DIM)
        queries = turn(lin[:, here], cos_rows, sin_rows).astype(BF16)
        keys = turn(lin[:, key_at], cos_rows, sin_rows).astype(BF16)
        values = lin[:, value_at].astype(BF16)
        low_ref[:, here] = queries
        low_ref[:, key_at] = keys
        low_ref[:, value_at] = values
        soft = soft_of(queries, keys, visible).astype(BF16)
        out_ref[:, here] = project(soft, values).astype(BF16)


def attend_back_body(blocks, inputs, outputs, grads_held):
    low_ref, seen_ref, weight_ref, cos_ref, sin_ref, follow_ref = inputs[:6]
    seen_tile, grad_tile, attended_ref = inputs[6:]
    out_ref, outer_ref = outputs
    step = pl.program_id(0)
    block = out_ref.shape[0]

    @pl.when(step < blocks)
    def _():
        attend_back_block(inputs[:6], out_ref)
        grads_held[pl.ds(pl.multiple_of(step * block, block), block), :] = out_ref[...]

    @pl.when(step >= blocks)
    def _():
        width = out_ref.shape[1]
        outer_ref[:, :width] = outer_sum(seen_tile[...], grads_held[...]).astype(BF16)
        outer_ref[:, width:] = outer_sum(grad_tile[...], attended_ref[...]).astype(BF16)


def attend_back_block(inputs, out_ref):
    low_ref, seen_ref, weight_ref, cos_ref, sin_ref, follow_ref = inputs
    width = weight_ref.shape[1]
    cos_rows, sin_rows = cos_ref[...], -sin_ref[...]
    visible = visible_of(follow_ref[0])
    scale = 1.0 / math.sqrt(HEAD_DIM)
    grad_all = project(seen_ref[...], weight_ref[...]).astype(BF16)
    for start in range(0, width, HEAD_DIM):
        here = slice(start, start + HEAD_DIM)
        key_at = slice(width + start, width + start + HEAD_DIM)
        value_at = slice(2 * width + start, 2 * width + start + HEAD_DIM)
        queries, keys, values = low_ref[:, here], low_ref[:, key_at], low_ref[:, value_at]
        grad = grad_all[:, here]
        soft = soft_of(queries, keys, visible)
        grad_soft = project_t(grad, values)
        inner = jnp.sum(soft * grad_soft, axis=1, keepdims=True)
        grad_scores = (soft * (grad_soft - inner)).astype(BF16)
        grad_query = project(grad_scores, keys) * scale
        grad_key = outer_sum(grad_scores, queries) * scale
        out_ref[:, here] = turn(grad_query, cos_rows, sin_rows).astype(BF16)
        out_ref[:, key_at] = turn(grad_key, cos_rows, sin_rows).astype(BF16)
        out_ref[:, value_at] = outer_sum(soft.astype(BF16), grad).astype(BF16)


def plane_peers():
    me_y, me_x = lax.axis_index("y"), lax.axis_index("x")
    return (
        (("x",), me_y * 2 + 1 - me_x),
        (("y",), (1 - me_y) * 2 + me_x),
        (("y", "x"), (1 - me_y) * 2 + 1 - me_x),
    )


def collect_copies(blocks, outs, send, recv, local):
    rank = lax.axis_index("y") * 2 + lax.axis_index("x")
    keeps, copies = [], []
    for index, (block, out) in enumerate(zip(blocks, outs)):
        rows = block.shape[0] // 4

        def piece(owner, block=block, rows=rows):
            return block.at[pl.ds(pl.multiple_of(owner * rows, rows), rows)]

        keeps.append(pltpu.make_async_copy(piece(rank), out.at[rank], local.at[index]))
        for number, (axes, owner) in enumerate(plane_peers()):
            copies.append(
                pltpu.make_async_remote_copy(
                    src_ref=piece(owner),
                    dst_ref=out.at[rank],
                    send_sem=send.at[3 * index + number],
                    recv_sem=recv.at[3 * index + number],
                    device_id=flip(*axes),
                    device_id_type=MESH,
                )
            )
    return keeps, copies


def collected_shape(block):
    return jax.ShapeDtypeStruct((4, block.shape[0] // 4, block.shape[1]), block.dtype)


def by_blocks(
    body, operands, specs, shapes, out_specs, blocks, name, ride, flops, collect=(), own_scratch=(), advances=()
):
    extra = len(collect)
    operands, shapes = list(operands) + list(collect), list(shapes)
    shapes += [collected_shape(block) for block in collect]
    anywhere = pl.BlockSpec(memory_space=pltpu.HBM)
    specs, out_specs = list(specs) + [anywhere] * extra, list(out_specs) + [anywhere] * extra
    scratch = list(own_scratch)
    if extra:
        scratch += [
            pltpu.SemaphoreType.DMA((3 * extra,)),
            pltpu.SemaphoreType.DMA((3 * extra,)),
            pltpu.SemaphoreType.DMA((extra,)),
        ]
    count_in, count_out = len(operands), len(shapes)
    all_in = count_in + len(ride.operands)
    all_out = count_out + len(ride.shapes)

    def kernel(*refs):
        inputs, outputs, held = refs[:all_in], refs[all_in : all_in + all_out], refs[all_in + all_out :]
        step = pl.program_id(0)
        ride.board(inputs[count_in:], outputs[count_out:], held[len(scratch) :])
        keeps, copies = [], []
        if extra:
            keeps, copies = collect_copies(
                inputs[count_in - extra : count_in], outputs[count_out - extra : count_out], *held[len(scratch) - 3 : len(scratch)]
            )
        if ride.copies or extra:

            @pl.when(step == 0)
            def _():
                greet([axes for axes, _ in plane_peers()] if extra else (), bool(ride.copies))
                ride.begin()
                for copy in keeps + copies:
                    copy.start()

        body(inputs[: count_in - extra], outputs[: count_out - extra], *held[: len(own_scratch)])
        for number in advances:
            pl.when(step == number)(ride.advance)
        if ride.copies or extra:

            @pl.when(step == blocks - 1)
            def _():
                for copy in keeps:
                    copy.wait()
                for copy in copies:
                    copy.wait()
                ride.finish()

    params = {"collective_id": IDS.index(name), "has_side_effects": True} if ride.steps or extra else {}
    got = pl.pallas_call(
        kernel,
        grid=(blocks,),
        in_specs=list(specs) + [anywhere] * len(ride.operands),
        out_specs=list(out_specs) + [anywhere] * len(ride.shapes),
        out_shape=list(shapes) + ride.shapes,
        scratch_shapes=scratch + ride.scratch,
        input_output_aliases={count_in + k: count_out + v for k, v in ride.aliases.items()},
        compiler_params=pltpu.CompilerParams(vmem_limit_bytes=VMEM_BYTES, **params),
        cost_estimate=pl.CostEstimate(flops=flops, bytes_accessed=40 << 20, transcendentals=0),
        name=name,
    )(*operands, *ride.operands)
    return list(got)


def row_spec(rows, columns):
    return pl.BlockSpec((rows, columns), lambda i: (i, 0))


def attend(seen, weight, cos_rows, sin_rows, places, block, ride):
    rows, depth = seen.shape
    width = weight.shape[1] // 4
    got = by_blocks(
        attend_body,
        [seen, weight, cos_rows, sin_rows, places],
        [
            row_spec(block, depth),
            pl.BlockSpec((depth, 3 * width), lambda i: (0, 0)),
            row_spec(block, HEAD_DIM),
            row_spec(block, HEAD_DIM),
            pl.BlockSpec((1, 1, block), lambda i: (i, 0, 0)),
        ],
        [
            jax.ShapeDtypeStruct((rows, 3 * width), BF16),
            jax.ShapeDtypeStruct((rows, width), BF16),
        ],
        [row_spec(block, 3 * width), row_spec(block, width)],
        rows // block,
        "attend",
        ride,
        4 * rows * block * width + 6 * rows * depth * width,
    )
    return got[:2], got[2:]


def attend_back(low, grad_all, weight, cos_rows, sin_rows, places, seen, attended, block, ride, collect):
    rows, depth = grad_all.shape
    width = weight.shape[1] // 4
    blocks = rows // block
    tile = 256

    def early(columns):
        return pl.BlockSpec((block, columns), lambda i: (jnp.minimum(i, blocks - 1), 0))

    def late(i):
        return jnp.maximum(i - blocks, 0)

    got = by_blocks(
        functools.partial(attend_back_body, blocks),
        [low, grad_all, weight, cos_rows, sin_rows, places, seen, grad_all, attended],
        [
            early(3 * width),
            early(depth),
            pl.BlockSpec((depth, width), lambda i: (0, 3)),
            early(HEAD_DIM),
            early(HEAD_DIM),
            pl.BlockSpec((1, 1, block), lambda i: (jnp.minimum(i, blocks - 1), 0, 0)),
            pl.BlockSpec((rows, tile), lambda i: (0, late(i))),
            pl.BlockSpec((rows, tile), lambda i: (0, late(i))),
            pl.BlockSpec((rows, width), lambda i: (0, 0)),
        ],
        [
            jax.ShapeDtypeStruct((rows, 3 * width), BF16),
            jax.ShapeDtypeStruct((depth, 4 * width), BF16),
        ],
        [early(3 * width), pl.BlockSpec((tile, 4 * width), lambda i: (late(i), 0))],
        blocks + depth // tile,
        "attend_back",
        ride,
        10 * rows * block * width + 10 * rows * depth * width,
        collect,
        [pltpu.VMEM((rows, 3 * width), BF16)],
        (blocks - 2, blocks + depth // tile - 3),
    )
    last = 2 + len(collect)
    return got[:last], got[last:]


def plane_places(segments, block):
    groups, size = segments.shape
    numbers = jnp.arange(SEGS, dtype=jnp.int32)
    starts = jnp.sum((segments[:, :, None] < numbers).astype(jnp.int32), axis=1)
    ends = jnp.sum((segments[:, :, None] <= numbers).astype(jnp.int32), axis=1)
    onehot = segments[:, :, None] == numbers
    row = jnp.arange(size, dtype=jnp.int32)[None, :]
    places = row - jnp.sum(jnp.where(onehot, starts[:, None, :], 0), axis=2)
    follow = jnp.sum(jnp.where(onehot, ends[:, None, :], 0), axis=2) - 1 - row
    return places.reshape(-1, 1, block), follow.reshape(-1, 1, block)


def after(values, *gates):
    return lax.optimization_barrier((values,) + gates)[0]


EVERY = ("z", "y", "x", "c")


def exchange(rows):
    return lax.all_to_all(rows, EVERY, split_axis=0, concat_axis=0, tiled=True)


def on_device(
    tokens_in,
    cotangent,
    segment_ids,
    destination,
    source,
    w_query,
    w_key,
    w_value,
    w_out,
    w_gate,
    w_up,
    w_down,
):
    tok_rows = tokens_in.shape[0]
    devices = lax.axis_size(EVERY)
    per_peer = tok_rows // devices
    row_index = jnp.arange(tok_rows, dtype=jnp.int32)
    peer_to = destination // tok_rows
    ahead_rows = (peer_to[None, :] == peer_to[:, None]) & (
        destination[None, :] < destination[:, None]
    )
    send_slot = peer_to * per_peer + jnp.sum(ahead_rows.astype(jnp.int32), axis=1)
    peer_from = source // tok_rows
    before = (peer_from[None, :] == peer_from[:, None]) & (row_index[None, :] < row_index[:, None])
    recv_slot = peer_from * per_peer + jnp.sum(before.astype(jnp.int32), axis=1)
    send_pick = (send_slot[:, None] == row_index[None, :]).astype(BF16)
    recv_pick = (recv_slot[:, None] == row_index[None, :]).astype(BF16)

    packed = outer_sum(send_pick, tokens_in).astype(BF16)
    table = rotation_table(tok_rows)
    weights = [w_query, w_key, w_value, w_out, w_gate, w_up, w_down]
    attention_whole, gate_whole, up_whole, down_whole, segments, landed = dispatch(
        weights,
        [False, False, False, True, False, False, True],
        4,
        segment_ids.reshape(-1, 128),
        packed.reshape(devices, per_peer, -1),
        2,
        "dispatch",
    )
    arrived = project(recv_pick, landed.reshape(tok_rows, -1))
    attention_w, gate_w = Gathered(attention_whole, 2), Gathered(gate_whole)
    up_w, down_w = Gathered(up_whole), Gathered(down_whole)
    head_width = w_query.shape[1] // 4
    places, follow = plane_places(segments.reshape(4, -1), tok_rows)
    normed_one, scale_one = norm_parts(arrived)
    def send_back(rows):
        return exchange(outer_sum(recv_pick, rows.astype(BF16)).astype(BF16))

    def riding(call, gathers=(), sums=()):
        ride = Ride(
            [weight.ride(count) for weight, count in gathers],
            [gradient.ride(count) for gradient, count in sums],
        )
        result, landed = call(ride)
        for (item, _), value in zip(tuple(gathers) + tuple(sums), landed):
            item.land(value)
        return result

    seen_one, cos_rows, sin_rows = riding(
        lambda ride: plane_gather_turns(
            normed_one.astype(BF16), table, places, "gather_one", ride
        ),
        [(attention_w, 1), (gate_w, 1)],
    )
    attention = attention_w.finish()
    upstream_low = project(
        recv_pick,
        exchange(outer_sum(send_pick, after(cotangent, seen_one)).astype(BF16)),
    ).astype(BF16)
    upstream = upstream_low.astype(F32)
    qkv_low, attended = riding(
        lambda ride: attend(seen_one, attention, cos_rows, sin_rows, follow, tok_rows, ride),
        [(gate_w, 1)],
    )
    middle = arrived + riding(
        lambda ride: plane_product([(attended, attention, 3 * head_width)], "product_out", ride),
        [(gate_w, 1), (up_w, 1)],
    )
    normed_two, scale_two = norm_parts(middle)
    seen_two = riding(
        lambda ride: plane_gather(normed_two.astype(BF16), "gather_two", ride), [(up_w, 2)]
    )
    gate_whole, up_whole = gate_w.finish(), up_w.finish()
    grad_two_all, hidden, by_gate, by_up, weight_down = riding(
        lambda ride: plane_gather_hidden(
            upstream_low, seen_two, gate_whole, up_whole, "gather_up", ride
        ),
        [(down_w, 3)],
    )
    down_whole = down_w.finish()
    summed_down = Summed(weight_down)
    grad_normed_two, weight_gate, weight_up = riding(
        lambda ride: plane_product_back(
            grad_two_all,
            down_whole,
            by_gate,
            by_up,
            gate_whole,
            up_whole,
            seen_two,
            "product_forward",
            ride,
        ),
        (),
        [(summed_down, 3)],
    )
    summed_gate, summed_up = Summed(weight_gate), Summed(weight_up)
    output = middle + riding(
        lambda ride: plane_product(
            [(after(hidden, grad_normed_two), down_whole, 0)], "product_down", ride
        ),
        (),
        [(summed_gate, 2)],
    )
    returned_out = send_back(output)
    grad_middle = upstream + norm_back(normed_two, scale_two, grad_normed_two)
    grad_one_all = riding(
        lambda ride: plane_gather(
            after(grad_middle.astype(BF16), output), "gather_middle", ride
        ),
        (),
        [(summed_gate, 1), (summed_up, 1)],
    )
    grad_qkv, weight_attention, own_down, own_gate = riding(
        lambda ride: attend_back(
            after(qkv_low, returned_out),
            grad_one_all,
            attention,
            cos_rows,
            sin_rows,
            follow,
            seen_one,
            attended,
            tok_rows,
            ride,
            (summed_down.finish(), summed_gate.finish()),
        ),
        (),
        [(summed_up, 2)],
    )
    summed_attention = Summed(weight_attention)
    grad_normed_one = riding(
        lambda ride: plane_product([(grad_qkv, attention, 0)], "product_qkv", ride),
        (),
        [(summed_attention, 2)],
    )
    grad_inputs = grad_middle + norm_back(normed_one, scale_one, grad_normed_one)
    own_up, last_attention = from_plane(summed_up.finish()), summed_attention.finish()
    own_attention = from_plane(last_attention)
    own_down, own_gate, own_up = [
        after(own, last_attention) for own in (own_down, own_gate, jnp.stack(own_up))
    ]

    return (
        project(send_pick, after(returned_out, grad_normed_one)),
        project(send_pick, send_back(grad_inputs)),
        side_by_side(own_attention, 0, head_width),
        side_by_side(own_attention, head_width, 2 * head_width),
        side_by_side(own_attention, 2 * head_width, 3 * head_width),
        side_by_side(own_attention, 3 * head_width).T,
        side_by_side(own_gate),
        side_by_side(own_up),
        side_by_side(own_down).T,
    )


def solution(mesh):
    groups, cores = mesh.shape["dp"], mesh.shape["tensor"]
    whole = Mesh(mesh.devices.reshape(groups // 4, 2, 2, cores), EVERY)
    rows = P(EVERY, None)
    tall = P(("z", "y", "x"), "c")
    wide = P("c", ("z", "y", "x"))
    in_specs = (
        rows,
        rows,
        P(("z", "y", "x")),
        P(EVERY),
        P(EVERY),
        tall,
        tall,
        tall,
        wide,
        tall,
        tall,
        wide,
    )
    out_specs = (rows, rows, tall, tall, tall, wide, tall, tall, wide)
    return jax.shard_map(
        on_device, mesh=whole, in_specs=in_specs, out_specs=out_specs, check_vma=False
    )
```
